32 devices in a mesh: gx: 4 (over x, core), gy: 8 (over z, y).
Axes of the slice: x: 2, y: 2, z: 4, core: 2. Of those that a mesh axis runs over, the one named last changes fastest.
Arguments:
- layer_input: bfloat16 [8192, 1152], P(('gx', 'gy')), may hold values from -6 to 6
- norm_one_gain: bfloat16 [1152], P('gy'), may hold values from 0.5 to 1.5
- norm_one_bias: bfloat16 [1152], P('gy'), may hold values from -1.75 to 1.75
- query_weight: bfloat16 [1152, 1152], P('gx', 'gy'), may hold values from -0.1875 to 0.1875
- query_bias: bfloat16 [1152], P('gy'), may hold values from -1.75 to 1.75
- key_weight: bfloat16 [1152, 1152], P('gx', 'gy'), may hold values from -0.1875 to 0.1875
- value_weight: bfloat16 [1152, 1152], P('gx', 'gy'), may hold values from -0.1875 to 0.1875
- value_bias: bfloat16 [1152], P('gy'), may hold values from -1.75 to 1.75
- output_weight: bfloat16 [1152, 1152], P('gy', 'gx'), may hold values from -1 to 1
- output_bias: bfloat16 [1152], P('gy'), may hold values from -1.75 to 1.75
- norm_two_gain: bfloat16 [1152], P('gy'), may hold values from 0.5 to 1.5
- norm_two_bias: bfloat16 [1152], P('gy'), may hold values from -1.75 to 1.75
- up_weight: bfloat16 [1152, 4304], P('gx', 'gy'), may hold values from -0.1875 to 0.1875
- up_bias: bfloat16 [4304], P('gy'), may hold values from -1.75 to 1.75
- down_weight: bfloat16 [4304, 1152], P('gy', 'gx'), may hold values from -0.09375 to 0.09375
- down_bias: bfloat16 [1152], P('gy'), may hold values from -1.75 to 1.75
- cotangent: bfloat16 [8192, 1152], P(('gx', 'gy')), may hold values from -6 to 6
Outputs:
- layer_output: bfloat16 [8192, 1152], P(('gx', 'gy'))
- grad_input: bfloat16 [8192, 1152], P(('gx', 'gy'))
- grad_norm_one_gain: float32 [1152], P('gy')
- grad_norm_one_bias: float32 [1152], P('gy')
- grad_query_weight: float32 [1152, 1152], P('gx', 'gy')
- grad_query_bias: float32 [1152], P('gy')
- grad_key_weight: float32 [1152, 1152], P('gx', 'gy')
- grad_value_weight: float32 [1152, 1152], P('gx', 'gy')
- grad_value_bias: float32 [1152], P('gy')
- grad_output_weight: float32 [1152, 1152], P('gy', 'gx')
- grad_output_bias: float32 [1152], P('gy')
- grad_norm_two_gain: float32 [1152], P('gy')
- grad_norm_two_bias: float32 [1152], P('gy')
- grad_up_weight: float32 [1152, 4304], P('gx', 'gy')
- grad_up_bias: float32 [4304], P('gy')
- grad_down_weight: float32 [4304, 1152], P('gy', 'gx')
- grad_down_bias: float32 [1152], P('gy')
The draws below stay inside these ranges and needn't reach their ends.
All inputs are finite; a program needn't handle non-finite values.
Results may differ from the reference program's by a relative error of at most 0.023.
Values may be sent and summed in bfloat16 or wider, within the bound.
A program may use at most 192 MiB of HBM per device.

```python
import jax
import jax.numpy as jnp
from jax import lax

D = 1152
HEADS = 16
HD = 72
FF = 4304
LENGTH = 1024
IMAGES = 8
TOKENS = 8192


def with_spikes(array, stream_key, source, target, shards_of, factor):
    owner, partner = [(jnp.arange(array.shape[axis_at]) // (array.shape[axis_at] // shards_of)).reshape([-1 if axis == axis_at else 1 for axis in range(array.ndim)]) for axis_at in (source, target)]
    chosen = jax.random.permutation(stream_key, shards_of)[partner]
    strong = (owner == chosen) | (owner == (partner + shards_of // 2) % shards_of)
    return jnp.where(strong, factor * array, array)


def steps_of(stream_key, extent, cuts, low, largest):
    def one(dim, blocks):
        steps = jax.random.uniform(jax.random.fold_in(jax.random.fold_in(stream_key, 6), dim), (blocks,), jnp.float32, low / len(cuts), largest / len(cuts))
        return jnp.repeat(jnp.exp(steps), extent[dim] // blocks).reshape((-1,) + (1,) * (len(extent) - dim - 1))

    loudness = one(*cuts[0])
    for cut in cuts[1:]:
        loudness = loudness * one(*cut)
    return loudness


def normal_values(own_key, dims, scale, most, cuts=(), dtype=jnp.bfloat16):
    factor_of = steps_of(own_key, dims, cuts, -0.22, 0.18) if cuts else 1.0
    drawn = jax.random.normal(own_key, dims, jnp.float32) * scale * factor_of
    return jnp.minimum(jnp.maximum(drawn, -most), most).astype(dtype)


def gaussian_with(stream_key, shape, width, most, shards, heavy, dtype=jnp.bfloat16):
    array = width * jax.random.normal(stream_key, shape, jnp.float32)
    if shards:
        array = array * steps_of(stream_key, shape, shards, -0.22, 0.18)
    return jnp.clip(with_spikes(array, jax.random.fold_in(stream_key, 3), *heavy), -most, most).astype(dtype)


def setup_inputs(seed: int = 0) -> dict:
    key_of = jax.random.split(jax.random.key(seed), 18)
    return {
        "layer_input": normal_values(key_of[0], (TOKENS, D), 1.0, 6.0, ((0, 32),)),
        "norm_one_gain": jnp.clip(1.0 + 0.1 * jax.random.normal(key_of[1], (D,), jnp.float32), 0.5, 1.5).astype(jnp.bfloat16),
        "norm_one_bias": normal_values(key_of[2], (D,), 0.3, 1.75, ((0, 8),)),
        "query_weight": normal_values(key_of[3], (D, D), D ** -0.5, 0.1875, ((0, 4), (1, 8))),
        "query_bias": normal_values(key_of[4], (D,), 0.3, 1.75, ((0, 8),)),
        "key_weight": normal_values(key_of[5], (D, D), D ** -0.5, 0.1875, ((0, 4), (1, 8))),
        "value_weight": normal_values(key_of[6], (D, D), D ** -0.5, 0.1875, ((0, 4), (1, 8))),
        "value_bias": normal_values(key_of[7], (D,), 0.3, 1.75, ((0, 8),)),
        "output_weight": normal_values(key_of[8], (D, D), (D // 32) ** -0.5, 1.0, ((0, 8), (1, 4))),
        "output_bias": normal_values(key_of[9], (D,), 0.3, 1.75, ((0, 8),)),
        "norm_two_gain": jnp.clip(1.0 + 0.1 * jax.random.normal(key_of[10], (D,), jnp.float32), 0.5, 1.5).astype(jnp.bfloat16),
        "norm_two_bias": normal_values(key_of[11], (D,), 0.3, 1.75, ((0, 8),)),
        "up_weight": normal_values(key_of[12], (D, FF), D ** -0.5, 0.1875, ((0, 4), (1, 8))),
        "up_bias": normal_values(key_of[13], (FF,), 0.3, 1.75, ((0, 8),)),
        "down_weight": normal_values(key_of[14], (FF, D), FF ** -0.5, 0.09375, ((0, 8), (1, 4))),
        "down_bias": normal_values(key_of[15], (D,), 0.3, 1.75, ((0, 8),)),
        "cotangent": gaussian_with(key_of[16], (TOKENS, D), 1.0, 6.0, ((0, 32),), (0, 1, 32, 2.75)),
    }


@jax.custom_vjp
def low(v):
    return lax.optimization_barrier(v.astype(jnp.bfloat16)).astype(jnp.float32)

@jax.custom_vjp
def low_back(v):
    return v

def low_keep(v):
    return (low(v), None)

def low_pass(kept, grad):
    return (grad,)

def back_keep(v):
    return (v, None)

def back_low(kept, grad):
    return (low(grad),)
low.defvjp(low_keep, low_pass)
low_back.defvjp(back_keep, back_low)

def matmul(left, right):
    return jnp.dot(left, right, precision=lax.Precision.HIGHEST, preferred_element_type=jnp.float32)

def layer_norm(value, gain, shift):
    center = value - lax.optimization_barrier(jnp.mean(value, axis=-1, keepdims=True))
    spread = lax.optimization_barrier(jnp.mean(center * center, axis=-1, keepdims=True))
    return center * lax.rsqrt(spread + 1e-06) * gain + shift

def attend_image(pieces):
    query, key, value = pieces
    scores = jnp.einsum('qhd,khd->hqk', query, key, precision=lax.Precision.HIGHEST) * HD ** (-0.5)
    scores = low_back(scores)
    probs = low(jax.nn.softmax(scores, axis=-1))
    return jnp.einsum('hqk,khd->qhd', probs, value, precision=lax.Precision.HIGHEST)

def forward(layer_input, norm_one_gain, norm_one_bias, query_weight, query_bias, key_weight, value_weight, value_bias, output_weight, output_bias, norm_two_gain, norm_two_bias, up_weight, up_bias, down_weight, down_bias):
    normed = low(layer_norm(layer_input, norm_one_gain, norm_one_bias))
    query = low_back(low(matmul(normed, query_weight) + query_bias))
    key = low_back(low(matmul(normed, key_weight)))
    value = low_back(low(matmul(normed, value_weight) + value_bias))
    shape = (IMAGES, LENGTH, HEADS, HD)
    mixed = lax.map(jax.checkpoint(attend_image), (query.reshape(shape), key.reshape(shape), value.reshape(shape)))
    mixed = low_back(low(mixed.reshape(IMAGES * LENGTH, D)))
    residual = layer_input + low_back(matmul(mixed, output_weight)) + output_bias
    normed_two = low(layer_norm(low(residual), norm_two_gain, norm_two_bias))
    upper = low_back(matmul(normed_two, up_weight) + up_bias)
    active = low(jax.nn.gelu(upper, approximate=True))
    return residual + matmul(active, down_weight) + down_bias

def reference(layer_input, norm_one_gain, norm_one_bias, query_weight, query_bias, key_weight, value_weight, value_bias, output_weight, output_bias, norm_two_gain, norm_two_bias, up_weight, up_bias, down_weight, down_bias, cotangent):
    params = [item.astype(jnp.float32) for item in (layer_input, norm_one_gain, norm_one_bias, query_weight, query_bias, key_weight, value_weight, value_bias, output_weight, output_bias, norm_two_gain, norm_two_bias, up_weight, up_bias, down_weight, down_bias)]
    result, pullback = jax.vjp(forward, *params)
    grads = pullback(cotangent.astype(jnp.float32))
    return (result.astype(jnp.bfloat16), grads[0].astype(jnp.bfloat16), grads[1], grads[2], grads[3], grads[4], grads[5], grads[6], grads[7], grads[8], grads[9], grads[10], grads[11], grads[12], grads[13], grads[14], grads[15])
```

```python
import functools
import math

import jax
import jax.numpy as jnp
from jax import lax
from jax.experimental import pallas as pl
from jax.experimental.pallas import tpu as pltpu
from jax.sharding import PartitionSpec as P

HD = 72
LENGTH = 1024
LANE = 128
BF = jnp.bfloat16
F32 = jnp.float32
MESH = pl.DeviceIdType.MESH
TP = 4
VMEM_LIMIT = 60 << 20
SCALE = HD ** (-0.5)
LOG2E = 1.4426950408889634
ROOT = math.sqrt(2.0 / math.pi)


def nn(left, right):
    return jnp.dot(left, right, preferred_element_type=F32)


def nt(left, right):
    return lax.dot_general(left, right, (((1,), (1,)), ((), ())), preferred_element_type=F32)


def tn(left, right):
    return lax.dot_general(left, right, (((0,), (0,)), ((), ())), preferred_element_type=F32)


def center_rows(rows):
    center = rows - jnp.mean(rows, axis=-1, keepdims=True)
    inverse = lax.rsqrt(jnp.mean(center * center, axis=-1, keepdims=True) + 1e-06)
    return center * inverse, inverse


def norm_back(grad, gain, hat, inverse):
    scaled = grad * gain
    mean = jnp.mean(scaled, axis=-1, keepdims=True)
    proj = jnp.mean(scaled * hat, axis=-1, keepdims=True)
    return inverse * (scaled - mean - hat * proj)


def lanes(value, start, width, keep):
    full = value.shape[1]
    moved = value if start == 0 else pltpu.roll(value, full - start, 1)
    part = moved[:, :width]
    return jnp.where(lax.broadcasted_iota(jnp.int32, part.shape, 1) < keep, part, 0.0)


def spread(value, start, full):
    wide = jnp.concatenate([value, jnp.zeros((value.shape[0], full - value.shape[1]), F32)], axis=1)
    return wide if start == 0 else pltpu.roll(wide, start, 1)


class Place:
    def __init__(self):
        gx, gy = lax.axis_index("gx"), lax.axis_index("gy")
        self.gx, self.gy = gx, gy
        self.t, self.r = lax.rem(gy, 4), lax.div(gy, 4)
        y, z = lax.rem(gy, 2), lax.rem(lax.div(gy, 2), 2)
        self.ty = self.t + 1 - 2 * y
        self.tz = self.t + 2 - 4 * z
        self.td = 3 - self.t
        base = 4 * self.r
        self.near_y = (gx, base + self.ty)
        self.near_z = (gx, base + self.tz)
        self.other_r = 1 - self.r
        self.half = (gx, lax.rem(gy + 4, 8))
        self.core_bit, self.x_bit = lax.rem(gx, 2), lax.div(gx, 2)
        self.gx_core = gx + 1 - 2 * self.core_bit
        self.gx_x = lax.rem(gx + 2, 4)
        self.core = (self.gx_core, gy)
        self.chip_x = (self.gx_x, gy)


def greet(peers):
    barrier = pltpu.get_barrier_semaphore()
    for peer in peers:
        pl.semaphore_signal(barrier, inc=1, device_id=peer, device_id_type=MESH)
    pl.semaphore_wait(barrier, len(peers))


class Sends:
    def __init__(self, send_sem, recv_sem):
        self.send_sem, self.recv_sem, self.copies = send_sem, recv_sem, {}

    def start(self, index, source, target, peer):
        copy = pltpu.make_async_remote_copy(
            src_ref=source,
            dst_ref=target,
            send_sem=self.send_sem.at[index],
            recv_sem=self.recv_sem.at[index],
            device_id=peer,
            device_id_type=MESH,
        )
        copy.start()
        self.copies[index] = copy

    def arrived(self, *indices):
        for index in indices:
            self.copies[index].wait_recv()

    def left(self):
        for copy in self.copies.values():
            copy.wait_send()


class Gather:
    def __init__(self, place, source, target, send_sem, recv_sem):
        self.p, self.dst = place, target
        self.sends = Sends(send_sem, recv_sem)
        half = source.shape[0] // 2
        self.lo, self.hi = pl.ds(0, half), pl.ds(half, half)
        self.src = source

    def begin(self):
        p, own = self.p, self.dst.at[self.p.t]
        for index, part, peer in (
            (0, self.lo, p.near_y),
            (2, self.hi, p.near_z),
            (1, self.hi, p.near_y),
            (3, self.lo, p.near_z),
        ):
            self.sends.start(index, self.src.at[part], own.at[part], peer)

    def forward(self):
        p = self.p
        self.sends.arrived(0)
        block = self.dst.at[p.ty].at[self.lo]
        self.sends.start(4, block, block, p.near_z)
        self.sends.arrived(2)
        block = self.dst.at[p.tz].at[self.hi]
        self.sends.start(5, block, block, p.near_y)

    def near(self):
        self.sends.arrived(1, 3)

    def far(self):
        self.sends.arrived(4, 5)

    def end(self):
        self.sends.left()


class Scatter:
    def __init__(self, place, part, from_y, from_z, relay_y, relay_z, send_sem, recv_sem):
        self.p, self.part = place, part
        self.from_y, self.from_z, self.relay_y, self.relay_z = from_y, from_z, relay_y, relay_z
        self.sends = Sends(send_sem, recv_sem)
        half = part.shape[1] // 2
        self.lo, self.hi = pl.ds(0, half), pl.ds(half, half)

    def far(self):
        p, block = self.p, self.part.at[self.p.td]
        self.sends.start(0, block.at[self.lo], self.relay_y, p.near_y)
        self.sends.start(1, block.at[self.hi], self.relay_z, p.near_z)

    def near_y(self):
        p = self.p
        self.sends.start(2, self.part.at[p.ty].at[self.lo], self.from_y.at[self.lo], p.near_y)

    def near_z(self):
        p = self.p
        self.sends.start(3, self.part.at[p.tz].at[self.hi], self.from_z.at[self.hi], p.near_z)

    def relay(self):
        p, half = self.p, self.relay_y.shape[0]
        self.sends.arrived(0)
        block = self.part.at[p.tz]
        block[:half] = (block[:half].astype(F32) + self.relay_y[...].astype(F32)).astype(BF)
        self.sends.start(4, block.at[self.lo], self.from_z.at[self.lo], p.near_z)
        self.sends.arrived(1)
        block = self.part.at[p.ty]
        block[half:] = (block[half:].astype(F32) + self.relay_z[...].astype(F32)).astype(BF)
        self.sends.start(5, block.at[self.hi], self.from_y.at[self.hi], p.near_y)

    def total(self):
        self.sends.arrived(2, 3, 4, 5)
        own = self.part[self.p.t].astype(F32)
        return own + self.from_y[...].astype(F32) + self.from_z[...].astype(F32)

    def end(self):
        self.sends.left()


class Spread:
    def __init__(self, place, source, target, send_sem, recv_sem, local_sem):
        self.p, self.src, self.dst = place, source, target
        self.sends = Sends(send_sem, recv_sem)
        self.local = pltpu.make_async_copy(source, target.at[place.r, place.gx], local_sem)

    def begin(self):
        p = self.p
        slot = self.dst.at[p.r, p.gx]
        self.sends.start(0, self.src, slot, p.half)
        self.sends.start(1, self.src, slot, p.chip_x)
        self.sends.start(2, self.src, slot, p.core)
        self.local.start()

    def second(self):
        p = self.p
        self.sends.arrived(0)
        slot = self.dst.at[p.other_r, p.gx]
        self.sends.start(3, slot, slot, p.chip_x)
        self.sends.start(4, slot, slot, p.core)

    def third(self):
        p = self.p
        self.sends.arrived(1)
        slot = self.dst.at[p.r, p.gx_x]
        self.sends.start(5, slot, slot, p.core)
        self.sends.arrived(3)
        slot = self.dst.at[p.other_r, p.gx_x]
        self.sends.start(6, slot, slot, p.core)

    def done(self):
        self.sends.arrived(2, 4, 5, 6)
        self.local.wait()

    def end(self):
        self.sends.left()


class Reduce:
    def __init__(self, place, source, own, first, second, third, send_sem, recv_sem):
        self.p, self.src, self.own = place, source, own
        self.b1, self.b2, self.b3 = first, second, third
        self.sends = Sends(send_sem, recv_sem)

    def begin(self):
        p = self.p
        index = 0
        for group in (p.other_r, p.r):
            for side in (1 - p.x_bit, p.x_bit):
                block = self.src.at[group, 2 * side + 1 - p.core_bit]
                self.sends.start(index, block, self.b1.at[group, side], p.core)
                index += 1

    def second(self):
        p = self.p
        for index, group in ((0, p.other_r), (2, p.r)):
            self.sends.arrived(index)
            block = self.b1.at[group, 1 - p.x_bit]
            block[...] = (
                block[...].astype(F32) + self.own(group, 1 - p.x_bit).astype(F32)
            ).astype(BF)
            self.sends.start(4 + index // 2, block, self.b2.at[group], p.chip_x)
        for index, group in ((1, p.other_r), (3, p.r)):
            self.sends.arrived(index)
            block = self.b1.at[group, p.x_bit]
            block[...] = (block[...].astype(F32) + self.own(group, p.x_bit).astype(F32)).astype(BF)

    def third(self):
        p = self.p
        self.sends.arrived(4)
        block = self.b2.at[p.other_r]
        block[...] = (
            block[...].astype(F32) + self.b1[p.other_r, p.x_bit].astype(F32)
        ).astype(BF)
        self.sends.start(6, block, self.b3, p.half)

    def total(self):
        p = self.p
        self.sends.arrived(5, 6)
        return (
            self.b2[p.r].astype(F32) + self.b1[p.r, p.x_bit].astype(F32) + self.b3[...].astype(F32)
        )

    def end(self):
        self.sends.left()


def flat(block):
    return block.reshape(block.shape[0] * block.shape[1], block.shape[2])


def attention_kernel(
    x, small, a_own, f_own, cot,
    o_res, o_n2, o_norm, o_qkv, o_lse, o_mix, o_vec, o_up, o_a, o_f, o_cot,
    x_all, small_all, a_all, v_t, out_s, part, from_y, from_z, relay_y, relay_z,
    x_ss, x_rs, s_ss, s_rs, a_ss, a_rs, f_ss, f_rs, c_ss, c_rs, p_ss, p_rs, l_sem,
):
    p = Place()
    rows, width = x.shape
    greet([(p.gx, lax.rem(p.gy + d, 8)) for d in range(1, 8)] + [p.core, p.chip_x])
    gather = Gather(p, x, x_all, x_ss, x_rs)
    gather.begin()
    smalls = Sends(s_ss, s_rs)
    for d in range(1, 8):
        peer = (p.gx, lax.rem(p.gy + d, 8))
        smalls.start(d - 1, small, small_all.at[p.gy], peer)
    attn_w = Spread(p, a_own, a_all, a_ss, a_rs, l_sem.at[0])
    attn_w.begin()
    feed_w = Spread(p, f_own, o_f, f_ss, f_rs, l_sem.at[1])
    cots = Gather(p, cot, o_cot, c_ss, c_rs)
    small_all[p.gy] = small[...]
    smalls.arrived(*range(7))
    vec = jnp.zeros((16, width), F32)
    per = width // 8
    wide = -(-per // LANE) * LANE
    for g in range(8):
        vec = vec + spread(small_all[g].astype(F32)[:, :wide], per * g, width)
    o_vec[...] = vec
    for group in range(2):
        o_up[group] = jnp.broadcast_to(small_all[p.t + 4 * group, 1:2, :].astype(F32), o_up.shape[1:])
    gain, shift = vec[2:3], vec[3:4]

    def norm(index, block):
        hat, _ = center_rows(block.astype(F32))
        o_norm[index] = (hat * gain + shift).astype(BF)

    norm(p.t, x[...])
    attn_w.second()
    gather.forward()
    gather.near()
    norm(p.ty, x_all[p.ty])
    norm(p.tz, x_all[p.tz])
    feed_w.begin()
    attn_w.third()
    gather.far()
    norm(p.td, x_all[p.td])
    attn_w.done()
    attn_copy = pltpu.make_async_copy(a_all, o_a, l_sem.at[2])
    attn_copy.start()
    cots.begin()

    def project(index, carry):
        block = o_norm[index]
        for group in range(2):
            bias = small_all[p.t + 4 * group, 0:1, :].astype(F32)[:, :512]
            packed = nn(block, flat(a_all[group])[:, :512]) + bias
            for piece in range(6):
                o_qkv[piece // 2, 2 * group + piece % 2, pl.ds(index * rows, rows)] = lanes(
                    packed, HD * piece, LANE, HD
                ).astype(BF)
        return carry

    lax.fori_loop(0, 4, project, 0)
    for head in range(4):
        v_t[head] = o_qkv[2, head].astype(F32).T.astype(BF)
    scatter = Scatter(p, part, from_y, from_z, relay_y, relay_z, p_ss, p_rs)

    def attend(index):
        def one(head, carry):
            start = pl.multiple_of(index * rows, rows)
            scores = nt(o_qkv[1, head], o_qkv[0, head, pl.ds(start, rows)])
            top = jnp.max(scores, axis=0, keepdims=True)
            expo = jnp.exp2((scores - top) * (SCALE * LOG2E))
            total = jnp.sum(expo, axis=0, keepdims=True)
            mixed = nn(v_t[head], expo.astype(BF)) / total
            out_s[head] = mixed.T
            o_lse[head, index] = jnp.broadcast_to(
                top * (SCALE * LOG2E) + jnp.log2(total), o_lse.shape[2:]
            )
            return carry

        lax.fori_loop(0, 4, one, 0)
        total = jnp.zeros((rows, width), F32)
        for group in range(2):
            mix = (
                spread(out_s[2 * group], 48, 256) + spread(out_s[2 * group + 1], 48 + HD, 256)
            ).astype(BF)
            o_mix[group, pl.ds(pl.multiple_of(index * rows, rows), rows)] = mix
            total = total + nt(mix, flat(a_all[group])[:, 384:640])
        part[index] = total.astype(BF)

    attend(p.td)
    scatter.far()
    feed_w.second()
    attend(p.ty)
    scatter.near_y()
    attend(p.tz)
    scatter.near_z()
    cots.forward()
    attend(p.t)
    scatter.relay()
    feed_w.third()
    summed = scatter.total()
    residual = x[...].astype(F32) + summed + vec[4:5]
    o_res[...] = residual
    hat, _ = center_rows(residual.astype(BF).astype(F32))
    o_n2[...] = (hat * vec[5:6] + vec[6:7]).astype(BF)
    cots.near()
    cots.far()
    feed_w.done()
    attn_copy.wait()
    smalls.left()
    for item in (gather, attn_w, feed_w, cots, scatter):
        item.end()


def feed_kernel(
    n2, res, vec, up_bias, cot, c_all_hbm, f_hbm,
    o_out, o_dres, o_e, o_gf, o_sums, o_cols,
    n_all, c_all, f_all, act_s, dup_s, part_m, part_d,
    m_y, m_z, m_ry, m_rz, d_y, d_z, d_ry, d_rz,
    n_ss, n_rs, m_ss, m_rs, d_ss, d_rs, l_sem,
):
    p = Place()
    rows, width = n2.shape
    hid = f_all.shape[3] // 2
    loads = [
        pltpu.make_async_copy(f_hbm, f_all, l_sem.at[0]),
        pltpu.make_async_copy(c_all_hbm.at[p.ty], c_all.at[p.ty], l_sem.at[1]),
        pltpu.make_async_copy(c_all_hbm.at[p.tz], c_all.at[p.tz], l_sem.at[2]),
        pltpu.make_async_copy(c_all_hbm.at[p.td], c_all.at[p.td], l_sem.at[3]),
    ]
    for load in loads:
        load.start()
    diag = (p.gx, 4 * p.r + p.td)
    greet([p.near_y, p.near_z, diag])
    gather = Gather(p, n2, n_all, n_ss, n_rs)
    gather.begin()
    n_all[p.t] = n2[...]
    c_all[p.t] = cot[...]
    for load in loads:
        load.wait()
    sc_m = Scatter(p, part_m, m_y, m_z, m_ry, m_rz, m_ss, m_rs)
    sc_d = Scatter(p, part_d, d_y, d_z, d_ry, d_rz, d_ss, d_rs)
    o_cols[...] = jnp.zeros_like(o_cols)

    def block(index):
        rows_two, rows_c = n_all[index], c_all[index]
        out_m = jnp.zeros((rows, width), F32)
        out_d = jnp.zeros((rows, width), F32)
        for group in range(2):
            upper = nn(rows_two, flat(f_all[group])[:, :hid]) + up_bias[group, 0:1]
            square = upper * upper
            tanh = jnp.tanh(ROOT * upper * (1.0 + 0.044715 * square))
            active = 0.5 * upper * (1.0 + tanh)
            slope = 0.5 * (1.0 + tanh) + 0.5 * upper * (1.0 - tanh * tanh) * (
                ROOT * (1.0 + 3.0 * 0.044715 * square)
            )
            act = active.astype(BF)
            act_s[group, index] = act
            dup = (nn(rows_c, flat(f_all[group])[:, hid:]) * slope).astype(BF)
            dup_s[group, index] = dup
            o_cols[group : group + 1] += jnp.sum(dup.astype(F32), axis=0, keepdims=True)
            out_m = out_m + nt(act, flat(f_all[group])[:, hid:])
            out_d = out_d + nt(dup, flat(f_all[group])[:, :hid])
        part_m[index] = out_m.astype(BF)
        part_d[index] = out_d.astype(BF)

    block(p.t)
    gather.forward()
    gather.near()
    block(p.ty)
    sc_d.near_y()
    sc_m.near_y()
    block(p.tz)
    sc_d.near_z()
    sc_m.near_z()
    gather.far()
    block(p.td)
    sc_d.far()
    sc_m.far()
    for group in range(2):
        grad = tn(flat(n_all[...]), flat(dup_s[group])).astype(BF)
        o_gf[group, :, :, :hid] = grad.reshape(4, width // 4, hid)
        if group == 0:
            sc_d.relay()
    sc_m.relay()
    for group in range(2):
        grad = tn(flat(c_all[...]), flat(act_s[group])).astype(BF)
        o_gf[group, :, :, hid:] = grad.reshape(4, width // 4, hid)
    grad = sc_d.total()
    hat, inverse = center_rows(res[...].astype(BF).astype(F32))
    cot_f = cot[...].astype(F32)
    d_res = cot_f + norm_back(grad, vec[5:6], hat, inverse)
    o_dres[...] = d_res
    o_e[...] = d_res.astype(BF)
    o_sums[...] = jnp.zeros_like(o_sums)
    o_sums[2:3] = jnp.sum(d_res, axis=0, keepdims=True)
    o_sums[3:4] = jnp.sum(grad * hat, axis=0, keepdims=True)
    o_sums[4:5] = jnp.sum(grad, axis=0, keepdims=True)
    o_sums[5:6] = jnp.sum(cot_f, axis=0, keepdims=True)
    o_out[...] = (res[...] + sc_m.total() + vec[7:8]).astype(BF)
    for item in (gather, sc_m, sc_d):
        item.end()


def back_kernel(
    e_own, d_res, x, vec, sums, cols, lse, norm_hbm, qkv_hbm, mix_hbm, a_hbm, gf_hbm,
    o_gx, o_ga, o_gf, o_small,
    e_all, norm_all, qkv, mix, a_all, k_t, dm_s, dq_s, dk_s, dv_s, pack_s, part,
    from_y, from_z, relay_y, relay_z,
    gf_own, f1, f2, f3, ga, a1, a2, a3, sv, rv, cs, rcs, rt,
    e_ss, e_rs, p_ss, p_rs, f_ss, f_rs, a_ss, a_rs, v_ss, v_rs, t_ss, t_rs, l_sem,
):
    p = Place()
    rows, width = e_own.shape
    loads = [
        pltpu.make_async_copy(qkv_hbm, qkv, l_sem.at[0]),
        pltpu.make_async_copy(a_hbm, a_all, l_sem.at[1]),
        pltpu.make_async_copy(mix_hbm, mix, l_sem.at[2]),
        pltpu.make_async_copy(norm_hbm, norm_all, l_sem.at[3]),
    ]
    for group in range(2):
        for side in range(2):
            loads.append(
                pltpu.make_async_copy(
                    gf_hbm.at[group, 2 * side + p.core_bit],
                    gf_own.at[group, side],
                    l_sem.at[4 + 2 * group + side],
                )
            )
    for load in loads:
        load.start()
    greet(
        [(p.gx, lax.rem(p.gy + d, 8)) for d in range(1, 8)]
        + [(lax.rem(p.gx + d, 4), p.gy) for d in range(1, 4)]
    )
    gather = Gather(p, e_own, e_all, e_ss, e_rs)
    gather.begin()
    feed_g = Reduce(p, gf_hbm, lambda g, s: gf_own[g, s], f1, f2, f3, f_ss, f_rs)
    feed_g.begin()
    e_all[p.t] = e_own[...]
    for load in loads:
        load.wait()
    for head in range(4):
        k_t[head] = qkv[1, head].astype(F32).T.astype(BF)
    dk_s[...] = jnp.zeros_like(dk_s)
    dv_s[...] = jnp.zeros_like(dv_s)

    def attend_back(index):
        block = e_all[index]
        for group in range(2):
            mixed = nn(block, flat(a_all[group])[:, 384:640])
            dm_s[2 * group] = lanes(mixed, 48, LANE, HD).astype(BF)
            dm_s[2 * group + 1] = lanes(mixed, 48 + HD, LANE, HD).astype(BF)

        def one(head, carry):
            start = pl.multiple_of(index * rows, rows)
            q_rows, d_mix = qkv[0, head, pl.ds(start, rows)], dm_s[head]
            scores = nt(qkv[1, head], q_rows)
            probs = jnp.exp2(scores * (SCALE * LOG2E) - lse[head, index, 0:1])
            d_probs = nt(qkv[2, head], d_mix)
            delta = jnp.sum(d_probs * probs, axis=0, keepdims=True)
            d_scores = (probs * (d_probs - delta)).astype(BF)
            dv_s[head] += nn(probs.astype(BF), d_mix)
            dk_s[head] += nn(d_scores, q_rows)
            dq_s[head, pl.ds(start, rows)] = nn(k_t[head], d_scores).T * SCALE
            return carry

        lax.fori_loop(0, 4, one, 0)

    attend_back(p.t)
    gather.forward()
    gather.near()
    feed_g.second()
    attend_back(p.ty)
    attend_back(p.tz)
    gather.far()
    attend_back(p.td)
    feed_g.third()
    scatter = Scatter(p, part, from_y, from_z, relay_y, relay_z, p_ss, p_rs)
    cs[...] = jnp.zeros_like(cs)

    def give(index):
        here = pl.ds(pl.multiple_of(index * rows, rows), rows)
        total = jnp.zeros((rows, width), F32)
        for group in range(2):
            packed = jnp.zeros((rows, 512), F32)
            for piece in range(6):
                head = 2 * group + piece % 2
                if piece < 2:
                    value = dq_s[head, here]
                elif piece < 4:
                    value = dk_s[head, here] * SCALE
                else:
                    value = dv_s[head, here]
                packed = packed + spread(value, HD * piece, 512)
            packed = packed.astype(BF)
            pack_s[group, here] = packed
            cs[group, 0:1, :512] += jnp.sum(packed.astype(F32), axis=0, keepdims=True)
            total = total + nt(packed, flat(a_all[group])[:, :512])
        part[index] = total.astype(BF)

    give(p.td)
    scatter.far()
    give(p.ty)
    scatter.near_y()
    give(p.tz)
    scatter.near_z()
    give(p.t)
    for group in range(2):
        main = tn(flat(norm_all[...]), pack_s[group])
        outer = tn(flat(e_all[...]), mix[group])
        both = jnp.concatenate(
            [main[:, :384], main[:, 384:] + outer[:, :128], outer[:, 128:]], axis=1
        )
        ga[group] = both.astype(BF).reshape(4, width // 4, 640)
        if group == 0:
            scatter.relay()
    attn_g = Reduce(
        p, ga, lambda g, s: ga[g, 2 * s + p.core_bit], a1, a2, a3, a_ss, a_rs
    )
    attn_g.begin()
    attn_g.second()
    grad = scatter.total()
    hat, inverse = center_rows(x[...].astype(F32))
    o_gx[...] = (d_res[...] + norm_back(grad, vec[2:3], hat, inverse)).astype(BF)
    row = lax.broadcasted_iota(jnp.int32, sums.shape, 0)
    all_sums = sums[...]
    all_sums = jnp.where(row == 0, jnp.sum(grad * hat, axis=0, keepdims=True), all_sums)
    all_sums = jnp.where(row == 1, jnp.sum(grad, axis=0, keepdims=True), all_sums)
    per = width // 8
    for g in range(8):
        sv[g] = lanes(all_sums, per * g, sv.shape[2], per)
    for group in range(2):
        cs[group, 1:2] = cols[group : group + 1]
    small = Sends(v_ss, v_rs)
    for d in range(1, 8):
        other = lax.rem(p.gy + d, 8)
        small.start(d - 1, sv.at[other], rv.at[p.gy], (p.gx, other))
    small.start(7, cs.at[p.other_r], rcs, p.half)
    rv[p.gy] = sv[p.gy]
    attn_g.third()
    small.arrived(*range(8))
    total = rv[0]
    for g in range(1, 8):
        total = total + rv[g]
    mine = rt.at[p.gx]
    mine[0:8] = jnp.concatenate(
        [total, jnp.zeros((8, rt.shape[2] - total.shape[1]), F32)], axis=1
    )
    mine[8:16] = cs[p.r] + rcs[...]
    wide = Sends(t_ss, t_rs)
    for d in range(1, 4):
        wide.start(d - 1, mine, mine, (lax.rem(p.gx + d, 4), p.gy))
    o_gf[...] = feed_g.total()
    wide.arrived(0, 1, 2)
    o_small[...] = rt[0] + rt[1] + rt[2] + rt[3]
    o_ga[...] = attn_g.total()
    small.left()
    wide.left()
    for item in (gather, feed_g, attn_g, scatter):
        item.end()


VM = pl.BlockSpec(memory_space=pltpu.VMEM)
ANY = pl.BlockSpec(memory_space=pl.ANY)


def dma(count):
    return pltpu.SemaphoreType.DMA((count,))


def pad_lanes(array, width):
    return jnp.pad(array, ((0, 0), (0, width - array.shape[1])))


def fast_shards(
    layer_input, norm_one_gain, norm_one_bias, query_weight, query_bias, key_weight, value_weight,
    value_bias, output_weight, output_bias, norm_two_gain, norm_two_bias, up_weight, up_bias,
    down_weight, down_bias, cotangent,
):
    rows, width = layer_input.shape
    per, hid = query_weight.shape[1], up_weight.shape[1]
    feat = query_weight.shape[0]
    hidp = -(-hid // LANE) * LANE
    aw = 640
    shape, bf, f32 = jax.ShapeDtypeStruct, BF, F32
    a_own = pad_lanes(
        jnp.concatenate([query_weight, key_weight, value_weight, output_weight.T], axis=1), aw
    )
    f_own = jnp.concatenate([pad_lanes(up_weight, hidp), pad_lanes(down_weight.T, hidp)], axis=1)
    none = jnp.zeros((per,), BF)
    line = lambda *items: pad_lanes(jnp.concatenate(items)[None], aw)
    small = jnp.concatenate(
        [line(query_bias, none, value_bias), line(up_bias)]
        + [
            line(item)
            for item in (
                norm_one_gain, norm_one_bias, output_bias, norm_two_gain, norm_two_bias, down_bias
            )
        ]
        + [jnp.zeros((8, aw), BF)],
        axis=0,
    )
    params = lambda number: pltpu.CompilerParams(
        collective_id=number, has_side_effects=True, vmem_limit_bytes=VMEM_LIMIT
    )
    half = (rows // 2, width)
    full = (rows, width)
    (res, n2, normed, qkv, lse, mix, vec, ups, a_all, f_all, c_all) = pl.pallas_call(
        attention_kernel,
        name="attention",
        out_shape=[
            shape(full, f32), shape(full, bf), shape((4, rows, width), bf),
            shape((3, 4, 4 * rows, LANE), bf), shape((4, 4, 8, rows), f32),
            shape((2, 4 * rows, 256), bf), shape((16, width), f32), shape((2, 8, aw), f32),
            shape((2, 4, feat, aw), bf), shape((2, 4, feat, 2 * hidp), bf), shape((4, rows, width), bf),
        ],
        in_specs=[VM, VM, ANY, ANY, ANY],
        out_specs=[VM] * 8 + [ANY] * 3,
        scratch_shapes=[
            pltpu.VMEM((4, rows, width), bf), pltpu.VMEM((8, 16, aw), bf),
            pltpu.VMEM((2, 4, feat, aw), bf), pltpu.VMEM((4, LANE, 4 * rows), bf),
            pltpu.VMEM((4, rows, LANE), f32), pltpu.VMEM((4, rows, width), bf),
            pltpu.VMEM(full, bf), pltpu.VMEM(full, bf), pltpu.VMEM(half, bf), pltpu.VMEM(half, bf),
            dma(6), dma(6), dma(7), dma(7), dma(7), dma(7), dma(7), dma(7), dma(6), dma(6),
            dma(6), dma(6), dma(3),
        ],
        compiler_params=params(0),
    )(layer_input, small, a_own, f_own, cotangent)
    (out, d_res, e, gf, sums, cols) = pl.pallas_call(
        feed_kernel,
        name="feed_forward",
        out_shape=[
            shape(full, bf), shape(full, f32), shape(full, bf),
            shape((2, 4, feat, 2 * hidp), bf), shape((8, width), f32), shape((8, hidp), f32),
        ],
        in_specs=[VM] * 5 + [ANY] * 2,
        out_specs=[VM] * 6,
        scratch_shapes=[
            pltpu.VMEM((4, rows, width), bf), pltpu.VMEM((4, rows, width), bf),
            pltpu.VMEM((2, 4, feat, 2 * hidp), bf), pltpu.VMEM((2, 4, rows, hidp), bf),
            pltpu.VMEM((2, 4, rows, hidp), bf), pltpu.VMEM((4, rows, width), bf),
            pltpu.VMEM((4, rows, width), bf),
            pltpu.VMEM(full, bf), pltpu.VMEM(full, bf), pltpu.VMEM(half, bf), pltpu.VMEM(half, bf),
            pltpu.VMEM(full, bf), pltpu.VMEM(full, bf), pltpu.VMEM(half, bf), pltpu.VMEM(half, bf),
            dma(6), dma(6), dma(6), dma(6), dma(6), dma(6), dma(4),
        ],
        compiler_params=params(1),
    )(n2, res, vec, ups, cotangent, c_all, f_all)
    wide = -(-per // LANE) * LANE
    (grad_input, ga, gfo, smalls) = pl.pallas_call(
        back_kernel,
        name="attention_back",
        out_shape=[
            shape(full, bf), shape((feat, aw), f32), shape((feat, 2 * hidp), f32),
            shape((16, aw), f32),
        ],
        in_specs=[VM] * 7 + [ANY] * 5,
        out_specs=[VM] * 4,
        scratch_shapes=[
            pltpu.VMEM((4, rows, width), bf), pltpu.VMEM((4, rows, width), bf),
            pltpu.VMEM((3, 4, 4 * rows, LANE), bf), pltpu.VMEM((2, 4 * rows, 256), bf),
            pltpu.VMEM((2, 4, feat, aw), bf), pltpu.VMEM((4, LANE, 4 * rows), bf),
            pltpu.VMEM((4, rows, LANE), bf), pltpu.VMEM((4, 4 * rows, LANE), f32),
            pltpu.VMEM((4, 4 * rows, LANE), f32), pltpu.VMEM((4, 4 * rows, LANE), f32),
            pltpu.VMEM((2, 4 * rows, 512), bf), pltpu.VMEM((4, rows, width), bf),
            pltpu.VMEM(full, bf), pltpu.VMEM(full, bf), pltpu.VMEM(half, bf), pltpu.VMEM(half, bf),
            pltpu.VMEM((2, 2, feat, 2 * hidp), bf), pltpu.VMEM((2, 2, feat, 2 * hidp), bf),
            pltpu.VMEM((2, feat, 2 * hidp), bf), pltpu.VMEM((feat, 2 * hidp), bf),
            pltpu.VMEM((2, 4, feat, aw), bf), pltpu.VMEM((2, 2, feat, aw), bf),
            pltpu.VMEM((2, feat, aw), bf), pltpu.VMEM((feat, aw), bf),
            pltpu.VMEM((8, 8, wide), f32), pltpu.VMEM((8, 8, wide), f32),
            pltpu.VMEM((2, 8, aw), f32), pltpu.VMEM((8, aw), f32), pltpu.VMEM((4, 16, aw), f32),
            dma(6), dma(6), dma(6), dma(6), dma(7), dma(7), dma(7), dma(7), dma(8), dma(8),
            dma(3), dma(3), dma(8),
        ],
        compiler_params=params(2),
    )(e, d_res, layer_input, vec, sums, cols, lse, normed, qkv, mix, a_all, gf)
    return (
        out,
        grad_input,
        smalls[0, :per],
        smalls[1, :per],
        ga[:, :per],
        smalls[8, :per],
        ga[:, per : 2 * per],
        ga[:, 2 * per : 3 * per],
        smalls[8, 2 * per : 3 * per],
        ga[:, 3 * per : 4 * per].T,
        smalls[2, :per],
        smalls[3, :per],
        smalls[4, :per],
        gfo[:, :hid],
        smalls[9, :hid],
        gfo[:, hidp : hidp + hid].T,
        smalls[5, :per],
    )


def dot_plain(left, right):
    return jnp.dot(left, right, preferred_element_type=jnp.float32)


def dot_right_t(left, right):
    return lax.dot_general(
        left, right, (((1,), (1,)), ((), ())), preferred_element_type=jnp.float32
    )


def dot_left_t(left, right):
    return lax.dot_general(
        left, right, (((0,), (0,)), ((), ())), preferred_element_type=jnp.float32
    )


def normalize(rows):
    center = rows - jnp.mean(rows, axis=-1, keepdims=True)
    inverse = lax.rsqrt(jnp.mean(center * center, axis=-1, keepdims=True) + 1e-06)
    return (center * inverse, inverse)


def gelu_tanh(value):
    return jax.nn.gelu(value, approximate=True)


def image_shape(array):
    heads = array.shape[1] // HD
    return (array.shape[0] // LENGTH, LENGTH, heads, HD)


def attend(query, key, value):
    shape = image_shape(query)
    scale = HD ** (-0.5)

    def one_image(carry, pieces):
        q_img, k_img, v_img = pieces
        scores = (
            jnp.einsum("qhd,khd->hqk", q_img, k_img, preferred_element_type=jnp.float32) * scale
        )
        top = jnp.max(scores, axis=-1, keepdims=True)
        expo = jnp.exp(scores - top)
        total = jnp.sum(expo, axis=-1, keepdims=True)
        probs = (expo / total).astype(jnp.bfloat16)
        mixed = jnp.einsum("hqk,khd->qhd", probs, v_img, preferred_element_type=jnp.float32).astype(
            jnp.bfloat16
        )
        return (carry, (mixed, (top + jnp.log(total))[..., 0]))

    _, (mixed, lse) = lax.scan(
        one_image, 0, (query.reshape(shape), key.reshape(shape), value.reshape(shape))
    )
    return (mixed.reshape(query.shape), lse)


def attend_back(query, key, value, lse, d_mixed):
    shape = image_shape(query)
    scale = HD ** (-0.5)

    def one_image(carry, pieces):
        q_img, k_img, v_img, lse_img, dm_img = pieces
        scores = (
            jnp.einsum("qhd,khd->hqk", q_img, k_img, preferred_element_type=jnp.float32) * scale
        )
        probs = jnp.exp(scores - lse_img[..., None])
        d_probs = jnp.einsum("qhd,khd->hqk", dm_img, v_img, preferred_element_type=jnp.float32)
        d_scores = (probs * (d_probs - jnp.sum(d_probs * probs, axis=-1, keepdims=True))).astype(
            jnp.bfloat16
        )
        d_value = jnp.einsum(
            "hqk,qhd->khd", probs.astype(jnp.bfloat16), dm_img, preferred_element_type=jnp.float32
        ).astype(jnp.bfloat16)
        d_query = (
            jnp.einsum("hqk,khd->qhd", d_scores, k_img, preferred_element_type=jnp.float32) * scale
        ).astype(jnp.bfloat16)
        d_key = (
            jnp.einsum("hqk,qhd->khd", d_scores, q_img, preferred_element_type=jnp.float32) * scale
        ).astype(jnp.bfloat16)
        return (carry, (d_query, d_key, d_value))

    _, (d_query, d_key, d_value) = lax.scan(
        one_image,
        0,
        (
            query.reshape(shape),
            key.reshape(shape),
            value.reshape(shape),
            lse,
            d_mixed.reshape(shape),
        ),
    )
    return (d_query.reshape(query.shape), d_key.reshape(query.shape), d_value.reshape(query.shape))


def forward_pass(
    layer_input,
    norm_one_gain,
    norm_one_bias,
    query_weight,
    query_bias,
    key_weight,
    value_weight,
    value_bias,
    output_weight,
    output_bias,
    norm_two_gain,
    norm_two_bias,
    up_weight,
    up_bias,
    down_weight,
    down_bias,
):
    w_query, w_key, w_value, w_output, w_up, w_down = (
        lax.all_gather(query_weight, "gx", axis=0, tiled=True),
        lax.all_gather(key_weight, "gx", axis=0, tiled=True),
        lax.all_gather(value_weight, "gx", axis=0, tiled=True),
        lax.all_gather(output_weight, "gx", axis=1, tiled=True),
        lax.all_gather(up_weight, "gx", axis=0, tiled=True),
        lax.all_gather(down_weight, "gx", axis=1, tiled=True),
    )
    rows_one, gain_one, shift_one, out_shift, down_shift = (
        lax.all_gather(layer_input, "gy", axis=0, tiled=True),
        lax.all_gather(norm_one_gain, "gy", axis=0, tiled=True),
        lax.all_gather(norm_one_bias, "gy", axis=0, tiled=True),
        lax.all_gather(output_bias, "gy", axis=0, tiled=True),
        lax.all_gather(down_bias, "gy", axis=0, tiled=True),
    )
    hat_one, inv_one = normalize(rows_one.astype(jnp.float32))
    normed = (hat_one * gain_one.astype(jnp.float32) + shift_one.astype(jnp.float32)).astype(
        jnp.bfloat16
    )
    query = (dot_plain(normed, w_query) + query_bias.astype(jnp.float32)).astype(jnp.bfloat16)
    key = dot_plain(normed, w_key).astype(jnp.bfloat16)
    value = (dot_plain(normed, w_value) + value_bias.astype(jnp.float32)).astype(jnp.bfloat16)
    mixed, lse = attend(query, key, value)
    attn_part = lax.psum_scatter(
        dot_plain(mixed, w_output).astype(jnp.bfloat16), "gy", scatter_dimension=0, tiled=True
    ).astype(jnp.float32)
    residual = layer_input.astype(jnp.float32) + attn_part + out_shift.astype(jnp.float32)
    rows_two, gain_two, shift_two = (
        lax.all_gather(residual.astype(jnp.bfloat16), "gy", axis=0, tiled=True),
        lax.all_gather(norm_two_gain, "gy", axis=0, tiled=True),
        lax.all_gather(norm_two_bias, "gy", axis=0, tiled=True),
    )
    hat_two, inv_two = normalize(rows_two.astype(jnp.float32))
    normed_two = (hat_two * gain_two.astype(jnp.float32) + shift_two.astype(jnp.float32)).astype(
        jnp.bfloat16
    )
    upper = dot_plain(normed_two, w_up) + up_bias.astype(jnp.float32)
    active = gelu_tanh(upper).astype(jnp.bfloat16)
    mlp_part = lax.psum_scatter(
        dot_plain(active, w_down).astype(jnp.bfloat16), "gy", scatter_dimension=0, tiled=True
    ).astype(jnp.float32)
    result = (residual + mlp_part + down_shift.astype(jnp.float32)).astype(jnp.bfloat16)
    saved = (
        w_query,
        w_key,
        w_value,
        w_output,
        w_up,
        w_down,
        hat_one,
        inv_one,
        normed,
        query,
        key,
        value,
        mixed,
        lse,
        hat_two,
        inv_two,
        normed_two,
        upper,
        active,
        gain_one,
        gain_two,
    )
    return saved, result


def shards(
    layer_input,
    norm_one_gain,
    norm_one_bias,
    query_weight,
    query_bias,
    key_weight,
    value_weight,
    value_bias,
    output_weight,
    output_bias,
    norm_two_gain,
    norm_two_bias,
    up_weight,
    up_bias,
    down_weight,
    down_bias,
    cotangent,
):
    inputs = (
        layer_input,
        norm_one_gain,
        norm_one_bias,
        query_weight,
        query_bias,
        key_weight,
        value_weight,
        value_bias,
        output_weight,
        output_bias,
        norm_two_gain,
        norm_two_bias,
        up_weight,
        up_bias,
        down_weight,
        down_bias,
    )
    saved, layer_output = forward_pass(*inputs)
    (
        w_query,
        w_key,
        w_value,
        w_output,
        w_up,
        w_down,
        hat_one,
        inv_one,
        normed,
        query,
        key,
        value,
        mixed,
        lse,
        hat_two,
        inv_two,
        normed_two,
        upper,
        active,
        gain_one,
        gain_two,
    ) = saved
    local = layer_input.shape[0]
    start = lax.axis_index("gy") * local
    grad_rows = lax.all_gather(cotangent, "gy", axis=0, tiled=True)
    d_active = dot_right_t(grad_rows, w_down)
    _, gelu_pull = jax.vjp(gelu_tanh, upper)
    d_upper = gelu_pull(d_active)[0].astype(jnp.bfloat16)
    grad_up_weight, grad_down_weight = (
        lax.psum_scatter(
            dot_left_t(normed_two, d_upper).astype(jnp.bfloat16),
            "gx",
            scatter_dimension=0,
            tiled=True,
        ).astype(jnp.float32),
        lax.psum_scatter(
            dot_left_t(active, grad_rows).astype(jnp.bfloat16),
            "gx",
            scatter_dimension=1,
            tiled=True,
        ).astype(jnp.float32),
    )
    d_normed_two = lax.psum_scatter(
        dot_right_t(d_upper, w_up).astype(jnp.bfloat16), "gy", scatter_dimension=0, tiled=True
    ).astype(jnp.float32)
    hat_two_local = lax.dynamic_slice_in_dim(hat_two, start, local, 0)
    inv_two_local = lax.dynamic_slice_in_dim(inv_two, start, local, 0)
    scaled_two = d_normed_two * gain_two.astype(jnp.float32)
    mean_two = jnp.mean(scaled_two, axis=-1, keepdims=True)
    proj_two = jnp.mean(scaled_two * hat_two_local, axis=-1, keepdims=True)
    cot_float = cotangent.astype(jnp.float32)
    d_residual = cot_float + inv_two_local * (scaled_two - mean_two - hat_two_local * proj_two)
    part_two_gain = jnp.sum(d_normed_two * hat_two_local, axis=0)
    part_two_bias = jnp.sum(d_normed_two, axis=0)
    part_up_bias = jnp.sum(d_upper.astype(jnp.float32), axis=0)
    part_down_bias = jnp.sum(cot_float, axis=0)
    grad_attn = lax.all_gather(d_residual.astype(jnp.bfloat16), "gy", axis=0, tiled=True)
    part_output_bias = jnp.sum(d_residual, axis=0)
    d_mixed = dot_right_t(grad_attn, w_output).astype(jnp.bfloat16)
    d_query, d_key, d_value = attend_back(query, key, value, lse, d_mixed)
    grad_query_weight, grad_key_weight, grad_value_weight, grad_output_weight = (
        lax.psum_scatter(
            dot_left_t(normed, d_query).astype(jnp.bfloat16), "gx", scatter_dimension=0, tiled=True
        ).astype(jnp.float32),
        lax.psum_scatter(
            dot_left_t(normed, d_key).astype(jnp.bfloat16), "gx", scatter_dimension=0, tiled=True
        ).astype(jnp.float32),
        lax.psum_scatter(
            dot_left_t(normed, d_value).astype(jnp.bfloat16), "gx", scatter_dimension=0, tiled=True
        ).astype(jnp.float32),
        lax.psum_scatter(
            dot_left_t(mixed, grad_attn).astype(jnp.bfloat16), "gx", scatter_dimension=1, tiled=True
        ).astype(jnp.float32),
    )
    d_normed = lax.psum_scatter(
        (
            dot_right_t(d_query, w_query)
            + dot_right_t(d_key, w_key)
            + dot_right_t(d_value, w_value)
        ).astype(jnp.bfloat16),
        "gy",
        scatter_dimension=0,
        tiled=True,
    ).astype(jnp.float32)
    hat_one_local = lax.dynamic_slice_in_dim(hat_one, start, local, 0)
    inv_one_local = lax.dynamic_slice_in_dim(inv_one, start, local, 0)
    scaled_one = d_normed * gain_one.astype(jnp.float32)
    mean_one = jnp.mean(scaled_one, axis=-1, keepdims=True)
    proj_one = jnp.mean(scaled_one * hat_one_local, axis=-1, keepdims=True)
    grad_input = (
        d_residual + inv_one_local * (scaled_one - mean_one - hat_one_local * proj_one)
    ).astype(jnp.bfloat16)
    part_one_gain = jnp.sum(d_normed * hat_one_local, axis=0)
    part_one_bias = jnp.sum(d_normed, axis=0)
    part_query_bias = jnp.sum(d_query.astype(jnp.float32), axis=0)
    part_value_bias = jnp.sum(d_value.astype(jnp.float32), axis=0)
    feat_one_gain, feat_one_bias, feat_output_bias, feat_two_gain, feat_two_bias, feat_down_bias = (
        lax.psum_scatter(part_one_gain, "gy", scatter_dimension=0, tiled=True),
        lax.psum_scatter(part_one_bias, "gy", scatter_dimension=0, tiled=True),
        lax.psum_scatter(part_output_bias, "gy", scatter_dimension=0, tiled=True),
        lax.psum_scatter(part_two_gain, "gy", scatter_dimension=0, tiled=True),
        lax.psum_scatter(part_two_bias, "gy", scatter_dimension=0, tiled=True),
        lax.psum_scatter(part_down_bias, "gy", scatter_dimension=0, tiled=True),
    )
    (
        grad_one_gain,
        grad_one_bias,
        grad_query_bias,
        grad_value_bias,
        grad_output_bias,
        grad_two_gain,
        grad_two_bias,
        grad_up_bias,
        grad_down_bias,
    ) = lax.psum(
        (
            feat_one_gain,
            feat_one_bias,
            part_query_bias,
            part_value_bias,
            feat_output_bias,
            feat_two_gain,
            feat_two_bias,
            part_up_bias,
            feat_down_bias,
        ),
        "gx",
    )
    return (
        layer_output,
        grad_input,
        grad_one_gain,
        grad_one_bias,
        grad_query_weight,
        grad_query_bias,
        grad_key_weight,
        grad_value_weight,
        grad_value_bias,
        grad_output_weight,
        grad_output_bias,
        grad_two_gain,
        grad_two_bias,
        grad_up_weight,
        grad_up_bias,
        grad_down_weight,
        grad_down_bias,
    )


def solution(mesh):
    fits = mesh.shape["gx"] == 4 and mesh.shape["gy"] == 8
    return jax.shard_map(
        fast_shards if fits else shards,
        mesh=mesh,
        in_specs=(
            P(("gx", "gy"), None),
            P("gy"),
            P("gy"),
            P("gx", "gy"),
            P("gy"),
            P("gx", "gy"),
            P("gx", "gy"),
            P("gy"),
            P("gy", "gx"),
            P("gy"),
            P("gy"),
            P("gy"),
            P("gx", "gy"),
            P("gy"),
            P("gy", "gx"),
            P("gy"),
            P(("gx", "gy"), None),
        ),
        out_specs=(
            P(("gx", "gy"), None),
            P(("gx", "gy"), None),
            P("gy"),
            P("gy"),
            P("gx", "gy"),
            P("gy"),
            P("gx", "gy"),
            P("gx", "gy"),
            P("gy"),
            P("gy", "gx"),
            P("gy"),
            P("gy"),
            P("gy"),
            P("gx", "gy"),
            P("gy"),
            P("gy", "gx"),
            P("gy"),
        ),
        check_vma=False,
    )
```

```python
import functools
import math

import jax
import jax.numpy as jnp
from jax import lax
from jax.experimental import pallas as pl
from jax.experimental.pallas import tpu as pltpu
from jax.sharding import PartitionSpec as P

HD = 72
LENGTH = 1024
LANE = 128
BF = jnp.bfloat16
F32 = jnp.float32
MESH = pl.DeviceIdType.MESH
TP = 4
VMEM_LIMIT = 60 << 20
SCALE = HD ** (-0.5)
CUT = 80
LOG2E = 1.4426950408889634
ROOT = math.sqrt(2.0 / math.pi)


def nn(left, right):
    return jnp.dot(left, right, preferred_element_type=F32)


def nt(left, right):
    return lax.dot_general(left, right, (((1,), (1,)), ((), ())), preferred_element_type=F32)


def tn(left, right):
    return lax.dot_general(left, right, (((0,), (0,)), ((), ())), preferred_element_type=F32)


def center_rows(rows):
    center = rows - jnp.mean(rows, axis=-1, keepdims=True)
    inverse = lax.rsqrt(jnp.mean(center * center, axis=-1, keepdims=True) + 1e-06)
    return center * inverse, inverse


def norm_back(grad, gain, hat, inverse):
    scaled = grad * gain
    mean = jnp.mean(scaled, axis=-1, keepdims=True)
    proj = jnp.mean(scaled * hat, axis=-1, keepdims=True)
    return inverse * (scaled - mean - hat * proj)


def lanes(value, start, width, keep):
    full = value.shape[1]
    moved = value if start == 0 else pltpu.roll(value, full - start, 1)
    part = moved[:, :width]
    return jnp.where(lax.broadcasted_iota(jnp.int32, part.shape, 1) < keep, part, 0.0)


def spread(value, start, full):
    wide = jnp.concatenate([value, jnp.zeros((value.shape[0], full - value.shape[1]), F32)], axis=1)
    return wide if start == 0 else pltpu.roll(wide, start, 1)


class Place:
    def __init__(self):
        gx, gy = lax.axis_index("gx"), lax.axis_index("gy")
        self.gx, self.gy = gx, gy
        self.t, self.r = lax.rem(gy, 4), lax.div(gy, 4)
        y, z = lax.rem(gy, 2), lax.rem(lax.div(gy, 2), 2)
        self.ty = self.t + 1 - 2 * y
        self.tz = self.t + 2 - 4 * z
        self.td = 3 - self.t
        base = 4 * self.r
        self.near_y = (gx, base + self.ty)
        self.near_z = (gx, base + self.tz)
        self.other_r = 1 - self.r
        self.half = (gx, lax.rem(gy + 4, 8))
        self.core_bit, self.x_bit = lax.rem(gx, 2), lax.div(gx, 2)
        self.gx_core = gx + 1 - 2 * self.core_bit
        self.gx_x = lax.rem(gx + 2, 4)
        self.core = (self.gx_core, gy)
        self.chip_x = (self.gx_x, gy)


def greet(peers):
    barrier = pltpu.get_barrier_semaphore()
    for peer in peers:
        pl.semaphore_signal(barrier, inc=1, device_id=peer, device_id_type=MESH)
    pl.semaphore_wait(barrier, len(peers))


class Sends:
    def __init__(self, send_sem, recv_sem):
        self.send_sem, self.recv_sem, self.copies = send_sem, recv_sem, {}

    def start(self, index, source, target, peer):
        copy = pltpu.make_async_remote_copy(
            src_ref=source,
            dst_ref=target,
            send_sem=self.send_sem.at[index],
            recv_sem=self.recv_sem.at[index],
            device_id=peer,
            device_id_type=MESH,
        )
        copy.start()
        self.copies[index] = copy

    def arrived(self, *indices):
        for index in indices:
            self.copies[index].wait_recv()

    def left(self):
        for copy in self.copies.values():
            copy.wait_send()


class Gather:
    def __init__(self, place, source, target, send_sem, recv_sem, cut):
        self.p, self.dst = place, target
        self.sends = Sends(send_sem, recv_sem)
        self.lo, self.hi = pl.ds(0, cut), pl.ds(cut, source.shape[0] - cut)
        self.src = source

    def begin(self):
        p, own = self.p, self.dst.at[self.p.t]
        for index, part, peer in (
            (0, self.lo, p.near_y),
            (2, self.hi, p.near_z),
            (1, self.hi, p.near_y),
            (3, self.lo, p.near_z),
        ):
            self.sends.start(index, self.src.at[part], own.at[part], peer)

    def forward(self):
        p = self.p
        self.sends.arrived(0)
        block = self.dst.at[p.ty].at[self.lo]
        self.sends.start(4, block, block, p.near_z)
        self.sends.arrived(2)
        block = self.dst.at[p.tz].at[self.hi]
        self.sends.start(5, block, block, p.near_y)

    def near(self):
        self.sends.arrived(1, 3)

    def far(self):
        self.sends.arrived(4, 5)

    def end(self):
        self.sends.left()


class Scatter:
    def __init__(self, place, part, from_y, from_z, relay_y, relay_z, send_sem, recv_sem):
        self.p, self.part = place, part
        self.from_y, self.from_z, self.relay_y, self.relay_z = from_y, from_z, relay_y, relay_z
        self.sends = Sends(send_sem, recv_sem)
        cut = relay_y.shape[0]
        self.cut = cut
        self.lo, self.hi = pl.ds(0, cut), pl.ds(cut, relay_z.shape[0])

    def far(self):
        p, block = self.p, self.part.at[self.p.td]
        self.sends.start(0, block.at[self.lo], self.relay_y, p.near_y)
        self.sends.start(1, block.at[self.hi], self.relay_z, p.near_z)

    def near_y(self):
        p = self.p
        self.sends.start(2, self.part.at[p.ty].at[self.lo], self.from_y.at[self.lo], p.near_y)

    def near_z(self):
        p = self.p
        self.sends.start(3, self.part.at[p.tz].at[self.hi], self.from_z.at[self.hi], p.near_z)

    def relay(self):
        p, cut = self.p, self.cut
        self.sends.arrived(0)
        block = self.part.at[p.tz]
        block[:cut] = (block[:cut].astype(F32) + self.relay_y[...].astype(F32)).astype(BF)
        self.sends.start(4, block.at[self.lo], self.from_z.at[self.lo], p.near_z)
        self.sends.arrived(1)
        block = self.part.at[p.ty]
        block[cut:] = (block[cut:].astype(F32) + self.relay_z[...].astype(F32)).astype(BF)
        self.sends.start(5, block.at[self.hi], self.from_y.at[self.hi], p.near_y)

    def total(self):
        self.sends.arrived(2, 3, 4, 5)
        own = self.part[self.p.t].astype(F32)
        return own + self.from_y[...].astype(F32) + self.from_z[...].astype(F32)

    def end(self):
        self.sends.left()


class Spread:
    def __init__(self, place, source, target, send_sem, recv_sem, local_sem, part):
        self.p, self.part = place, part
        self.src, self.dst = source.at[part], target
        self.sends = Sends(send_sem, recv_sem)
        self.local = pltpu.make_async_copy(
            self.src, target.at[place.r, place.gx].at[part], local_sem
        )

    def slot(self, group, column):
        return self.dst.at[group, column].at[self.part]

    def begin(self):
        p = self.p
        slot = self.slot(p.r, p.gx)
        self.sends.start(0, self.src, slot, p.half)
        self.sends.start(1, self.src, slot, p.chip_x)
        self.sends.start(2, self.src, slot, p.core)
        self.local.start()

    def second(self):
        p = self.p
        self.sends.arrived(0)
        slot = self.slot(p.other_r, p.gx)
        self.sends.start(3, slot, slot, p.chip_x)
        self.sends.start(4, slot, slot, p.core)

    def third(self):
        p = self.p
        self.sends.arrived(1)
        slot = self.slot(p.r, p.gx_x)
        self.sends.start(5, slot, slot, p.core)
        self.sends.arrived(3)
        slot = self.slot(p.other_r, p.gx_x)
        self.sends.start(6, slot, slot, p.core)

    def done(self):
        self.sends.arrived(2, 4, 5, 6)
        self.local.wait()

    def end(self):
        self.sends.left()


class Reduce:
    def __init__(self, place, source, own, first, second, third, send_sem, recv_sem):
        self.p, self.src, self.own = place, source, own
        self.b1, self.b2, self.b3 = first, second, third
        self.sends = Sends(send_sem, recv_sem)

    def begin(self):
        p = self.p
        for index, group, side in (
            (0, p.other_r, 1 - p.x_bit),
            (2, p.r, 1 - p.x_bit),
            (1, p.other_r, p.x_bit),
            (3, p.r, p.x_bit),
        ):
            block = self.src.at[group, 2 * side + 1 - p.core_bit]
            self.sends.start(index, block, self.b1.at[group, side], p.core)

    def add(self, index, group, side):
        self.sends.arrived(index)
        block = self.b1.at[group, side]
        block[...] = (block[...].astype(F32) + self.own(group, side).astype(F32)).astype(BF)
        return block

    def second(self):
        p = self.p
        block = self.add(0, p.other_r, 1 - p.x_bit)
        self.sends.start(4, block, self.b2.at[p.other_r], p.chip_x)
        block = self.add(2, p.r, 1 - p.x_bit)
        self.sends.start(5, block, self.b2.at[p.r], p.chip_x)
        self.add(1, p.other_r, p.x_bit)
        self.add(3, p.r, p.x_bit)

    def third(self):
        p = self.p
        self.sends.arrived(4)
        block = self.b2.at[p.other_r]
        block[...] = (
            block[...].astype(F32) + self.b1[p.other_r, p.x_bit].astype(F32)
        ).astype(BF)
        self.sends.start(6, block, self.b3, p.half)

    def total(self):
        p = self.p
        self.sends.arrived(5, 6)
        return (
            self.b2[p.r].astype(F32) + self.b1[p.r, p.x_bit].astype(F32) + self.b3[...].astype(F32)
        )

    def end(self):
        self.sends.left()


def flat(block):
    return block.reshape(block.shape[0] * block.shape[1], block.shape[2])


def attention_kernel(
    x, cot, q_w, k_w, v_w, o_w, u_w, d_w, q_b, v_b, u_b, g1, b1, ob, g2, b2, db,
    o_res, o_n2, o_norm, o_qkv, o_lse, o_mix, o_vec, o_up, o_a, o_f, o_cot,
    a_own, f_own, small, x_all, small_all, a_all, v_t, out_s, part,
    from_y, from_z, relay_y, relay_z,
    x_ss, x_rs, s_ss, s_rs, a_ss, a_rs, f_ss, f_rs, c_ss, c_rs, p_ss, p_rs, l_sem,
):
    p = Place()
    rows, width = x.shape
    feat = a_own.shape[0]
    greet([(p.gx, lax.rem(p.gy + d, 8)) for d in range(1, 8)] + [p.core, p.chip_x])
    gather = Gather(p, x, x_all, x_ss, x_rs, CUT)
    gather.begin()
    stack = jnp.concatenate([w[...].astype(F32) for w in (q_w, k_w, v_w, o_w)], axis=0).T
    a_own[...] = jnp.concatenate(
        [stack, jnp.zeros((feat, a_own.shape[1] - stack.shape[1]), F32)], axis=1
    ).astype(BF)
    parts = (pl.ds(0, feat // 2), pl.ds(feat // 2, feat // 2))
    attn_w = [
        Spread(p, a_own, a_all, a_ss.at[i], a_rs.at[i], l_sem.at[i], parts[i]) for i in range(2)
    ]
    for item in attn_w:
        item.begin()
    per, hid = q_b.shape[0], u_b.shape[0]
    small[...] = jnp.zeros_like(small)
    small[0:1, :per] = q_b[...].astype(F32).reshape(1, per)
    value_row = jnp.concatenate(
        [v_b[...].astype(F32).reshape(1, per), jnp.zeros((1, small.shape[1] - per), F32)], axis=1
    )
    small[0:1] += pltpu.roll(value_row, 2 * per, 1)
    small[1:2, :hid] = u_b[...].astype(F32).reshape(1, hid)
    for index, item in enumerate((g1, b1, ob, g2, b2, db)):
        small[2 + index : 3 + index, :per] = item[...].astype(F32).reshape(1, per)
    small_all[p.gy] = small[...]
    smalls = Sends(s_ss, s_rs)
    for d in range(1, 8):
        smalls.start(d - 1, small, small_all.at[p.gy], (p.gx, lax.rem(p.gy + d, 8)))
    hidp = f_own.shape[1] // 2
    for start, item in ((0, u_w), (hidp, d_w)):
        f_own[:, start + hidp - LANE : start + hidp] = jnp.zeros((feat, LANE), BF)
        f_own[:, start : start + hid] = item[...]
    feed_w = [
        Spread(p, f_own, o_f, f_ss.at[i], f_rs.at[i], l_sem.at[2 + i], parts[i]) for i in range(2)
    ]
    cots = Gather(p, cot, o_cot, c_ss, c_rs, CUT)
    smalls.arrived(*range(7))
    vec = jnp.zeros((8, width), F32)
    wide = -(-per // LANE) * LANE
    for g in range(8):
        vec = vec + spread(small_all[g][:, :wide], per * g, width)
    o_vec[...] = vec
    for group in range(2):
        o_up[group] = jnp.broadcast_to(small_all[p.t + 4 * group, 1:2, :], o_up.shape[1:])
    gain, shift = vec[2:3], vec[3:4]

    def norm(index, block):
        hat, _ = center_rows(block.astype(F32))
        o_norm[index] = (hat * gain + shift).astype(BF)

    norm(p.t, x[...])
    gather.forward()
    attn_w[0].second()
    attn_w[1].second()
    for item in feed_w:
        item.begin()
    gather.near()
    norm(p.ty, x_all[p.ty])
    norm(p.tz, x_all[p.tz])
    gather.far()
    norm(p.td, x_all[p.td])
    for item in attn_w:
        item.third()
    cots.begin()
    for item in attn_w:
        item.done()
    attn_copy = pltpu.make_async_copy(a_all, o_a, l_sem.at[4])
    attn_copy.start()

    def project(index, carry):
        block = o_norm[index]
        for group in range(2):
            bias = small_all[p.t + 4 * group, 0:1, :512]
            packed = nn(block, flat(a_all[group])[:, :512]) + bias
            for piece in range(6):
                o_qkv[piece // 2, 2 * group + piece % 2, pl.ds(index * rows, rows)] = lanes(
                    packed, HD * piece, LANE, HD
                ).astype(BF)
        return carry

    lax.fori_loop(0, 4, project, 0)
    for head in range(4):
        v_t[head] = o_qkv[2, head].astype(F32).T.astype(BF)
    scatter = Scatter(p, part, from_y, from_z, relay_y, relay_z, p_ss, p_rs)

    def attend(index):
        def one(head, carry):
            start = pl.multiple_of(index * rows, rows)
            scores = nt(o_qkv[1, head], o_qkv[0, head, pl.ds(start, rows)])
            top = jnp.max(scores, axis=0, keepdims=True)
            expo = jnp.exp2((scores - top) * (SCALE * LOG2E))
            total = jnp.sum(expo, axis=0, keepdims=True)
            mixed = nn(v_t[head], expo.astype(BF)) / total
            out_s[head] = mixed.T
            o_lse[head, index] = jnp.broadcast_to(
                top * (SCALE * LOG2E) + jnp.log2(total), o_lse.shape[2:]
            )
            return carry

        lax.fori_loop(0, 4, one, 0)
        total = jnp.zeros((rows, width), F32)
        for group in range(2):
            mix = (
                spread(out_s[2 * group], 48, 256) + spread(out_s[2 * group + 1], 48 + HD, 256)
            ).astype(BF)
            o_mix[group, pl.ds(pl.multiple_of(index * rows, rows), rows)] = mix
            total = total + nt(mix, flat(a_all[group])[:, 384:640])
        part[index] = total.astype(BF)

    attend(p.td)
    scatter.far()
    feed_w[0].second()
    attend(p.ty)
    scatter.near_y()
    feed_w[1].second()
    attend(p.tz)
    scatter.near_z()
    scatter.relay()
    cots.forward()
    attend(p.t)
    feed_w[0].third()
    feed_w[1].third()
    summed = scatter.total()
    residual = x[...].astype(F32) + summed + vec[4:5]
    o_res[...] = residual
    hat, _ = center_rows(residual.astype(BF).astype(F32))
    o_n2[...] = (hat * vec[5:6] + vec[6:7]).astype(BF)
    cots.near()
    cots.far()
    for item in feed_w:
        item.done()
    attn_copy.wait()
    smalls.left()
    for item in (gather, *attn_w, *feed_w, cots, scatter):
        item.end()


def feed_kernel(
    n2, res, vec, up_bias, cot, c_all_hbm, f_hbm,
    part_m, o_dres, o_e, o_gf, o_sums, o_cols,
    n_all, c_all, f_all, act_s, dup_s, part_d,
    d_y, d_z, d_ry, d_rz,
    n_ss, n_rs, d_ss, d_rs, l_sem,
):
    p = Place()
    rows, width = n2.shape
    hid = f_all.shape[3] // 2
    loads = [
        pltpu.make_async_copy(f_hbm, f_all, l_sem.at[0]),
        pltpu.make_async_copy(c_all_hbm.at[p.ty], c_all.at[p.ty], l_sem.at[1]),
        pltpu.make_async_copy(c_all_hbm.at[p.tz], c_all.at[p.tz], l_sem.at[2]),
        pltpu.make_async_copy(c_all_hbm.at[p.td], c_all.at[p.td], l_sem.at[3]),
    ]
    for load in loads:
        load.start()
    diag = (p.gx, 4 * p.r + p.td)
    greet([p.near_y, p.near_z, diag])
    gather = Gather(p, n2, n_all, n_ss, n_rs, rows // 2)
    gather.begin()
    n_all[p.t] = n2[...]
    c_all[p.t] = cot[...]
    for load in loads:
        load.wait()
    sc_d = Scatter(p, part_d, d_y, d_z, d_ry, d_rz, d_ss, d_rs)
    o_cols[...] = jnp.zeros_like(o_cols)

    def block(index):
        rows_two, rows_c = n_all[index], c_all[index]
        out_m = jnp.zeros((rows, width), F32)
        out_d = jnp.zeros((rows, width), F32)
        for group in range(2):
            upper = nn(rows_two, flat(f_all[group])[:, :hid]) + up_bias[group, 0:1]
            square = upper * upper
            tanh = jnp.tanh(ROOT * upper * (1.0 + 0.044715 * square))
            active = 0.5 * upper * (1.0 + tanh)
            slope = 0.5 * (1.0 + tanh) + 0.5 * upper * (1.0 - tanh * tanh) * (
                ROOT * (1.0 + 3.0 * 0.044715 * square)
            )
            act = active.astype(BF)
            act_s[group, index] = act
            dup = (nn(rows_c, flat(f_all[group])[:, hid:]) * slope).astype(BF)
            dup_s[group, index] = dup
            o_cols[group : group + 1] += jnp.sum(dup.astype(F32), axis=0, keepdims=True)
            out_m = out_m + nt(act, flat(f_all[group])[:, hid:])
            out_d = out_d + nt(dup, flat(f_all[group])[:, :hid])
        part_m[index] = out_m.astype(BF)
        part_d[index] = out_d.astype(BF)

    block(p.t)
    gather.forward()
    gather.near()
    block(p.ty)
    sc_d.near_y()
    block(p.tz)
    sc_d.near_z()
    gather.far()
    block(p.td)
    sc_d.far()
    for group in range(2):
        grad = tn(flat(n_all[...]), flat(dup_s[group])).astype(BF)
        o_gf[group, :, :, :hid] = grad.reshape(4, width // 4, hid)
        if group == 0:
            sc_d.relay()
    for group in range(2):
        grad = tn(flat(c_all[...]), flat(act_s[group])).astype(BF)
        o_gf[group, :, :, hid:] = grad.reshape(4, width // 4, hid)
    grad = sc_d.total()
    hat, inverse = center_rows(res[...].astype(BF).astype(F32))
    cot_f = cot[...].astype(F32)
    d_res = cot_f + norm_back(grad, vec[5:6], hat, inverse)
    o_dres[...] = d_res
    o_e[...] = d_res.astype(BF)
    o_sums[...] = jnp.zeros_like(o_sums)
    o_sums[2:3] = jnp.sum(d_res, axis=0, keepdims=True)
    o_sums[3:4] = jnp.sum(grad * hat, axis=0, keepdims=True)
    o_sums[4:5] = jnp.sum(grad, axis=0, keepdims=True)
    o_sums[5:6] = jnp.sum(cot_f, axis=0, keepdims=True)
    for item in (gather, sc_d):
        item.end()


def back_kernel(
    e_own, d_res, x, res, vec, sums, cols, lse, norm_hbm, qkv_hbm, mix_hbm, a_hbm, gf_hbm, m_hbm,
    o_out, o_gx, o_ga, o_gf, o_small,
    e_all, norm_all, qkv, mix, a_all, k_t, dm_s, dq_s, dk_s, dv_s, pack_s, part,
    from_y, from_z, relay_y, relay_z, part_m, m_y, m_z, m_ry, m_rz,
    gf_own, f1, f2, f3, ga, a1, a2, a3, sv, rv, cs, rcs, rt,
    e_ss, e_rs, p_ss, p_rs, m_ss, m_rs, f_ss, f_rs, a_ss, a_rs, v_ss, v_rs, t_ss, t_rs, l_sem,
):
    p = Place()
    rows, width = e_own.shape
    loads = [
        pltpu.make_async_copy(qkv_hbm, qkv, l_sem.at[0]),
        pltpu.make_async_copy(a_hbm, a_all, l_sem.at[1]),
        pltpu.make_async_copy(mix_hbm, mix, l_sem.at[2]),
        pltpu.make_async_copy(norm_hbm, norm_all, l_sem.at[3]),
        pltpu.make_async_copy(m_hbm, part_m, l_sem.at[8]),
    ]
    for group in range(2):
        for side in range(2):
            loads.append(
                pltpu.make_async_copy(
                    gf_hbm.at[group, 2 * side + p.core_bit],
                    gf_own.at[group, side],
                    l_sem.at[4 + 2 * group + side],
                )
            )
    for load in loads:
        load.start()
    greet(
        [(p.gx, lax.rem(p.gy + d, 8)) for d in range(1, 8)]
        + [(lax.rem(p.gx + d, 4), p.gy) for d in range(1, 4)]
    )
    gather = Gather(p, e_own, e_all, e_ss, e_rs, CUT)
    gather.begin()
    feed_g = Reduce(p, gf_hbm, lambda g, s: gf_own[g, s], f1, f2, f3, f_ss, f_rs)
    feed_g.begin()
    e_all[p.t] = e_own[...]
    for load in loads:
        load.wait()
    for head in range(4):
        k_t[head] = qkv[1, head].astype(F32).T.astype(BF)
    dk_s[...] = jnp.zeros_like(dk_s)
    dv_s[...] = jnp.zeros_like(dv_s)

    def attend_back(index):
        block = e_all[index]
        for group in range(2):
            mixed = nn(block, flat(a_all[group])[:, 384:640])
            dm_s[2 * group] = lanes(mixed, 48, LANE, HD).astype(BF)
            dm_s[2 * group + 1] = lanes(mixed, 48 + HD, LANE, HD).astype(BF)

        def one(head, carry):
            start = pl.multiple_of(index * rows, rows)
            q_rows, d_mix = qkv[0, head, pl.ds(start, rows)], dm_s[head]
            scores = nt(qkv[1, head], q_rows)
            probs = jnp.exp2(scores * (SCALE * LOG2E) - lse[head, index, 0:1])
            d_probs = nt(qkv[2, head], d_mix)
            delta = jnp.sum(d_probs * probs, axis=0, keepdims=True)
            d_scores = (probs * (d_probs - delta)).astype(BF)
            dv_s[head] += nn(probs.astype(BF), d_mix)
            dk_s[head] += nn(d_scores, q_rows)
            dq_s[head, pl.ds(start, rows)] = nn(k_t[head], d_scores).T * SCALE
            return carry

        lax.fori_loop(0, 4, one, 0)

    sc_m = Scatter(p, part_m, m_y, m_z, m_ry, m_rz, m_ss, m_rs)
    attend_back(p.t)
    gather.forward()
    feed_g.second()
    gather.near()
    attend_back(p.ty)
    sc_m.far()
    attend_back(p.tz)
    feed_g.third()
    sc_m.near_y()
    sc_m.near_z()
    gather.far()
    attend_back(p.td)
    scatter = Scatter(p, part, from_y, from_z, relay_y, relay_z, p_ss, p_rs)
    cs[...] = jnp.zeros_like(cs)

    def give(index):
        here = pl.ds(pl.multiple_of(index * rows, rows), rows)
        total = jnp.zeros((rows, width), F32)
        for group in range(2):
            packed = jnp.zeros((rows, 512), F32)
            for piece in range(6):
                head = 2 * group + piece % 2
                if piece < 2:
                    value = dq_s[head, here]
                elif piece < 4:
                    value = dk_s[head, here] * SCALE
                else:
                    value = dv_s[head, here]
                packed = packed + spread(value, HD * piece, 512)
            packed = packed.astype(BF)
            pack_s[group, here] = packed
            cs[group, 0:1, :512] += jnp.sum(packed.astype(F32), axis=0, keepdims=True)
            total = total + nt(packed, flat(a_all[group])[:, :512])
        part[index] = total.astype(BF)

    give(p.td)
    scatter.far()
    give(p.ty)
    scatter.near_y()
    give(p.tz)
    scatter.near_z()
    give(p.t)
    sc_m.relay()
    for group in range(2):
        main = tn(flat(norm_all[...]), pack_s[group])
        outer = tn(flat(e_all[...]), mix[group])
        both = jnp.concatenate(
            [main[:, :384], main[:, 384:] + outer[:, :128], outer[:, 128:]], axis=1
        )
        ga[group] = both.astype(BF).reshape(4, width // 4, 640)
        if group == 0:
            scatter.relay()
    attn_g = Reduce(
        p, ga, lambda g, s: ga[g, 2 * s + p.core_bit], a1, a2, a3, a_ss, a_rs
    )
    attn_g.begin()
    attn_g.second()
    o_out[...] = (res[...] + sc_m.total() + vec[7:8]).astype(BF)
    grad = scatter.total()
    hat, inverse = center_rows(x[...].astype(F32))
    o_gx[...] = (d_res[...] + norm_back(grad, vec[2:3], hat, inverse)).astype(BF)
    row = lax.broadcasted_iota(jnp.int32, sums.shape, 0)
    all_sums = sums[...]
    all_sums = jnp.where(row == 0, jnp.sum(grad * hat, axis=0, keepdims=True), all_sums)
    all_sums = jnp.where(row == 1, jnp.sum(grad, axis=0, keepdims=True), all_sums)
    per = width // 8
    for g in range(8):
        sv[g] = lanes(all_sums, per * g, sv.shape[2], per)
    for group in range(2):
        cs[group, 1:2] = cols[group : group + 1]
    small = Sends(v_ss, v_rs)
    for d in range(1, 8):
        other = lax.rem(p.gy + d, 8)
        small.start(d - 1, sv.at[other], rv.at[p.gy], (p.gx, other))
    small.start(7, cs.at[p.other_r], rcs, p.half)
    rv[p.gy] = sv[p.gy]
    attn_g.third()
    small.arrived(*range(8))
    total = rv[0]
    for g in range(1, 8):
        total = total + rv[g]
    mine = rt.at[p.gx]
    mine[0:8] = jnp.concatenate(
        [total, jnp.zeros((8, rt.shape[2] - total.shape[1]), F32)], axis=1
    )
    mine[8:16] = cs[p.r] + rcs[...]
    wide = Sends(t_ss, t_rs)
    for d in range(1, 4):
        wide.start(d - 1, mine, mine, (lax.rem(p.gx + d, 4), p.gy))
    o_gf[...] = feed_g.total()
    wide.arrived(0, 1, 2)
    o_small[...] = rt[0] + rt[1] + rt[2] + rt[3]
    o_ga[...] = attn_g.total()
    small.left()
    wide.left()
    for item in (gather, feed_g, attn_g, scatter, sc_m):
        item.end()


VM = pl.BlockSpec(memory_space=pltpu.VMEM)
ANY = pl.BlockSpec(memory_space=pl.ANY)


def dma(shape):
    return pltpu.SemaphoreType.DMA(shape)


def finish_kernel(
    out, gx, ga, gf, small,
    o_out, o_gx, o_g1, o_b1, o_q, o_qb, o_k, o_v, o_vb, o_o, o_ob, o_g2, o_b2, o_u, o_ub, o_d, o_db,
):
    per, hid = o_g1.shape[0], o_ub.shape[0]
    hidp = gf.shape[1] // 2
    o_out[...] = out[...]
    o_gx[...] = gx[...]
    stack = ga[...].T
    for index, item in enumerate((o_q, o_k, o_v, o_o)):
        item[...] = stack[per * index : per * (index + 1)]
    o_u[...] = gf[:, :hid]
    o_d[...] = gf[:, hidp : hidp + hid]
    for index, item in enumerate((o_g1, o_b1, o_ob, o_g2, o_b2, o_db)):
        item[...] = small[index : index + 1, :per].reshape(per)
    o_qb[...] = small[8:9, :per].reshape(per)
    o_vb[...] = pltpu.roll(small[8:9], small.shape[1] - 2 * per, 1)[:, :per].reshape(per)
    o_ub[...] = small[9:10, :hid].reshape(hid)


def fast_shards(
    layer_input, norm_one_gain, norm_one_bias, query_weight, query_bias, key_weight, value_weight,
    value_bias, output_weight, output_bias, norm_two_gain, norm_two_bias, up_weight, up_bias,
    down_weight, down_bias, cotangent,
):
    rows, width = layer_input.shape
    per, hid = query_weight.shape[1], up_weight.shape[1]
    feat = query_weight.shape[0]
    hidp = -(-hid // LANE) * LANE
    aw = 640
    shape, bf, f32 = jax.ShapeDtypeStruct, BF, F32
    params = lambda number: pltpu.CompilerParams(
        collective_id=number, has_side_effects=True, vmem_limit_bytes=VMEM_LIMIT
    )
    full = (rows, width)
    block4 = pltpu.VMEM((4, rows, width), bf)

    def landing(cut):
        return [
            pltpu.VMEM(full, bf), pltpu.VMEM(full, bf),
            pltpu.VMEM((cut, width), bf), pltpu.VMEM((rows - cut, width), bf),
        ]

    (res, n2, normed, qkv, lse, mix, vec, ups, a_all, f_all, c_all) = pl.pallas_call(
        attention_kernel,
        name="attention",
        out_shape=[
            shape(full, f32), shape(full, bf), shape((4, rows, width), bf),
            shape((3, 4, 4 * rows, LANE), bf), shape((4, 4, 8, rows), f32),
            shape((2, 4 * rows, 256), bf), shape((8, width), f32), shape((2, 8, aw), f32),
            shape((2, 4, feat, aw), bf), shape((2, 4, feat, 2 * hidp), bf), shape((4, rows, width), bf),
        ],
        in_specs=[VM] * 17,
        out_specs=[VM] * 8 + [ANY] * 3,
        scratch_shapes=[
            pltpu.VMEM((feat, aw), bf), pltpu.VMEM((feat, 2 * hidp), bf), pltpu.VMEM((8, aw), f32),
            block4, pltpu.VMEM((8, 8, aw), f32),
            pltpu.VMEM((2, 4, feat, aw), bf), pltpu.VMEM((4, LANE, 4 * rows), bf),
            pltpu.VMEM((4, rows, LANE), f32), block4, *landing(rows - CUT),
            dma((6,)), dma((6,)), dma((7,)), dma((7,)), dma((2, 7)), dma((2, 7)), dma((2, 7)),
            dma((2, 7)), dma((6,)), dma((6,)), dma((6,)), dma((6,)), dma((5,)),
        ],
        compiler_params=params(0),
    )(
        layer_input, cotangent, query_weight.T, key_weight.T, value_weight.T, output_weight,
        up_weight, down_weight.T, query_bias, value_bias, up_bias, norm_one_gain, norm_one_bias,
        output_bias, norm_two_gain, norm_two_bias, down_bias,
    )
    (part_m, d_res, e, gf, sums, cols) = pl.pallas_call(
        feed_kernel,
        name="feed_forward",
        out_shape=[
            shape((4, rows, width), bf), shape(full, f32), shape(full, bf),
            shape((2, 4, feat, 2 * hidp), bf), shape((8, width), f32), shape((8, hidp), f32),
        ],
        in_specs=[VM] * 5 + [ANY] * 2,
        out_specs=[VM] * 6,
        scratch_shapes=[
            block4, block4,
            pltpu.VMEM((2, 4, feat, 2 * hidp), bf), pltpu.VMEM((2, 4, rows, hidp), bf),
            pltpu.VMEM((2, 4, rows, hidp), bf), block4, *landing(rows // 2),
            dma((6,)), dma((6,)), dma((6,)), dma((6,)), dma((4,)),
        ],
        compiler_params=params(1),
    )(n2, res, vec, ups, cotangent, c_all, f_all)
    wide = -(-per // LANE) * LANE
    (out, grad_input, ga, gfo, smalls) = pl.pallas_call(
        back_kernel,
        name="attention_back",
        out_shape=[
            shape(full, bf), shape(full, bf), shape((feat, aw), f32), shape((feat, 2 * hidp), f32),
            shape((16, aw), f32),
        ],
        in_specs=[VM] * 8 + [ANY] * 6,
        out_specs=[VM] * 5,
        scratch_shapes=[
            block4, block4,
            pltpu.VMEM((3, 4, 4 * rows, LANE), bf), pltpu.VMEM((2, 4 * rows, 256), bf),
            pltpu.VMEM((2, 4, feat, aw), bf), pltpu.VMEM((4, LANE, 4 * rows), bf),
            pltpu.VMEM((4, rows, LANE), bf), pltpu.VMEM((4, 4 * rows, LANE), f32),
            pltpu.VMEM((4, 4 * rows, LANE), f32), pltpu.VMEM((4, 4 * rows, LANE), f32),
            pltpu.VMEM((2, 4 * rows, 512), bf), block4, *landing(rows - CUT),
            block4, *landing(rows - CUT),
            pltpu.VMEM((2, 2, feat, 2 * hidp), bf), pltpu.VMEM((2, 2, feat, 2 * hidp), bf),
            pltpu.VMEM((2, feat, 2 * hidp), bf), pltpu.VMEM((feat, 2 * hidp), bf),
            pltpu.VMEM((2, 4, feat, aw), bf), pltpu.VMEM((2, 2, feat, aw), bf),
            pltpu.VMEM((2, feat, aw), bf), pltpu.VMEM((feat, aw), bf),
            pltpu.VMEM((8, 8, wide), f32), pltpu.VMEM((8, 8, wide), f32),
            pltpu.VMEM((2, 8, aw), f32), pltpu.VMEM((8, aw), f32), pltpu.VMEM((4, 16, aw), f32),
            dma((6,)), dma((6,)), dma((6,)), dma((6,)), dma((6,)), dma((6,)), dma((7,)), dma((7,)),
            dma((7,)), dma((7,)), dma((8,)), dma((8,)), dma((3,)), dma((3,)), dma((9,)),
        ],
        compiler_params=params(2),
    )(e, d_res, layer_input, res, vec, sums, cols, lse, normed, qkv, mix, a_all, gf, part_m)
    line = shape((per,), f32)
    turned = shape((per, feat), f32)
    done = pl.pallas_call(
        finish_kernel,
        name="finish",
        out_shape=[
            shape(full, bf), shape(full, bf), line, line, turned, line, turned, turned, line,
            turned, line, line, line, shape((feat, hid), f32), shape((hid,), f32),
            shape((feat, hid), f32), line,
        ],
        in_specs=[VM] * 5,
        out_specs=[VM] * 17,
        compiler_params=pltpu.CompilerParams(vmem_limit_bytes=VMEM_LIMIT),
    )(out, grad_input, ga, gfo, smalls)
    done = list(done)
    for index in (4, 6, 7, 15):
        done[index] = done[index].T
    return tuple(done)


def dot_plain(left, right):
    return jnp.dot(left, right, preferred_element_type=jnp.float32)


def dot_right_t(left, right):
    return lax.dot_general(
        left, right, (((1,), (1,)), ((), ())), preferred_element_type=jnp.float32
    )


def dot_left_t(left, right):
    return lax.dot_general(
        left, right, (((0,), (0,)), ((), ())), preferred_element_type=jnp.float32
    )


def normalize(rows):
    center = rows - jnp.mean(rows, axis=-1, keepdims=True)
    inverse = lax.rsqrt(jnp.mean(center * center, axis=-1, keepdims=True) + 1e-06)
    return (center * inverse, inverse)


def gelu_tanh(value):
    return jax.nn.gelu(value, approximate=True)


def image_shape(array):
    heads = array.shape[1] // HD
    return (array.shape[0] // LENGTH, LENGTH, heads, HD)


def attend(query, key, value):
    shape = image_shape(query)
    scale = HD ** (-0.5)

    def one_image(carry, pieces):
        q_img, k_img, v_img = pieces
        scores = (
            jnp.einsum("qhd,khd->hqk", q_img, k_img, preferred_element_type=jnp.float32) * scale
        )
        top = jnp.max(scores, axis=-1, keepdims=True)
        expo = jnp.exp(scores - top)
        total = jnp.sum(expo, axis=-1, keepdims=True)
        probs = (expo / total).astype(jnp.bfloat16)
        mixed = jnp.einsum("hqk,khd->qhd", probs, v_img, preferred_element_type=jnp.float32).astype(
            jnp.bfloat16
        )
        return (carry, (mixed, (top + jnp.log(total))[..., 0]))

    _, (mixed, lse) = lax.scan(
        one_image, 0, (query.reshape(shape), key.reshape(shape), value.reshape(shape))
    )
    return (mixed.reshape(query.shape), lse)


def attend_back(query, key, value, lse, d_mixed):
    shape = image_shape(query)
    scale = HD ** (-0.5)

    def one_image(carry, pieces):
        q_img, k_img, v_img, lse_img, dm_img = pieces
        scores = (
            jnp.einsum("qhd,khd->hqk", q_img, k_img, preferred_element_type=jnp.float32) * scale
        )
        probs = jnp.exp(scores - lse_img[..., None])
        d_probs = jnp.einsum("qhd,khd->hqk", dm_img, v_img, preferred_element_type=jnp.float32)
        d_scores = (probs * (d_probs - jnp.sum(d_probs * probs, axis=-1, keepdims=True))).astype(
            jnp.bfloat16
        )
        d_value = jnp.einsum(
            "hqk,qhd->khd", probs.astype(jnp.bfloat16), dm_img, preferred_element_type=jnp.float32
        ).astype(jnp.bfloat16)
        d_query = (
            jnp.einsum("hqk,khd->qhd", d_scores, k_img, preferred_element_type=jnp.float32) * scale
        ).astype(jnp.bfloat16)
        d_key = (
            jnp.einsum("hqk,qhd->khd", d_scores, q_img, preferred_element_type=jnp.float32) * scale
        ).astype(jnp.bfloat16)
        return (carry, (d_query, d_key, d_value))

    _, (d_query, d_key, d_value) = lax.scan(
        one_image,
        0,
        (
            query.reshape(shape),
            key.reshape(shape),
            value.reshape(shape),
            lse,
            d_mixed.reshape(shape),
        ),
    )
    return (d_query.reshape(query.shape), d_key.reshape(query.shape), d_value.reshape(query.shape))


def forward_pass(
    layer_input,
    norm_one_gain,
    norm_one_bias,
    query_weight,
    query_bias,
    key_weight,
    value_weight,
    value_bias,
    output_weight,
    output_bias,
    norm_two_gain,
    norm_two_bias,
    up_weight,
    up_bias,
    down_weight,
    down_bias,
):
    w_query, w_key, w_value, w_output, w_up, w_down = (
        lax.all_gather(query_weight, "gx", axis=0, tiled=True),
        lax.all_gather(key_weight, "gx", axis=0, tiled=True),
        lax.all_gather(value_weight, "gx", axis=0, tiled=True),
        lax.all_gather(output_weight, "gx", axis=1, tiled=True),
        lax.all_gather(up_weight, "gx", axis=0, tiled=True),
        lax.all_gather(down_weight, "gx", axis=1, tiled=True),
    )
    rows_one, gain_one, shift_one, out_shift, down_shift = (
        lax.all_gather(layer_input, "gy", axis=0, tiled=True),
        lax.all_gather(norm_one_gain, "gy", axis=0, tiled=True),
        lax.all_gather(norm_one_bias, "gy", axis=0, tiled=True),
        lax.all_gather(output_bias, "gy", axis=0, tiled=True),
        lax.all_gather(down_bias, "gy", axis=0, tiled=True),
    )
    hat_one, inv_one = normalize(rows_one.astype(jnp.float32))
    normed = (hat_one * gain_one.astype(jnp.float32) + shift_one.astype(jnp.float32)).astype(
        jnp.bfloat16
    )
    query = (dot_plain(normed, w_query) + query_bias.astype(jnp.float32)).astype(jnp.bfloat16)
    key = dot_plain(normed, w_key).astype(jnp.bfloat16)
    value = (dot_plain(normed, w_value) + value_bias.astype(jnp.float32)).astype(jnp.bfloat16)
    mixed, lse = attend(query, key, value)
    attn_part = lax.psum_scatter(
        dot_plain(mixed, w_output).astype(jnp.bfloat16), "gy", scatter_dimension=0, tiled=True
    ).astype(jnp.float32)
    residual = layer_input.astype(jnp.float32) + attn_part + out_shift.astype(jnp.float32)
    rows_two, gain_two, shift_two = (
        lax.all_gather(residual.astype(jnp.bfloat16), "gy", axis=0, tiled=True),
        lax.all_gather(norm_two_gain, "gy", axis=0, tiled=True),
        lax.all_gather(norm_two_bias, "gy", axis=0, tiled=True),
    )
    hat_two, inv_two = normalize(rows_two.astype(jnp.float32))
    normed_two = (hat_two * gain_two.astype(jnp.float32) + shift_two.astype(jnp.float32)).astype(
        jnp.bfloat16
    )
    upper = dot_plain(normed_two, w_up) + up_bias.astype(jnp.float32)
    active = gelu_tanh(upper).astype(jnp.bfloat16)
    mlp_part = lax.psum_scatter(
        dot_plain(active, w_down).astype(jnp.bfloat16), "gy", scatter_dimension=0, tiled=True
    ).astype(jnp.float32)
    result = (residual + mlp_part + down_shift.astype(jnp.float32)).astype(jnp.bfloat16)
    saved = (
        w_query,
        w_key,
        w_value,
        w_output,
        w_up,
        w_down,
        hat_one,
        inv_one,
        normed,
        query,
        key,
        value,
        mixed,
        lse,
        hat_two,
        inv_two,
        normed_two,
        upper,
        active,
        gain_one,
        gain_two,
    )
    return saved, result


def shards(
    layer_input,
    norm_one_gain,
    norm_one_bias,
    query_weight,
    query_bias,
    key_weight,
    value_weight,
    value_bias,
    output_weight,
    output_bias,
    norm_two_gain,
    norm_two_bias,
    up_weight,
    up_bias,
    down_weight,
    down_bias,
    cotangent,
):
    inputs = (
        layer_input,
        norm_one_gain,
        norm_one_bias,
        query_weight,
        query_bias,
        key_weight,
        value_weight,
        value_bias,
        output_weight,
        output_bias,
        norm_two_gain,
        norm_two_bias,
        up_weight,
        up_bias,
        down_weight,
        down_bias,
    )
    saved, layer_output = forward_pass(*inputs)
    (
        w_query,
        w_key,
        w_value,
        w_output,
        w_up,
        w_down,
        hat_one,
        inv_one,
        normed,
        query,
        key,
        value,
        mixed,
        lse,
        hat_two,
        inv_two,
        normed_two,
        upper,
        active,
        gain_one,
        gain_two,
    ) = saved
    local = layer_input.shape[0]
    start = lax.axis_index("gy") * local
    grad_rows = lax.all_gather(cotangent, "gy", axis=0, tiled=True)
    d_active = dot_right_t(grad_rows, w_down)
    _, gelu_pull = jax.vjp(gelu_tanh, upper)
    d_upper = gelu_pull(d_active)[0].astype(jnp.bfloat16)
    grad_up_weight, grad_down_weight = (
        lax.psum_scatter(
            dot_left_t(normed_two, d_upper).astype(jnp.bfloat16),
            "gx",
            scatter_dimension=0,
            tiled=True,
        ).astype(jnp.float32),
        lax.psum_scatter(
            dot_left_t(active, grad_rows).astype(jnp.bfloat16),
            "gx",
            scatter_dimension=1,
            tiled=True,
        ).astype(jnp.float32),
    )
    d_normed_two = lax.psum_scatter(
        dot_right_t(d_upper, w_up).astype(jnp.bfloat16), "gy", scatter_dimension=0, tiled=True
    ).astype(jnp.float32)
    hat_two_local = lax.dynamic_slice_in_dim(hat_two, start, local, 0)
    inv_two_local = lax.dynamic_slice_in_dim(inv_two, start, local, 0)
    scaled_two = d_normed_two * gain_two.astype(jnp.float32)
    mean_two = jnp.mean(scaled_two, axis=-1, keepdims=True)
    proj_two = jnp.mean(scaled_two * hat_two_local, axis=-1, keepdims=True)
    cot_float = cotangent.astype(jnp.float32)
    d_residual = cot_float + inv_two_local * (scaled_two - mean_two - hat_two_local * proj_two)
    part_two_gain = jnp.sum(d_normed_two * hat_two_local, axis=0)
    part_two_bias = jnp.sum(d_normed_two, axis=0)
    part_up_bias = jnp.sum(d_upper.astype(jnp.float32), axis=0)
    part_down_bias = jnp.sum(cot_float, axis=0)
    grad_attn = lax.all_gather(d_residual.astype(jnp.bfloat16), "gy", axis=0, tiled=True)
    part_output_bias = jnp.sum(d_residual, axis=0)
    d_mixed = dot_right_t(grad_attn, w_output).astype(jnp.bfloat16)
    d_query, d_key, d_value = attend_back(query, key, value, lse, d_mixed)
    grad_query_weight, grad_key_weight, grad_value_weight, grad_output_weight = (
        lax.psum_scatter(
            dot_left_t(normed, d_query).astype(jnp.bfloat16), "gx", scatter_dimension=0, tiled=True
        ).astype(jnp.float32),
        lax.psum_scatter(
            dot_left_t(normed, d_key).astype(jnp.bfloat16), "gx", scatter_dimension=0, tiled=True
        ).astype(jnp.float32),
        lax.psum_scatter(
            dot_left_t(normed, d_value).astype(jnp.bfloat16), "gx", scatter_dimension=0, tiled=True
        ).astype(jnp.float32),
        lax.psum_scatter(
            dot_left_t(mixed, grad_attn).astype(jnp.bfloat16), "gx", scatter_dimension=1, tiled=True
        ).astype(jnp.float32),
    )
    d_normed = lax.psum_scatter(
        (
            dot_right_t(d_query, w_query)
            + dot_right_t(d_key, w_key)
            + dot_right_t(d_value, w_value)
        ).astype(jnp.bfloat16),
        "gy",
        scatter_dimension=0,
        tiled=True,
    ).astype(jnp.float32)
    hat_one_local = lax.dynamic_slice_in_dim(hat_one, start, local, 0)
    inv_one_local = lax.dynamic_slice_in_dim(inv_one, start, local, 0)
    scaled_one = d_normed * gain_one.astype(jnp.float32)
    mean_one = jnp.mean(scaled_one, axis=-1, keepdims=True)
    proj_one = jnp.mean(scaled_one * hat_one_local, axis=-1, keepdims=True)
    grad_input = (
        d_residual + inv_one_local * (scaled_one - mean_one - hat_one_local * proj_one)
    ).astype(jnp.bfloat16)
    part_one_gain = jnp.sum(d_normed * hat_one_local, axis=0)
    part_one_bias = jnp.sum(d_normed, axis=0)
    part_query_bias = jnp.sum(d_query.astype(jnp.float32), axis=0)
    part_value_bias = jnp.sum(d_value.astype(jnp.float32), axis=0)
    feat_one_gain, feat_one_bias, feat_output_bias, feat_two_gain, feat_two_bias, feat_down_bias = (
        lax.psum_scatter(part_one_gain, "gy", scatter_dimension=0, tiled=True),
        lax.psum_scatter(part_one_bias, "gy", scatter_dimension=0, tiled=True),
        lax.psum_scatter(part_output_bias, "gy", scatter_dimension=0, tiled=True),
        lax.psum_scatter(part_two_gain, "gy", scatter_dimension=0, tiled=True),
        lax.psum_scatter(part_two_bias, "gy", scatter_dimension=0, tiled=True),
        lax.psum_scatter(part_down_bias, "gy", scatter_dimension=0, tiled=True),
    )
    (
        grad_one_gain,
        grad_one_bias,
        grad_query_bias,
        grad_value_bias,
        grad_output_bias,
        grad_two_gain,
        grad_two_bias,
        grad_up_bias,
        grad_down_bias,
    ) = lax.psum(
        (
            feat_one_gain,
            feat_one_bias,
            part_query_bias,
            part_value_bias,
            feat_output_bias,
            feat_two_gain,
            feat_two_bias,
            part_up_bias,
            feat_down_bias,
        ),
        "gx",
    )
    return (
        layer_output,
        grad_input,
        grad_one_gain,
        grad_one_bias,
        grad_query_weight,
        grad_query_bias,
        grad_key_weight,
        grad_value_weight,
        grad_value_bias,
        grad_output_weight,
        grad_output_bias,
        grad_two_gain,
        grad_two_bias,
        grad_up_weight,
        grad_up_bias,
        grad_down_weight,
        grad_down_bias,
    )


def solution(mesh):
    fits = mesh.shape["gx"] == 4 and mesh.shape["gy"] == 8
    return jax.shard_map(
        fast_shards if fits else shards,
        mesh=mesh,
        in_specs=(
            P(("gx", "gy"), None),
            P("gy"),
            P("gy"),
            P("gx", "gy"),
            P("gy"),
            P("gx", "gy"),
            P("gx", "gy"),
            P("gy"),
            P("gy", "gx"),
            P("gy"),
            P("gy"),
            P("gy"),
            P("gx", "gy"),
            P("gy"),
            P("gy", "gx"),
            P("gy"),
            P(("gx", "gy"), None),
        ),
        out_specs=(
            P(("gx", "gy"), None),
            P(("gx", "gy"), None),
            P("gy"),
            P("gy"),
            P("gx", "gy"),
            P("gy"),
            P("gx", "gy"),
            P("gx", "gy"),
            P("gy"),
            P("gy", "gx"),
            P("gy"),
            P("gy"),
            P("gy"),
            P("gx", "gy"),
            P("gy"),
            P("gy", "gx"),
            P("gy"),
        ),
        check_vma=False,
    )
```

```python
import functools
import math

import jax
import jax.numpy as jnp
from jax import lax
from jax.experimental import pallas as pl
from jax.experimental.pallas import tpu as pltpu
from jax.sharding import PartitionSpec as P

HD = 72
LENGTH = 1024
LANE = 128
BF = jnp.bfloat16
F32 = jnp.float32
MESH = pl.DeviceIdType.MESH
TP = 4
VMEM_LIMIT = 63 << 20
SCALE = HD ** (-0.5)
CUT = 80
LOG2E = 1.4426950408889634
ROOT = math.sqrt(2.0 / math.pi)


def nn(left, right):
    return jnp.dot(left, right, preferred_element_type=F32)


def nt(left, right):
    return lax.dot_general(left, right, (((1,), (1,)), ((), ())), preferred_element_type=F32)


def tn(left, right):
    return lax.dot_general(left, right, (((0,), (0,)), ((), ())), preferred_element_type=F32)


def center_rows(rows):
    center = rows - jnp.mean(rows, axis=-1, keepdims=True)
    inverse = lax.rsqrt(jnp.mean(center * center, axis=-1, keepdims=True) + 1e-06)
    return center * inverse, inverse


def norm_back(grad, gain, hat, inverse):
    scaled = grad * gain
    mean = jnp.mean(scaled, axis=-1, keepdims=True)
    proj = jnp.mean(scaled * hat, axis=-1, keepdims=True)
    return inverse * (scaled - mean - hat * proj)


def lanes(value, start, width, keep):
    full = value.shape[1]
    moved = value if start == 0 else pltpu.roll(value, full - start, 1)
    part = moved[:, :width]
    return jnp.where(lax.broadcasted_iota(jnp.int32, part.shape, 1) < keep, part, 0.0)


def spread(value, start, full):
    wide = jnp.concatenate([value, jnp.zeros((value.shape[0], full - value.shape[1]), F32)], axis=1)
    return wide if start == 0 else pltpu.roll(wide, start, 1)


class Place:
    def __init__(self):
        gx, gy = lax.axis_index("gx"), lax.axis_index("gy")
        self.gx, self.gy = gx, gy
        self.t, self.r = lax.rem(gy, 4), lax.div(gy, 4)
        y, z = lax.rem(gy, 2), lax.rem(lax.div(gy, 2), 2)
        self.ty = self.t + 1 - 2 * y
        self.tz = self.t + 2 - 4 * z
        self.td = 3 - self.t
        base = 4 * self.r
        self.near_y = (gx, base + self.ty)
        self.near_z = (gx, base + self.tz)
        self.other_r = 1 - self.r
        self.half = (gx, lax.rem(gy + 4, 8))
        self.core_bit, self.x_bit = lax.rem(gx, 2), lax.div(gx, 2)
        self.gx_core = gx + 1 - 2 * self.core_bit
        self.gx_x = lax.rem(gx + 2, 4)
        self.core = (self.gx_core, gy)
        self.chip_x = (self.gx_x, gy)


def greet(peers):
    barrier = pltpu.get_barrier_semaphore()
    for peer in peers:
        pl.semaphore_signal(barrier, inc=1, device_id=peer, device_id_type=MESH)
    pl.semaphore_wait(barrier, len(peers))


class Sends:
    def __init__(self, send_sem, recv_sem):
        self.send_sem, self.recv_sem, self.copies = send_sem, recv_sem, {}

    def start(self, index, source, target, peer):
        copy = pltpu.make_async_remote_copy(
            src_ref=source,
            dst_ref=target,
            send_sem=self.send_sem.at[index],
            recv_sem=self.recv_sem.at[index],
            device_id=peer,
            device_id_type=MESH,
        )
        copy.start()
        self.copies[index] = copy

    def arrived(self, *indices):
        for index in indices:
            self.copies[index].wait_recv()

    def left(self):
        for copy in self.copies.values():
            copy.wait_send()


class Gather:
    def __init__(self, place, source, target, send_sem, recv_sem, cut):
        self.p, self.dst = place, target
        self.sends = Sends(send_sem, recv_sem)
        self.lo, self.hi = pl.ds(0, cut), pl.ds(cut, source.shape[0] - cut)
        self.src = source

    def begin(self):
        p, own = self.p, self.dst.at[self.p.t]
        for index, part, peer in (
            (0, self.lo, p.near_y),
            (2, self.hi, p.near_z),
            (1, self.hi, p.near_y),
            (3, self.lo, p.near_z),
        ):
            self.sends.start(index, self.src.at[part], own.at[part], peer)

    def forward(self):
        p = self.p
        self.sends.arrived(0)
        block = self.dst.at[p.ty].at[self.lo]
        self.sends.start(4, block, block, p.near_z)
        self.sends.arrived(2)
        block = self.dst.at[p.tz].at[self.hi]
        self.sends.start(5, block, block, p.near_y)

    def near(self):
        self.sends.arrived(1, 3)

    def far(self):
        self.sends.arrived(4, 5)

    def end(self):
        self.sends.left()


class Scatter:
    def __init__(self, place, part, from_y, from_z, relay_y, relay_z, send_sem, recv_sem):
        self.p, self.part = place, part
        self.from_y, self.from_z, self.relay_y, self.relay_z = from_y, from_z, relay_y, relay_z
        self.sends = Sends(send_sem, recv_sem)
        cut = relay_y.shape[0]
        self.cut = cut
        self.lo, self.hi = pl.ds(0, cut), pl.ds(cut, relay_z.shape[0])

    def far(self):
        p, block = self.p, self.part.at[self.p.td]
        self.sends.start(0, block.at[self.lo], self.relay_y, p.near_y)
        self.sends.start(1, block.at[self.hi], self.relay_z, p.near_z)

    def near_y(self):
        p = self.p
        self.sends.start(2, self.part.at[p.ty].at[self.lo], self.from_y.at[self.lo], p.near_y)

    def near_z(self):
        p = self.p
        self.sends.start(3, self.part.at[p.tz].at[self.hi], self.from_z.at[self.hi], p.near_z)

    def relay(self):
        p, cut = self.p, self.cut
        self.sends.arrived(0)
        block = self.part.at[p.tz]
        block[:cut] = (block[:cut].astype(F32) + self.relay_y[...].astype(F32)).astype(BF)
        self.sends.start(4, block.at[self.lo], self.from_z.at[self.lo], p.near_z)
        self.sends.arrived(1)
        block = self.part.at[p.ty]
        block[cut:] = (block[cut:].astype(F32) + self.relay_z[...].astype(F32)).astype(BF)
        self.sends.start(5, block.at[self.hi], self.from_y.at[self.hi], p.near_y)

    def total(self):
        self.sends.arrived(2, 3, 4, 5)
        own = self.part[self.p.t].astype(F32)
        return own + self.from_y[...].astype(F32) + self.from_z[...].astype(F32)

    def end(self):
        self.sends.left()


class Spread:
    def __init__(self, place, source, target, send_sem, recv_sem, local_sem, part):
        self.p, self.part = place, part
        self.src, self.dst = source.at[part], target
        self.sends = Sends(send_sem, recv_sem)
        self.local = pltpu.make_async_copy(
            self.src, target.at[place.r, place.gx].at[part], local_sem
        )

    def slot(self, group, column):
        return self.dst.at[group, column].at[self.part]

    def begin(self):
        p = self.p
        slot = self.slot(p.r, p.gx)
        self.sends.start(0, self.src, slot, p.half)
        self.sends.start(1, self.src, slot, p.chip_x)
        self.sends.start(2, self.src, slot, p.core)
        self.local.start()

    def second(self):
        p = self.p
        self.sends.arrived(0)
        slot = self.slot(p.other_r, p.gx)
        self.sends.start(3, slot, slot, p.chip_x)
        self.sends.start(4, slot, slot, p.core)

    def third(self):
        p = self.p
        self.sends.arrived(1)
        slot = self.slot(p.r, p.gx_x)
        self.sends.start(5, slot, slot, p.core)
        self.sends.arrived(3)
        slot = self.slot(p.other_r, p.gx_x)
        self.sends.start(6, slot, slot, p.core)

    def done(self):
        self.sends.arrived(2, 4, 5, 6)
        self.local.wait()

    def end(self):
        self.sends.left()


class Reduce:
    def __init__(self, place, source, first, second, third, send_sem, recv_sem):
        self.p, self.src = place, source
        self.b1, self.b2, self.b3 = first, second, third
        self.sends = Sends(send_sem, recv_sem)

    def begin(self):
        p = self.p
        for index, group, side in (
            (0, p.other_r, 1 - p.x_bit),
            (2, p.r, 1 - p.x_bit),
            (1, p.other_r, p.x_bit),
            (3, p.r, p.x_bit),
        ):
            block = self.src.at[group, 2 * side + 1 - p.core_bit]
            self.sends.start(index, block, self.b1.at[group, side], p.core)

    def add(self, index, group, side):
        self.sends.arrived(index)
        block = self.b1.at[group, side]
        block[...] = (block[...].astype(F32) + self.src[group, 2 * side + self.p.core_bit].astype(F32)).astype(BF)
        return block

    def second(self):
        p = self.p
        block = self.add(0, p.other_r, 1 - p.x_bit)
        self.sends.start(4, block, self.b2.at[p.other_r], p.chip_x)
        block = self.add(2, p.r, 1 - p.x_bit)
        self.sends.start(5, block, self.b2.at[p.r], p.chip_x)
        self.add(1, p.other_r, p.x_bit)
        self.add(3, p.r, p.x_bit)

    def third(self):
        p = self.p
        self.sends.arrived(4)
        block = self.b2.at[p.other_r]
        block[...] = (
            block[...].astype(F32) + self.b1[p.other_r, p.x_bit].astype(F32)
        ).astype(BF)
        self.sends.start(6, block, self.b3, p.half)

    def pieces(self, target, sems):
        p = self.p
        self.sends.arrived(5, 6)
        copies = []
        for index, block in enumerate((self.b2.at[p.r], self.b1.at[p.r, p.x_bit], self.b3)):
            copies.append(pltpu.make_async_copy(block, target.at[index], sems.at[index]))
            copies[-1].start()
        return copies

    def end(self):
        self.sends.left()


def flat(block):
    return block.reshape(block.shape[0] * block.shape[1], block.shape[2])


def layer_kernel(
    x, cot, q_w, k_w, v_w, o_w, u_w, d_w, q_b, v_b, u_b, g1, b1, ob, g2, b2, db,
    o_out, o_gx, o_small, o_ga, o_gf,
    a_own, f_own, small, small_all, a_all, f_all, rows_all, c_all, normed, qkv, turned, mix, lse,
    out_s, part, part_m, from_y, from_z, relay_y, relay_z, act_s, dup_s, res, d_res, e_own,
    dm_s, dk_s, dv_s, f1, f2, f3, a1, a2, a3, sums, sv, rv, cols, cs, rcs, rt,
    x_ss, x_rs, s_ss, s_rs, a_ss, a_rs, f_ss, f_rs, c_ss, c_rs, p_ss, p_rs,
    n_ss, n_rs, d_ss, d_rs, e_ss, e_rs, r_ss, r_rs, m_ss, m_rs, fg_ss, fg_rs, ag_ss, ag_rs,
    v_ss, v_rs, t_ss, t_rs, l_sem, free_sem,
):
    p = Place()
    rows, width = x.shape
    feat = a_own.shape[0]
    per, hid = q_b.shape[0], u_b.shape[0]
    hidp = f_own.shape[1] // 2
    greet(
        [(p.gx, lax.rem(p.gy + d, 8)) for d in range(1, 8)]
        + [(lax.rem(p.gx + d, 4), p.gy) for d in range(1, 4)]
    )
    gather = Gather(p, x, rows_all, x_ss, x_rs, CUT)
    gather.begin()
    stack = jnp.concatenate([w[...].astype(F32) for w in (q_w, k_w, v_w, o_w)], axis=0).T
    a_own[...] = jnp.concatenate(
        [stack, jnp.zeros((feat, a_own.shape[1] - stack.shape[1]), F32)], axis=1
    ).astype(BF)
    parts = (pl.ds(0, feat // 2), pl.ds(feat // 2, feat // 2))
    attn_w = [
        Spread(p, a_own, a_all, a_ss.at[i], a_rs.at[i], l_sem.at[i], parts[i]) for i in range(2)
    ]
    for item in attn_w:
        item.begin()
    small[...] = jnp.zeros_like(small)
    small[0:1, :per] = q_b[...].astype(F32).reshape(1, per)
    value_row = jnp.concatenate(
        [v_b[...].astype(F32).reshape(1, per), jnp.zeros((1, small.shape[1] - per), F32)], axis=1
    )
    small[0:1] += pltpu.roll(value_row, 2 * per, 1)
    small[1:2, :hid] = u_b[...].astype(F32).reshape(1, hid)
    for index, item in enumerate((g1, b1, ob, g2, b2, db)):
        small[2 + index : 3 + index, :per] = item[...].astype(F32).reshape(1, per)
    small_all[p.gy] = small[...]
    smalls = Sends(s_ss, s_rs)
    for d in range(1, 8):
        smalls.start(d - 1, small, small_all.at[p.gy], (p.gx, lax.rem(p.gy + d, 8)))
    for start, item in ((0, u_w), (hidp, d_w)):
        f_own[:, start + hidp - LANE : start + hidp] = jnp.zeros((feat, LANE), BF)
        f_own[:, start : start + hid] = item[...]
    feed_w = [
        Spread(p, f_own, f_all, f_ss.at[i], f_rs.at[i], l_sem.at[2 + i], parts[i])
        for i in range(2)
    ]
    cots = Gather(p, cot, c_all, c_ss, c_rs, CUT)
    c_all[p.t] = cot[...]
    smalls.arrived(*range(7))
    vec = jnp.zeros((8, width), F32)
    wide_per = -(-per // LANE) * LANE
    for g in range(8):
        vec = vec + spread(small_all[g][:, :wide_per], per * g, width)

    def norm(index, block):
        hat, _ = center_rows(block.astype(F32))
        normed[index] = (hat * vec[2:3] + vec[3:4]).astype(BF)

    norm(p.t, x[...])
    gather.forward()
    attn_w[0].second()
    attn_w[1].second()
    for item in feed_w:
        item.begin()
    gather.near()
    norm(p.ty, rows_all[p.ty])
    norm(p.tz, rows_all[p.tz])
    cots.begin()
    gather.far()
    norm(p.td, rows_all[p.td])
    for item in attn_w:
        item.third()
    for item in attn_w:
        item.done()

    def project(index, carry):
        block = normed[index]
        for group in range(2):
            bias = small_all[p.t + 4 * group, 0:1, :512]
            packed = nn(block, flat(a_all[group])[:, :512]) + bias
            for piece in range(6):
                qkv[piece // 2, 2 * group + piece % 2, pl.ds(index * rows, rows)] = lanes(
                    packed, HD * piece, LANE, HD
                ).astype(BF)
        return carry

    lax.fori_loop(0, 4, project, 0)
    for head in range(4):
        turned[head] = qkv[2, head].astype(F32).T.astype(BF)
    scatter = Scatter(p, part, from_y, from_z, relay_y, relay_z, p_ss, p_rs)

    def attend(index):
        def one(head, carry):
            start = pl.multiple_of(index * rows, rows)
            scores = nt(qkv[1, head], qkv[0, head, pl.ds(start, rows)])
            top = jnp.max(scores, axis=0, keepdims=True)
            expo = jnp.exp2((scores - top) * (SCALE * LOG2E))
            total = jnp.sum(expo, axis=0, keepdims=True)
            mixed = nn(turned[head], expo.astype(BF)) / total
            out_s[head] = mixed.T
            lse[head, index] = jnp.broadcast_to(
                top * (SCALE * LOG2E) + jnp.log2(total), lse.shape[2:]
            )
            return carry

        lax.fori_loop(0, 4, one, 0)
        total = jnp.zeros((rows, width), F32)
        for group in range(2):
            both = (
                spread(out_s[2 * group], 48, 256) + spread(out_s[2 * group + 1], 48 + HD, 256)
            ).astype(BF)
            mix[group, pl.ds(pl.multiple_of(index * rows, rows), rows)] = both
            total = total + nt(both, flat(a_all[group])[:, 384:640])
        part[index] = total.astype(BF)

    gather.end()
    attend(p.td)
    scatter.far()
    feed_w[0].second()
    attend(p.ty)
    scatter.near_y()
    feed_w[1].second()
    attend(p.tz)
    scatter.near_z()
    scatter.relay()
    cots.forward()
    attend(p.t)
    feed_w[0].third()
    feed_w[1].third()
    residual = x[...].astype(F32) + scatter.total() + vec[4:5]
    res[...] = residual
    hat, _ = center_rows(residual.astype(BF).astype(F32))
    rows_all[p.t] = (hat * vec[5:6] + vec[6:7]).astype(BF)
    gather_n = Gather(p, rows_all.at[p.t], rows_all, n_ss, n_rs, rows // 2)
    gather_n.begin()
    for item in (scatter, *attn_w):
        item.end()
    for item in feed_w:
        item.done()
    scatter_d = Scatter(p, part, from_y, from_z, relay_y, relay_z, d_ss, d_rs)
    cols[...] = jnp.zeros_like(cols)

    def feed(index):
        rows_two, rows_c = rows_all[index], c_all[index]
        out_m = jnp.zeros((rows, width), F32)
        out_d = jnp.zeros((rows, width), F32)
        for group in range(2):
            upper = (
                nn(rows_two, flat(f_all[group])[:, :hidp]) + small_all[p.t + 4 * group, 1:2, :hidp]
            )
            square = upper * upper
            tanh = jnp.tanh(ROOT * upper * (1.0 + 0.044715 * square))
            active = 0.5 * upper * (1.0 + tanh)
            slope = 0.5 * (1.0 + tanh) + 0.5 * upper * (1.0 - tanh * tanh) * (
                ROOT * (1.0 + 3.0 * 0.044715 * square)
            )
            act = active.astype(BF)
            act_s[group, index] = act
            dup = (nn(rows_c, flat(f_all[group])[:, hidp:]) * slope).astype(BF)
            dup_s[group, index] = dup
            cols[group : group + 1] += jnp.sum(dup.astype(F32), axis=0, keepdims=True)
            out_m = out_m + nt(act, flat(f_all[group])[:, hidp:])
            out_d = out_d + nt(dup, flat(f_all[group])[:, :hidp])
        part_m[index] = out_m.astype(BF)
        part[index] = out_d.astype(BF)

    feed(p.t)
    gather_n.forward()
    gather_n.near()
    cots.near()
    feed(p.ty)
    scatter_d.near_y()
    feed(p.tz)
    scatter_d.near_z()
    gather_n.far()
    cots.far()
    feed(p.td)
    scatter_d.far()
    for item in feed_w:
        item.end()
    for group in range(2):
        grad = tn(flat(rows_all[...]), flat(dup_s[group])).astype(BF)
        f_all[group, :, :, :hidp] = grad.reshape(4, feat, hidp)
        if group == 0:
            scatter_d.relay()
    for group in range(2):
        grad = tn(flat(c_all[...]), flat(act_s[group])).astype(BF)
        f_all[group, :, :, hidp:] = grad.reshape(4, feat, hidp)
    gather_n.end()
    cots.end()
    for peer in (p.near_y, p.near_z):
        pl.semaphore_signal(free_sem, inc=1, device_id=peer, device_id_type=MESH)
    feed_g = Reduce(p, f_all, f1, f2, f3, fg_ss, fg_rs)
    feed_g.begin()
    grad = scatter_d.total()
    hat, inverse = center_rows(res[...].astype(BF).astype(F32))
    cot_f = cot[...].astype(F32)
    d_residual = cot_f + norm_back(grad, vec[5:6], hat, inverse)
    d_res[...] = d_residual
    e_own[...] = d_residual.astype(BF)
    pl.semaphore_wait(free_sem, 2)
    gather_e = Gather(p, e_own, rows_all, e_ss, e_rs, CUT)
    gather_e.begin()
    rows_all[p.t] = e_own[...]
    sums[...] = jnp.zeros_like(sums)
    sums[2:3] = jnp.sum(d_residual, axis=0, keepdims=True)
    sums[3:4] = jnp.sum(grad * hat, axis=0, keepdims=True)
    sums[4:5] = jnp.sum(grad, axis=0, keepdims=True)
    sums[5:6] = jnp.sum(cot_f, axis=0, keepdims=True)
    cut_m = rows - CUT
    scatter_m = Scatter(
        p, part_m, c_all.at[0], c_all.at[1], c_all.at[2].at[pl.ds(0, cut_m)],
        c_all.at[2].at[pl.ds(cut_m, CUT)], m_ss, m_rs,
    )
    scatter_d.end()
    for head in range(4):
        turned[head] = qkv[1, head].astype(F32).T.astype(BF)
    dk_s[...] = jnp.zeros_like(dk_s)
    dv_s[...] = jnp.zeros_like(dv_s)

    def attend_back(index):
        block = rows_all[index]
        for group in range(2):
            mixed = nn(block, flat(a_all[group])[:, 384:640])
            dm_s[2 * group] = lanes(mixed, 48, LANE, HD).astype(BF)
            dm_s[2 * group + 1] = lanes(mixed, 48 + HD, LANE, HD).astype(BF)

        def one(head, carry):
            start = pl.multiple_of(index * rows, rows)
            q_rows, d_mix = qkv[0, head, pl.ds(start, rows)], dm_s[head]
            scores = nt(qkv[1, head], q_rows)
            probs = jnp.exp2(scores * (SCALE * LOG2E) - lse[head, index, 0:1])
            d_probs = nt(qkv[2, head], d_mix)
            delta = jnp.sum(d_probs * probs, axis=0, keepdims=True)
            d_scores = (probs * (d_probs - delta)).astype(BF)
            dv_s[head] += nn(probs.astype(BF), d_mix)
            dk_s[head] += nn(d_scores, q_rows)
            out_s[head] = nn(turned[head], d_scores).T * SCALE
            return carry

        lax.fori_loop(0, 4, one, 0)
        for head in range(4):
            place = LANE * (head % 2)
            dup_s[head // 2, index, :, place : place + LANE] = out_s[head].astype(BF)

    attend_back(p.t)
    gather_e.forward()
    scatter_m.far()
    feed_g.second()
    gather_e.near()
    scatter_m.near_y()
    scatter_m.near_z()
    attend_back(p.ty)
    attend_back(p.tz)
    feed_g.third()
    gather_e.far()
    attend_back(p.td)
    scatter_n = Scatter(p, part, from_y, from_z, relay_y, relay_z, r_ss, r_rs)
    cs[...] = jnp.zeros_like(cs)

    def give(index):
        here = pl.ds(pl.multiple_of(index * rows, rows), rows)
        total = jnp.zeros((rows, width), F32)
        for group in range(2):
            packed = jnp.zeros((rows, 512), F32)
            for piece in range(6):
                head = 2 * group + piece % 2
                if piece < 2:
                    value = dup_s[group, index, :, LANE * piece : LANE * (piece + 1)].astype(F32)
                elif piece < 4:
                    value = dk_s[head, here] * SCALE
                else:
                    value = dv_s[head, here]
                packed = packed + spread(value, HD * piece, 512)
            packed = packed.astype(BF)
            act_s[group, index, :, :512] = packed
            cs[group, 0:1, :512] += jnp.sum(packed.astype(F32), axis=0, keepdims=True)
            total = total + nt(packed, flat(a_all[group])[:, :512])
        part[index] = total.astype(BF)

    give(p.td)
    scatter_n.far()
    give(p.ty)
    scatter_n.near_y()
    give(p.tz)
    scatter_n.near_z()
    give(p.t)
    scatter_m.relay()
    for group in range(2):
        main = tn(flat(normed[...]), flat(act_s[group])[:, :512])
        outer = tn(flat(rows_all[...]), mix[group])
        both = jnp.concatenate(
            [main[:, :384], main[:, 384:] + outer[:, :128], outer[:, 128:]], axis=1
        )
        a_all[group] = both.astype(BF).reshape(4, feat, 640)
        if group == 0:
            scatter_n.relay()
    attn_g = Reduce(p, a_all, a1, a2, a3, ag_ss, ag_rs)
    attn_g.begin()
    attn_g.second()
    o_out[...] = (res[...] + scatter_m.total() + vec[7:8]).astype(BF)
    grad = scatter_n.total()
    hat, inverse = center_rows(x[...].astype(F32))
    o_gx[...] = (d_res[...] + norm_back(grad, vec[2:3], hat, inverse)).astype(BF)
    row = lax.broadcasted_iota(jnp.int32, sums.shape, 0)
    all_sums = sums[...]
    all_sums = jnp.where(row == 0, jnp.sum(grad * hat, axis=0, keepdims=True), all_sums)
    all_sums = jnp.where(row == 1, jnp.sum(grad, axis=0, keepdims=True), all_sums)
    for g in range(8):
        sv[g] = lanes(all_sums, per * g, sv.shape[2], per)
    for group in range(2):
        cs[group, 1:2] = cols[group : group + 1]
    slices = Sends(v_ss, v_rs)
    for d in range(1, 8):
        other = lax.rem(p.gy + d, 8)
        slices.start(d - 1, sv.at[other], rv.at[p.gy], (p.gx, other))
    slices.start(7, cs.at[p.other_r], rcs, p.half)
    rv[p.gy] = sv[p.gy]
    attn_g.third()
    slices.arrived(*range(8))
    total = rv[0]
    for g in range(1, 8):
        total = total + rv[g]
    mine = rt.at[p.gx]
    mine[0:8] = jnp.concatenate(
        [total, jnp.zeros((8, rt.shape[2] - total.shape[1]), F32)], axis=1
    )
    mine[8:16] = cs[p.r] + rcs[...]
    totals = Sends(t_ss, t_rs)
    for d in range(1, 4):
        totals.start(d - 1, mine, mine, (lax.rem(p.gx + d, 4), p.gy))
    copies = feed_g.pieces(o_gf, l_sem.at[pl.ds(4, 3)])
    totals.arrived(0, 1, 2)
    o_small[...] = rt[0] + rt[1] + rt[2] + rt[3]
    copies += attn_g.pieces(o_ga, l_sem.at[pl.ds(7, 3)])
    for copy in copies:
        copy.wait()
    for item in (smalls, slices, totals):
        item.left()
    for item in (gather_e, feed_g, attn_g, scatter_n, scatter_m):
        item.end()


VM = pl.BlockSpec(memory_space=pltpu.VMEM)
ANY = pl.BlockSpec(memory_space=pl.ANY)


def dma(shape):
    return pltpu.SemaphoreType.DMA(shape)


def finish_kernel(
    out, gx, ga, gf, small,
    o_out, o_gx, o_g1, o_b1, o_q, o_qb, o_k, o_v, o_vb, o_o, o_ob, o_g2, o_b2, o_u, o_ub, o_d, o_db,
):
    per, hid = o_g1.shape[0], o_ub.shape[0]
    hidp = gf.shape[2] // 2
    o_out[...] = out[...]
    o_gx[...] = gx[...]
    stack = (ga[0].astype(F32) + ga[1].astype(F32) + ga[2].astype(F32)).T
    for index, item in enumerate((o_q, o_k, o_v, o_o)):
        item[...] = stack[per * index : per * (index + 1)]
    grads = gf[0].astype(F32) + gf[1].astype(F32) + gf[2].astype(F32)
    o_u[...] = grads[:, :hid]
    o_d[...] = grads[:, hidp : hidp + hid]
    for index, item in enumerate((o_g1, o_b1, o_ob, o_g2, o_b2, o_db)):
        item[...] = small[index : index + 1, :per].reshape(per)
    o_qb[...] = small[8:9, :per].reshape(per)
    o_vb[...] = pltpu.roll(small[8:9], small.shape[1] - 2 * per, 1)[:, :per].reshape(per)
    o_ub[...] = small[9:10, :hid].reshape(hid)


def fast_shards(
    layer_input, norm_one_gain, norm_one_bias, query_weight, query_bias, key_weight, value_weight,
    value_bias, output_weight, output_bias, norm_two_gain, norm_two_bias, up_weight, up_bias,
    down_weight, down_bias, cotangent,
):
    rows, width = layer_input.shape
    per, hid = query_weight.shape[1], up_weight.shape[1]
    feat = query_weight.shape[0]
    hidp = -(-hid // LANE) * LANE
    aw = 640
    shape, bf, f32 = jax.ShapeDtypeStruct, BF, F32
    params = lambda number: pltpu.CompilerParams(
        collective_id=number, has_side_effects=True, vmem_limit_bytes=VMEM_LIMIT
    )
    full = (rows, width)
    block4 = pltpu.VMEM((4, rows, width), bf)

    wide = -(-per // LANE) * LANE
    block = pltpu.VMEM(full, bf)
    hidden = pltpu.VMEM((2, 4, rows, hidp), bf)
    heads = pltpu.VMEM((4, 4 * rows, LANE), f32)
    six, seven = dma((6,)), dma((7,))
    (out, grad_input, smalls, ga, gfo) = pl.pallas_call(
        layer_kernel,
        name="layer",
        out_shape=[
            shape(full, bf), shape(full, bf), shape((16, aw), f32), shape((3, feat, aw), bf),
            shape((3, feat, 2 * hidp), bf),
        ],
        in_specs=[VM] * 17,
        out_specs=[VM] * 3 + [ANY] * 2,
        scratch_shapes=[
            pltpu.VMEM((feat, aw), bf), pltpu.VMEM((feat, 2 * hidp), bf), pltpu.VMEM((8, aw), f32),
            pltpu.VMEM((8, 8, aw), f32), pltpu.VMEM((2, 4, feat, aw), bf),
            pltpu.VMEM((2, 4, feat, 2 * hidp), bf), block4, block4, block4,
            pltpu.VMEM((3, 4, 4 * rows, LANE), bf), pltpu.VMEM((4, LANE, 4 * rows), bf),
            pltpu.VMEM((2, 4 * rows, 256), bf), pltpu.VMEM((4, 4, 8, rows), f32),
            pltpu.VMEM((4, rows, LANE), f32), block4, block4, block, block,
            pltpu.VMEM((rows // 2, width), bf), pltpu.VMEM((rows // 2, width), bf),
            hidden, hidden, pltpu.VMEM(full, f32), pltpu.VMEM(full, f32), block,
            pltpu.VMEM((4, rows, LANE), bf), heads, heads,
            pltpu.VMEM((2, 2, feat, 2 * hidp), bf), pltpu.VMEM((2, feat, 2 * hidp), bf),
            pltpu.VMEM((feat, 2 * hidp), bf), pltpu.VMEM((2, 2, feat, aw), bf),
            pltpu.VMEM((2, feat, aw), bf), pltpu.VMEM((feat, aw), bf),
            pltpu.VMEM((8, width), f32), pltpu.VMEM((8, 8, wide), f32),
            pltpu.VMEM((8, 8, wide), f32), pltpu.VMEM((8, hidp), f32), pltpu.VMEM((2, 8, aw), f32),
            pltpu.VMEM((8, aw), f32), pltpu.VMEM((4, 16, aw), f32),
            six, six, seven, seven, dma((2, 7)), dma((2, 7)), dma((2, 7)), dma((2, 7)), six, six,
            six, six, six, six, six, six, six, six, six, six, six, six, seven, seven, seven, seven,
            dma((8,)), dma((8,)), dma((3,)), dma((3,)), dma((10,)), pltpu.SemaphoreType.REGULAR,
        ],
        compiler_params=params(0),
    )(
        layer_input, cotangent, query_weight.T, key_weight.T, value_weight.T, output_weight,
        up_weight, down_weight.T, query_bias, value_bias, up_bias, norm_one_gain, norm_one_bias,
        output_bias, norm_two_gain, norm_two_bias, down_bias,
    )
    line = shape((per,), f32)
    turned = shape((per, feat), f32)
    done = pl.pallas_call(
        finish_kernel,
        name="finish",
        out_shape=[
            shape(full, bf), shape(full, bf), line, line, turned, line, turned, turned, line,
            turned, line, line, line, shape((feat, hid), f32), shape((hid,), f32),
            shape((feat, hid), f32), line,
        ],
        in_specs=[VM] * 5,
        out_specs=[VM] * 17,
        compiler_params=pltpu.CompilerParams(vmem_limit_bytes=VMEM_LIMIT),
    )(out, grad_input, ga, gfo, smalls)
    done = list(done)
    for index in (4, 6, 7, 15):
        done[index] = done[index].T
    return tuple(done)


def dot_plain(left, right):
    return jnp.dot(left, right, preferred_element_type=jnp.float32)


def dot_right_t(left, right):
    return lax.dot_general(
        left, right, (((1,), (1,)), ((), ())), preferred_element_type=jnp.float32
    )


def dot_left_t(left, right):
    return lax.dot_general(
        left, right, (((0,), (0,)), ((), ())), preferred_element_type=jnp.float32
    )


def normalize(rows):
    center = rows - jnp.mean(rows, axis=-1, keepdims=True)
    inverse = lax.rsqrt(jnp.mean(center * center, axis=-1, keepdims=True) + 1e-06)
    return (center * inverse, inverse)


def gelu_tanh(value):
    return jax.nn.gelu(value, approximate=True)


def image_shape(array):
    heads = array.shape[1] // HD
    return (array.shape[0] // LENGTH, LENGTH, heads, HD)


def attend(query, key, value):
    shape = image_shape(query)
    scale = HD ** (-0.5)

    def one_image(carry, pieces):
        q_img, k_img, v_img = pieces
        scores = (
            jnp.einsum("qhd,khd->hqk", q_img, k_img, preferred_element_type=jnp.float32) * scale
        )
        top = jnp.max(scores, axis=-1, keepdims=True)
        expo = jnp.exp(scores - top)
        total = jnp.sum(expo, axis=-1, keepdims=True)
        probs = (expo / total).astype(jnp.bfloat16)
        mixed = jnp.einsum("hqk,khd->qhd", probs, v_img, preferred_element_type=jnp.float32).astype(
            jnp.bfloat16
        )
        return (carry, (mixed, (top + jnp.log(total))[..., 0]))

    _, (mixed, lse) = lax.scan(
        one_image, 0, (query.reshape(shape), key.reshape(shape), value.reshape(shape))
    )
    return (mixed.reshape(query.shape), lse)


def attend_back(query, key, value, lse, d_mixed):
    shape = image_shape(query)
    scale = HD ** (-0.5)

    def one_image(carry, pieces):
        q_img, k_img, v_img, lse_img, dm_img = pieces
        scores = (
            jnp.einsum("qhd,khd->hqk", q_img, k_img, preferred_element_type=jnp.float32) * scale
        )
        probs = jnp.exp(scores - lse_img[..., None])
        d_probs = jnp.einsum("qhd,khd->hqk", dm_img, v_img, preferred_element_type=jnp.float32)
        d_scores = (probs * (d_probs - jnp.sum(d_probs * probs, axis=-1, keepdims=True))).astype(
            jnp.bfloat16
        )
        d_value = jnp.einsum(
            "hqk,qhd->khd", probs.astype(jnp.bfloat16), dm_img, preferred_element_type=jnp.float32
        ).astype(jnp.bfloat16)
        d_query = (
            jnp.einsum("hqk,khd->qhd", d_scores, k_img, preferred_element_type=jnp.float32) * scale
        ).astype(jnp.bfloat16)
        d_key = (
            jnp.einsum("hqk,qhd->khd", d_scores, q_img, preferred_element_type=jnp.float32) * scale
        ).astype(jnp.bfloat16)
        return (carry, (d_query, d_key, d_value))

    _, (d_query, d_key, d_value) = lax.scan(
        one_image,
        0,
        (
            query.reshape(shape),
            key.reshape(shape),
            value.reshape(shape),
            lse,
            d_mixed.reshape(shape),
        ),
    )
    return (d_query.reshape(query.shape), d_key.reshape(query.shape), d_value.reshape(query.shape))


def forward_pass(
    layer_input,
    norm_one_gain,
    norm_one_bias,
    query_weight,
    query_bias,
    key_weight,
    value_weight,
    value_bias,
    output_weight,
    output_bias,
    norm_two_gain,
    norm_two_bias,
    up_weight,
    up_bias,
    down_weight,
    down_bias,
):
    w_query, w_key, w_value, w_output, w_up, w_down = (
        lax.all_gather(query_weight, "gx", axis=0, tiled=True),
        lax.all_gather(key_weight, "gx", axis=0, tiled=True),
        lax.all_gather(value_weight, "gx", axis=0, tiled=True),
        lax.all_gather(output_weight, "gx", axis=1, tiled=True),
        lax.all_gather(up_weight, "gx", axis=0, tiled=True),
        lax.all_gather(down_weight, "gx", axis=1, tiled=True),
    )
    rows_one, gain_one, shift_one, out_shift, down_shift = (
        lax.all_gather(layer_input, "gy", axis=0, tiled=True),
        lax.all_gather(norm_one_gain, "gy", axis=0, tiled=True),
        lax.all_gather(norm_one_bias, "gy", axis=0, tiled=True),
        lax.all_gather(output_bias, "gy", axis=0, tiled=True),
        lax.all_gather(down_bias, "gy", axis=0, tiled=True),
    )
    hat_one, inv_one = normalize(rows_one.astype(jnp.float32))
    normed = (hat_one * gain_one.astype(jnp.float32) + shift_one.astype(jnp.float32)).astype(
        jnp.bfloat16
    )
    query = (dot_plain(normed, w_query) + query_bias.astype(jnp.float32)).astype(jnp.bfloat16)
    key = dot_plain(normed, w_key).astype(jnp.bfloat16)
    value = (dot_plain(normed, w_value) + value_bias.astype(jnp.float32)).astype(jnp.bfloat16)
    mixed, lse = attend(query, key, value)
    attn_part = lax.psum_scatter(
        dot_plain(mixed, w_output).astype(jnp.bfloat16), "gy", scatter_dimension=0, tiled=True
    ).astype(jnp.float32)
    residual = layer_input.astype(jnp.float32) + attn_part + out_shift.astype(jnp.float32)
    rows_two, gain_two, shift_two = (
        lax.all_gather(residual.astype(jnp.bfloat16), "gy", axis=0, tiled=True),
        lax.all_gather(norm_two_gain, "gy", axis=0, tiled=True),
        lax.all_gather(norm_two_bias, "gy", axis=0, tiled=True),
    )
    hat_two, inv_two = normalize(rows_two.astype(jnp.float32))
    normed_two = (hat_two * gain_two.astype(jnp.float32) + shift_two.astype(jnp.float32)).astype(
        jnp.bfloat16
    )
    upper = dot_plain(normed_two, w_up) + up_bias.astype(jnp.float32)
    active = gelu_tanh(upper).astype(jnp.bfloat16)
    mlp_part = lax.psum_scatter(
        dot_plain(active, w_down).astype(jnp.bfloat16), "gy", scatter_dimension=0, tiled=True
    ).astype(jnp.float32)
    result = (residual + mlp_part + down_shift.astype(jnp.float32)).astype(jnp.bfloat16)
    saved = (
        w_query,
        w_key,
        w_value,
        w_output,
        w_up,
        w_down,
        hat_one,
        inv_one,
        normed,
        query,
        key,
        value,
        mixed,
        lse,
        hat_two,
        inv_two,
        normed_two,
        upper,
        active,
        gain_one,
        gain_two,
    )
    return saved, result


def shards(
    layer_input,
    norm_one_gain,
    norm_one_bias,
    query_weight,
    query_bias,
    key_weight,
    value_weight,
    value_bias,
    output_weight,
    output_bias,
    norm_two_gain,
    norm_two_bias,
    up_weight,
    up_bias,
    down_weight,
    down_bias,
    cotangent,
):
    inputs = (
        layer_input,
        norm_one_gain,
        norm_one_bias,
        query_weight,
        query_bias,
        key_weight,
        value_weight,
        value_bias,
        output_weight,
        output_bias,
        norm_two_gain,
        norm_two_bias,
        up_weight,
        up_bias,
        down_weight,
        down_bias,
    )
    saved, layer_output = forward_pass(*inputs)
    (
        w_query,
        w_key,
        w_value,
        w_output,
        w_up,
        w_down,
        hat_one,
        inv_one,
        normed,
        query,
        key,
        value,
        mixed,
        lse,
        hat_two,
        inv_two,
        normed_two,
        upper,
        active,
        gain_one,
        gain_two,
    ) = saved
    local = layer_input.shape[0]
    start = lax.axis_index("gy") * local
    grad_rows = lax.all_gather(cotangent, "gy", axis=0, tiled=True)
    d_active = dot_right_t(grad_rows, w_down)
    _, gelu_pull = jax.vjp(gelu_tanh, upper)
    d_upper = gelu_pull(d_active)[0].astype(jnp.bfloat16)
    grad_up_weight, grad_down_weight = (
        lax.psum_scatter(
            dot_left_t(normed_two, d_upper).astype(jnp.bfloat16),
            "gx",
            scatter_dimension=0,
            tiled=True,
        ).astype(jnp.float32),
        lax.psum_scatter(
            dot_left_t(active, grad_rows).astype(jnp.bfloat16),
            "gx",
            scatter_dimension=1,
            tiled=True,
        ).astype(jnp.float32),
    )
    d_normed_two = lax.psum_scatter(
        dot_right_t(d_upper, w_up).astype(jnp.bfloat16), "gy", scatter_dimension=0, tiled=True
    ).astype(jnp.float32)
    hat_two_local = lax.dynamic_slice_in_dim(hat_two, start, local, 0)
    inv_two_local = lax.dynamic_slice_in_dim(inv_two, start, local, 0)
    scaled_two = d_normed_two * gain_two.astype(jnp.float32)
    mean_two = jnp.mean(scaled_two, axis=-1, keepdims=True)
    proj_two = jnp.mean(scaled_two * hat_two_local, axis=-1, keepdims=True)
    cot_float = cotangent.astype(jnp.float32)
    d_residual = cot_float + inv_two_local * (scaled_two - mean_two - hat_two_local * proj_two)
    part_two_gain = jnp.sum(d_normed_two * hat_two_local, axis=0)
    part_two_bias = jnp.sum(d_normed_two, axis=0)
    part_up_bias = jnp.sum(d_upper.astype(jnp.float32), axis=0)
    part_down_bias = jnp.sum(cot_float, axis=0)
    grad_attn = lax.all_gather(d_residual.astype(jnp.bfloat16), "gy", axis=0, tiled=True)
    part_output_bias = jnp.sum(d_residual, axis=0)
    d_mixed = dot_right_t(grad_attn, w_output).astype(jnp.bfloat16)
    d_query, d_key, d_value = attend_back(query, key, value, lse, d_mixed)
    grad_query_weight, grad_key_weight, grad_value_weight, grad_output_weight = (
        lax.psum_scatter(
            dot_left_t(normed, d_query).astype(jnp.bfloat16), "gx", scatter_dimension=0, tiled=True
        ).astype(jnp.float32),
        lax.psum_scatter(
            dot_left_t(normed, d_key).astype(jnp.bfloat16), "gx", scatter_dimension=0, tiled=True
        ).astype(jnp.float32),
        lax.psum_scatter(
            dot_left_t(normed, d_value).astype(jnp.bfloat16), "gx", scatter_dimension=0, tiled=True
        ).astype(jnp.float32),
        lax.psum_scatter(
            dot_left_t(mixed, grad_attn).astype(jnp.bfloat16), "gx", scatter_dimension=1, tiled=True
        ).astype(jnp.float32),
    )
    d_normed = lax.psum_scatter(
        (
            dot_right_t(d_query, w_query)
            + dot_right_t(d_key, w_key)
            + dot_right_t(d_value, w_value)
        ).astype(jnp.bfloat16),
        "gy",
        scatter_dimension=0,
        tiled=True,
    ).astype(jnp.float32)
    hat_one_local = lax.dynamic_slice_in_dim(hat_one, start, local, 0)
    inv_one_local = lax.dynamic_slice_in_dim(inv_one, start, local, 0)
    scaled_one = d_normed * gain_one.astype(jnp.float32)
    mean_one = jnp.mean(scaled_one, axis=-1, keepdims=True)
    proj_one = jnp.mean(scaled_one * hat_one_local, axis=-1, keepdims=True)
    grad_input = (
        d_residual + inv_one_local * (scaled_one - mean_one - hat_one_local * proj_one)
    ).astype(jnp.bfloat16)
    part_one_gain = jnp.sum(d_normed * hat_one_local, axis=0)
    part_one_bias = jnp.sum(d_normed, axis=0)
    part_query_bias = jnp.sum(d_query.astype(jnp.float32), axis=0)
    part_value_bias = jnp.sum(d_value.astype(jnp.float32), axis=0)
    feat_one_gain, feat_one_bias, feat_output_bias, feat_two_gain, feat_two_bias, feat_down_bias = (
        lax.psum_scatter(part_one_gain, "gy", scatter_dimension=0, tiled=True),
        lax.psum_scatter(part_one_bias, "gy", scatter_dimension=0, tiled=True),
        lax.psum_scatter(part_output_bias, "gy", scatter_dimension=0, tiled=True),
        lax.psum_scatter(part_two_gain, "gy", scatter_dimension=0, tiled=True),
        lax.psum_scatter(part_two_bias, "gy", scatter_dimension=0, tiled=True),
        lax.psum_scatter(part_down_bias, "gy", scatter_dimension=0, tiled=True),
    )
    (
        grad_one_gain,
        grad_one_bias,
        grad_query_bias,
        grad_value_bias,
        grad_output_bias,
        grad_two_gain,
        grad_two_bias,
        grad_up_bias,
        grad_down_bias,
    ) = lax.psum(
        (
            feat_one_gain,
            feat_one_bias,
            part_query_bias,
            part_value_bias,
            feat_output_bias,
            feat_two_gain,
            feat_two_bias,
            part_up_bias,
            feat_down_bias,
        ),
        "gx",
    )
    return (
        layer_output,
        grad_input,
        grad_one_gain,
        grad_one_bias,
        grad_query_weight,
        grad_query_bias,
        grad_key_weight,
        grad_value_weight,
        grad_value_bias,
        grad_output_weight,
        grad_output_bias,
        grad_two_gain,
        grad_two_bias,
        grad_up_weight,
        grad_up_bias,
        grad_down_weight,
        grad_down_bias,
    )


def solution(mesh):
    fits = mesh.shape["gx"] == 4 and mesh.shape["gy"] == 8
    return jax.shard_map(
        fast_shards if fits else shards,
        mesh=mesh,
        in_specs=(
            P(("gx", "gy"), None),
            P("gy"),
            P("gy"),
            P("gx", "gy"),
            P("gy"),
            P("gx", "gy"),
            P("gx", "gy"),
            P("gy"),
            P("gy", "gx"),
            P("gy"),
            P("gy"),
            P("gy"),
            P("gx", "gy"),
            P("gy"),
            P("gy", "gx"),
            P("gy"),
            P(("gx", "gy"), None),
        ),
        out_specs=(
            P(("gx", "gy"), None),
            P(("gx", "gy"), None),
            P("gy"),
            P("gy"),
            P("gx", "gy"),
            P("gy"),
            P("gx", "gy"),
            P("gx", "gy"),
            P("gy"),
            P("gy", "gx"),
            P("gy"),
            P("gy"),
            P("gy"),
            P("gx", "gy"),
            P("gy"),
            P("gy", "gx"),
            P("gy"),
        ),
        check_vma=False,
    )
```

```python
import functools
import math

import jax
import jax.numpy as jnp
from jax import lax
from jax.experimental import pallas as pl
from jax.experimental.pallas import tpu as pltpu
from jax.sharding import PartitionSpec as P

HD = 72
LENGTH = 1024
LANE = 128
BF = jnp.bfloat16
F32 = jnp.float32
MESH = pl.DeviceIdType.MESH
TP = 4
VMEM_LIMIT = 63 << 20
SCALE = HD ** (-0.5)
CUT = 80
HALF_CUT = 48
LOG2E = 1.4426950408889634
ROOT = math.sqrt(2.0 / math.pi)


def nn(left, right):
    return jnp.dot(left, right, preferred_element_type=F32)


def nt(left, right):
    return lax.dot_general(left, right, (((1,), (1,)), ((), ())), preferred_element_type=F32)


def tn(left, right):
    return lax.dot_general(left, right, (((0,), (0,)), ((), ())), preferred_element_type=F32)


def center_rows(rows):
    center = rows - jnp.mean(rows, axis=-1, keepdims=True)
    inverse = lax.rsqrt(jnp.mean(center * center, axis=-1, keepdims=True) + 1e-06)
    return center * inverse, inverse


def norm_back(grad, gain, hat, inverse):
    scaled = grad * gain
    mean = jnp.mean(scaled, axis=-1, keepdims=True)
    proj = jnp.mean(scaled * hat, axis=-1, keepdims=True)
    return inverse * (scaled - mean - hat * proj)


def lanes(value, start, width, keep):
    full = value.shape[1]
    moved = value if start == 0 else pltpu.roll(value, full - start, 1)
    part = moved[:, :width]
    return jnp.where(lax.broadcasted_iota(jnp.int32, part.shape, 1) < keep, part, 0.0)


def spread(value, start, full):
    wide = jnp.concatenate([value, jnp.zeros((value.shape[0], full - value.shape[1]), F32)], axis=1)
    return wide if start == 0 else pltpu.roll(wide, start, 1)


class Place:
    def __init__(self):
        gx, gy = lax.axis_index("gx"), lax.axis_index("gy")
        self.gx, self.gy = gx, gy
        self.t, self.r = lax.rem(gy, 4), lax.div(gy, 4)
        y, z = lax.rem(gy, 2), lax.rem(lax.div(gy, 2), 2)
        self.ty = self.t + 1 - 2 * y
        self.tz = self.t + 2 - 4 * z
        self.td = 3 - self.t
        base = 4 * self.r
        self.near_y = (gx, base + self.ty)
        self.near_z = (gx, base + self.tz)
        self.other_r = 1 - self.r
        self.half = (gx, lax.rem(gy + 4, 8))
        self.core_bit, self.x_bit = lax.rem(gx, 2), lax.div(gx, 2)
        self.gx_core = gx + 1 - 2 * self.core_bit
        self.gx_x = lax.rem(gx + 2, 4)
        self.core = (self.gx_core, gy)
        self.chip_x = (self.gx_x, gy)


def greet(peers, meanwhile):
    barrier = pltpu.get_barrier_semaphore()
    for peer in peers:
        pl.semaphore_signal(barrier, inc=1, device_id=peer, device_id_type=MESH)
    meanwhile()
    pl.semaphore_wait(barrier, len(peers))


class Sends:
    def __init__(self, send_sem, recv_sem):
        self.send_sem, self.recv_sem, self.copies = send_sem, recv_sem, {}

    def start(self, index, source, target, peer):
        copy = pltpu.make_async_remote_copy(
            src_ref=source,
            dst_ref=target,
            send_sem=self.send_sem.at[index],
            recv_sem=self.recv_sem.at[index],
            device_id=peer,
            device_id_type=MESH,
        )
        copy.start()
        self.copies[index] = copy

    def arrived(self, *indices):
        for index in indices:
            self.copies[index].wait_recv()

    def left(self):
        for copy in self.copies.values():
            copy.wait_send()


class Gather:
    def __init__(self, place, source, target, send_sem, recv_sem, cut):
        self.p, self.dst = place, target
        self.sends = Sends(send_sem, recv_sem)
        self.lo, self.hi = pl.ds(0, cut), pl.ds(cut, source.shape[0] - cut)
        self.src = source

    def begin(self):
        p, own = self.p, self.dst.at[self.p.t]
        for index, part, peer in (
            (0, self.lo, p.near_y),
            (2, self.hi, p.near_z),
            (1, self.hi, p.near_y),
            (3, self.lo, p.near_z),
        ):
            self.sends.start(index, self.src.at[part], own.at[part], peer)

    def forward(self):
        p = self.p
        self.sends.arrived(0)
        block = self.dst.at[p.ty].at[self.lo]
        self.sends.start(4, block, block, p.near_z)
        self.sends.arrived(2)
        block = self.dst.at[p.tz].at[self.hi]
        self.sends.start(5, block, block, p.near_y)

    def near(self):
        self.sends.arrived(1, 3)

    def far(self):
        self.sends.arrived(4, 5)

    def end(self):
        self.sends.left()


class Scatter:
    def __init__(self, place, part, from_y, from_z, relay_y, relay_z, send_sem, recv_sem):
        self.p, self.part = place, part
        self.from_y, self.from_z, self.relay_y, self.relay_z = from_y, from_z, relay_y, relay_z
        self.sends = Sends(send_sem, recv_sem)
        cut = relay_y.shape[0]
        self.cut = cut
        self.lo, self.hi = pl.ds(0, cut), pl.ds(cut, relay_z.shape[0])

    def far(self):
        p, block = self.p, self.part.at[self.p.td]
        self.sends.start(0, block.at[self.lo], self.relay_y, p.near_y)
        self.sends.start(1, block.at[self.hi], self.relay_z, p.near_z)

    def near_y(self):
        p = self.p
        self.sends.start(2, self.part.at[p.ty].at[self.lo], self.from_y.at[self.lo], p.near_y)

    def near_z(self):
        p = self.p
        self.sends.start(3, self.part.at[p.tz].at[self.hi], self.from_z.at[self.hi], p.near_z)

    def relay(self):
        p, cut = self.p, self.cut
        self.sends.arrived(0)
        block = self.part.at[p.tz]
        block[:cut] = (block[:cut].astype(F32) + self.relay_y[...].astype(F32)).astype(BF)
        self.sends.start(4, block.at[self.lo], self.from_z.at[self.lo], p.near_z)
        self.sends.arrived(1)
        block = self.part.at[p.ty]
        block[cut:] = (block[cut:].astype(F32) + self.relay_z[...].astype(F32)).astype(BF)
        self.sends.start(5, block.at[self.hi], self.from_y.at[self.hi], p.near_y)

    def total(self):
        self.sends.arrived(2, 3, 4, 5)
        own = self.part[self.p.t].astype(F32)
        return own + self.from_y[...].astype(F32) + self.from_z[...].astype(F32)

    def end(self):
        self.sends.left()


class Spread:
    def __init__(self, place, source, target, send_sem, recv_sem, local_sem, part):
        self.p, self.part = place, part
        self.src, self.dst = source.at[part], target
        self.sends = Sends(send_sem, recv_sem)
        self.local = pltpu.make_async_copy(
            self.src, target.at[place.r, place.gx].at[part], local_sem
        )

    def slot(self, group, column):
        return self.dst.at[group, column].at[self.part]

    def begin(self):
        p = self.p
        slot = self.slot(p.r, p.gx)
        self.sends.start(0, self.src, slot, p.half)
        self.sends.start(1, self.src, slot, p.chip_x)
        self.sends.start(2, self.src, slot, p.core)
        self.local.start()

    def second(self):
        p = self.p
        self.sends.arrived(0)
        slot = self.slot(p.other_r, p.gx)
        self.sends.start(3, slot, slot, p.chip_x)
        self.sends.start(4, slot, slot, p.core)

    def third(self):
        p = self.p
        self.sends.arrived(1)
        slot = self.slot(p.r, p.gx_x)
        self.sends.start(5, slot, slot, p.core)
        self.sends.arrived(3)
        slot = self.slot(p.other_r, p.gx_x)
        self.sends.start(6, slot, slot, p.core)

    def done(self):
        self.sends.arrived(2, 4, 5, 6)
        self.local.wait()

    def end(self):
        self.sends.left()


class Reduce:
    def __init__(self, place, source, first, second, third, send_sem, recv_sem, part):
        self.p, self.part = place, part
        self.src, self.b1, self.b2, self.b3 = source, first, second, third.at[part]
        self.sends = Sends(send_sem, recv_sem)

    def begin(self, late):
        p = self.p
        group = p.r if late else p.other_r
        for index, side in ((2 * late, 1 - p.x_bit), (2 * late + 1, p.x_bit)):
            block = self.src.at[group, 2 * side + 1 - p.core_bit].at[self.part]
            self.sends.start(index, block, self.b1.at[group, side].at[self.part], p.core)

    def add(self, index, group, side):
        self.sends.arrived(index)
        block = self.b1.at[group, side].at[self.part]
        mine = self.src.at[group, 2 * side + self.p.core_bit].at[self.part]
        block[...] = (block[...].astype(F32) + mine[...].astype(F32)).astype(BF)
        return block

    def second(self, late):
        p = self.p
        group = p.r if late else p.other_r
        block = self.add(2 * late, group, 1 - p.x_bit)
        self.sends.start(4 + late, block, self.b2.at[group].at[self.part], p.chip_x)
        self.add(2 * late + 1, group, p.x_bit)

    def third(self):
        p = self.p
        self.sends.arrived(4)
        block = self.b2.at[p.other_r].at[self.part]
        mine = self.b1.at[p.other_r, p.x_bit].at[self.part]
        block[...] = (block[...].astype(F32) + mine[...].astype(F32)).astype(BF)
        self.sends.start(6, block, self.b3, p.half)

    def pieces(self, target, sems):
        p = self.p
        self.sends.arrived(5, 6)
        copies = []
        for index, block in enumerate(
            (self.b2.at[p.r].at[self.part], self.b1.at[p.r, p.x_bit].at[self.part], self.b3)
        ):
            copies.append(
                pltpu.make_async_copy(block, target.at[index].at[self.part], sems.at[index])
            )
            copies[-1].start()
        return copies

    def end(self):
        self.sends.left()


def flat(block):
    return block.reshape(block.shape[0] * block.shape[1], block.shape[2])


def layer_kernel(
    x, cot, q_w, k_w, v_w, o_w, u_w, d_w, q_b, v_b, u_b, g1, b1, ob, g2, b2, db,
    o_out, o_gx, o_small, o_ga, o_gf, m_land,
    a_own, f_own, small, small_all, a_all, f_all, rows_all, c_all, normed, qkv, turned, mix, lse,
    out_s, part, part_m, from_y, from_z, relay_y, relay_z, m_relay_y, m_relay_z, act_s, dup_s, res, d_res,
    dm_s, dk_s, dv_s, f1, f2, f3, a1, a2, a3, sums, sv, rv, cols, cs, rcs, rt,
    x_ss, x_rs, s_ss, s_rs, a_ss, a_rs, f_ss, f_rs, c_ss, c_rs, p_ss, p_rs,
    n_ss, n_rs, d_ss, d_rs, e_ss, e_rs, r_ss, r_rs, m_ss, m_rs, fg_ss, fg_rs, ag_ss, ag_rs,
    v_ss, v_rs, t_ss, t_rs, l_sem, free_sem,
):
    p = Place()
    rows, width = x.shape
    feat = a_own.shape[0]
    per, hid = q_b.shape[0], u_b.shape[0]
    hidp = f_own.shape[1] // 2

    def pack():
        stack = jnp.concatenate([w[...].astype(F32) for w in (q_w, k_w, v_w, o_w)], axis=0).T
        a_own[...] = jnp.concatenate(
            [stack, jnp.zeros((feat, a_own.shape[1] - stack.shape[1]), F32)], axis=1
        ).astype(BF)
        small[...] = jnp.zeros_like(small)
        small[0:1, :per] = q_b[...].astype(F32).reshape(1, per)
        value_row = jnp.concatenate(
            [v_b[...].astype(F32).reshape(1, per), jnp.zeros((1, small.shape[1] - per), F32)], axis=1
        )
        small[0:1] += pltpu.roll(value_row, 2 * per, 1)
        small[1:2, :hid] = u_b[...].astype(F32).reshape(1, hid)
        for index, item in enumerate((g1, b1, ob, g2, b2, db)):
            small[2 + index : 3 + index, :per] = item[...].astype(F32).reshape(1, per)

    greet(
        [(p.gx, lax.rem(p.gy + d, 8)) for d in range(1, 8)]
        + [(lax.rem(p.gx + d, 4), p.gy) for d in range(1, 4)],
        pack,
    )
    gather = Gather(p, x, rows_all, x_ss, x_rs, CUT)
    gather.begin()
    parts = (pl.ds(0, feat // 2), pl.ds(feat // 2, feat // 2))
    mid = rows // 2
    halves = (pl.ds(0, mid), pl.ds(mid, mid))

    def gathers(send_sem, recv_sem):
        return [
            Gather(
                p, rows_all.at[p.t].at[half], rows_all.at[:, half], send_sem.at[i], recv_sem.at[i],
                HALF_CUT,
            )
            for i, half in enumerate(halves)
        ]

    def scatters(send_sem, recv_sem):
        long, short = mid - HALF_CUT, HALF_CUT
        return [
            Scatter(
                p, part.at[:, half], from_y.at[half], from_z.at[half],
                relay_y.at[pl.ds(long * i, long)], relay_z.at[pl.ds(short * i, short)],
                send_sem.at[i], recv_sem.at[i],
            )
            for i, half in enumerate(halves)
        ]

    attn_w = [
        Spread(p, a_own, a_all, a_ss.at[i], a_rs.at[i], l_sem.at[i], parts[i]) for i in range(2)
    ]
    for item in attn_w:
        item.begin()
    small_all[p.gy] = small[...]
    smalls = Sends(s_ss, s_rs)
    for d in range(1, 8):
        smalls.start(d - 1, small, small_all.at[p.gy], (p.gx, lax.rem(p.gy + d, 8)))
    for start, item in ((0, u_w), (hidp, d_w)):
        f_own[:, start + hidp - LANE : start + hidp] = jnp.zeros((feat, LANE), BF)
        f_own[:, start : start + hid] = item[...]
    feed_w = [
        Spread(p, f_own, f_all, f_ss.at[i], f_rs.at[i], l_sem.at[2 + i], parts[i])
        for i in range(2)
    ]
    cots = Gather(p, cot, c_all, c_ss, c_rs, CUT)
    c_all[p.t] = cot[...]
    smalls.arrived(*range(7))
    vec = jnp.zeros((8, width), F32)
    wide_per = -(-per // LANE) * LANE
    for g in range(8):
        vec = vec + spread(small_all[g][:, :wide_per], per * g, width)

    def norm(index, block):
        hat, _ = center_rows(block.astype(F32))
        normed[index] = (hat * vec[2:3] + vec[3:4]).astype(BF)

    norm(p.t, x[...])
    gather.forward()
    attn_w[0].second()
    attn_w[1].second()
    for item in feed_w:
        item.begin()
    gather.near()
    norm(p.ty, rows_all[p.ty])
    norm(p.tz, rows_all[p.tz])
    cots.begin()
    gather.far()
    norm(p.td, rows_all[p.td])
    for item in attn_w:
        item.third()
    for item in attn_w:
        item.done()

    def project(index, carry):
        block = normed[index]
        for group in range(2):
            bias = small_all[p.t + 4 * group, 0:1, :512]
            packed = nn(block, flat(a_all[group])[:, :512]) + bias
            for piece in range(6):
                qkv[piece // 2, 2 * group + piece % 2, pl.ds(index * rows, rows)] = lanes(
                    packed, HD * piece, LANE, HD
                ).astype(BF)
        return carry

    lax.fori_loop(0, 4, project, 0)
    for head in range(4):
        turned[head] = qkv[2, head].astype(F32).T.astype(BF)
    scatter = scatters(p_ss, p_rs)

    def attend(index):
        def one(head, carry):
            start = pl.multiple_of(index * rows, rows)
            scores = nt(qkv[1, head], qkv[0, head, pl.ds(start, rows)])
            top = jnp.max(scores, axis=0, keepdims=True)
            expo = jnp.exp2((scores - top) * (SCALE * LOG2E))
            total = jnp.sum(expo, axis=0, keepdims=True)
            mixed = nn(turned[head], expo.astype(BF)) / total
            out_s[head] = mixed.T
            lse[head, index] = jnp.broadcast_to(
                top * (SCALE * LOG2E) + jnp.log2(total), lse.shape[2:]
            )
            return carry

        lax.fori_loop(0, 4, one, 0)
        total = jnp.zeros((rows, width), F32)
        for group in range(2):
            both = (
                spread(out_s[2 * group], 48, 256) + spread(out_s[2 * group + 1], 48 + HD, 256)
            ).astype(BF)
            mix[group, pl.ds(pl.multiple_of(index * rows, rows), rows)] = both
            total = total + nt(both, flat(a_all[group])[:, 384:640])
        part[index] = total.astype(BF)

    gather.end()
    attend(p.td)
    for item in scatter:
        item.far()
    attend(p.ty)
    for item in scatter:
        item.near_y()
    attend(p.tz)
    for item in scatter:
        item.near_z()
    for item in scatter:
        item.relay()
    feed_w[0].second()
    cots.forward()
    attend(p.t)
    gather_n = gathers(n_ss, n_rs)
    for half, item, out in zip(halves, scatter, gather_n):
        residual = x[half].astype(F32) + item.total() + vec[4:5]
        res[half] = residual
        hat, _ = center_rows(residual.astype(BF).astype(F32))
        rows_all[p.t, half] = (hat * vec[5:6] + vec[6:7]).astype(BF)
        out.begin()
    for item in (*scatter, *attn_w):
        item.end()
    feed_w[1].second()
    for item in feed_w:
        item.third()
    for item in feed_w:
        item.done()
    scatter_d = scatters(d_ss, d_rs)
    cols[...] = jnp.zeros_like(cols)

    def feed(index):
        rows_two, rows_c = rows_all[index], c_all[index]
        out_m = jnp.zeros((rows, width), F32)
        out_d = jnp.zeros((rows, width), F32)
        for group in range(2):
            upper = (
                nn(rows_two, flat(f_all[group])[:, :hidp]) + small_all[p.t + 4 * group, 1:2, :hidp]
            )
            square = upper * upper
            tanh = jnp.tanh(ROOT * upper * (1.0 + 0.044715 * square))
            active = 0.5 * upper * (1.0 + tanh)
            slope = 0.5 * (1.0 + tanh) + 0.5 * upper * (1.0 - tanh * tanh) * (
                ROOT * (1.0 + 3.0 * 0.044715 * square)
            )
            act = active.astype(BF)
            act_s[group, index] = act
            dup = (nn(rows_c, flat(f_all[group])[:, hidp:]) * slope).astype(BF)
            dup_s[group, index] = dup
            cols[group : group + 1] += jnp.sum(dup.astype(F32), axis=0, keepdims=True)
            out_m = out_m + nt(act, flat(f_all[group])[:, hidp:])
            out_d = out_d + nt(dup, flat(f_all[group])[:, :hidp])
        part_m[index] = out_m.astype(BF)
        part[index] = out_d.astype(BF)

    gather_n[0].forward()
    feed(p.t)
    gather_n[1].forward()
    for item in gather_n:
        item.near()
    cots.near()
    feed(p.ty)
    for item in scatter_d:
        item.near_y()
    feed(p.tz)
    for item in scatter_d:
        item.near_z()
    for item in gather_n:
        item.far()
    cots.far()
    feed(p.td)
    for item in scatter_d:
        item.far()
    for item in feed_w:
        item.end()
    feed_g = [
        Reduce(p, f_all, f1, f2, f3, fg_ss.at[i], fg_rs.at[i], parts[i]) for i in range(2)
    ]

    def feed_grads(group):
        grad = tn(flat(rows_all[...]), flat(dup_s[group])).astype(BF)
        f_all[group, :, :, :hidp] = grad.reshape(4, feat, hidp)
        grad = tn(flat(c_all[...]), flat(act_s[group])).astype(BF)
        f_all[group, :, :, hidp:] = grad.reshape(4, feat, hidp)

    feed_grads(p.other_r)
    for item in feed_g:
        item.begin(0)
    for item in scatter_d:
        item.relay()
    scatter_m = Scatter(
        p, part_m, m_land.at[0], m_land.at[1], m_relay_y, m_relay_z, m_ss, m_rs
    )
    feed_grads(p.r)
    for item in feed_g:
        item.begin(1)
    for item in gather_n:
        item.end()
    cots.end()
    for peer in (p.near_y, p.near_z):
        pl.semaphore_signal(free_sem, inc=1, device_id=peer, device_id_type=MESH)
    for item in feed_g:
        item.second(0)
    sums[...] = jnp.zeros_like(sums)
    gather_e = gathers(e_ss, e_rs)
    for half, item, out in zip(halves, scatter_d, gather_e):
        grad = item.total()
        hat, inverse = center_rows(res[half].astype(BF).astype(F32))
        cot_f = cot[half].astype(F32)
        d_residual = cot_f + norm_back(grad, vec[5:6], hat, inverse)
        d_res[half] = d_residual
        rows_all[p.t, half] = d_residual.astype(BF)
        if out is gather_e[0]:
            pl.semaphore_wait(free_sem, 2)
        out.begin()
        sums[2:3] += jnp.sum(d_residual, axis=0, keepdims=True)
        sums[3:4] += jnp.sum(grad * hat, axis=0, keepdims=True)
        sums[4:5] += jnp.sum(grad, axis=0, keepdims=True)
        sums[5:6] += jnp.sum(cot_f, axis=0, keepdims=True)
    for item in feed_g:
        item.second(1)
    for item in scatter_d:
        item.end()
    for head in range(4):
        turned[head] = qkv[1, head].astype(F32).T.astype(BF)
    dk_s[...] = jnp.zeros_like(dk_s)
    dv_s[...] = jnp.zeros_like(dv_s)

    def attend_back(index):
        block = rows_all[index]
        for group in range(2):
            mixed = nn(block, flat(a_all[group])[:, 384:640])
            dm_s[2 * group] = lanes(mixed, 48, LANE, HD).astype(BF)
            dm_s[2 * group + 1] = lanes(mixed, 48 + HD, LANE, HD).astype(BF)

        def one(head, carry):
            start = pl.multiple_of(index * rows, rows)
            q_rows, d_mix = qkv[0, head, pl.ds(start, rows)], dm_s[head]
            scores = nt(qkv[1, head], q_rows)
            probs = jnp.exp2(scores * (SCALE * LOG2E) - lse[head, index, 0:1])
            d_probs = nt(qkv[2, head], d_mix)
            delta = jnp.sum(d_probs * probs, axis=0, keepdims=True)
            d_scores = (probs * (d_probs - delta)).astype(BF)
            dv_s[head] += nn(probs.astype(BF), d_mix)
            dk_s[head] += nn(d_scores, q_rows)
            out_s[head] = nn(turned[head], d_scores).T * SCALE
            return carry

        lax.fori_loop(0, 4, one, 0)
        for head in range(4):
            place = LANE * (head % 2)
            dup_s[head // 2, index, :, place : place + LANE] = out_s[head].astype(BF)

    gather_e[0].forward()
    attend_back(p.t)
    gather_e[1].forward()
    for item in feed_g:
        item.third()
    for item in gather_e:
        item.near()
    attend_back(p.ty)
    scatter_m.far()
    scatter_m.near_y()
    scatter_m.near_z()
    attend_back(p.tz)
    for item in gather_e:
        item.far()
    attend_back(p.td)
    scatter_n = scatters(r_ss, r_rs)
    cs[...] = jnp.zeros_like(cs)

    def give(index):
        here = pl.ds(pl.multiple_of(index * rows, rows), rows)
        total = jnp.zeros((rows, width), F32)
        for group in range(2):
            packed = jnp.zeros((rows, 512), F32)
            for piece in range(6):
                head = 2 * group + piece % 2
                if piece < 2:
                    value = dup_s[group, index, :, LANE * piece : LANE * (piece + 1)].astype(F32)
                elif piece < 4:
                    value = dk_s[head, here] * SCALE
                else:
                    value = dv_s[head, here]
                packed = packed + spread(value, HD * piece, 512)
            packed = packed.astype(BF)
            act_s[group, index, :, :512] = packed
            cs[group, 0:1, :512] += jnp.sum(packed.astype(F32), axis=0, keepdims=True)
            total = total + nt(packed, flat(a_all[group])[:, :512])
        part[index] = total.astype(BF)
        sums[0:1] += jnp.sum(total * normed[index].astype(F32), axis=0, keepdims=True)
        sums[1:2] += jnp.sum(total, axis=0, keepdims=True)

    give(p.td)
    for item in scatter_n:
        item.far()
    give(p.ty)
    for item in scatter_n:
        item.near_y()
    give(p.tz)
    for item in scatter_n:
        item.near_z()
    give(p.t)
    scatter_m.relay()
    sums[0:1] = (sums[0:1] - vec[3:4] * sums[1:2]) / vec[2:3]
    all_sums = sums[...]
    for g in range(8):
        sv[g] = lanes(all_sums, per * g, sv.shape[2], per)
    for group in range(2):
        cs[group, 1:2] = cols[group : group + 1]
    slices = Sends(v_ss, v_rs)
    for d in range(1, 8):
        other = lax.rem(p.gy + d, 8)
        slices.start(d - 1, sv.at[other], rv.at[p.gy], (p.gx, other))
    slices.start(7, cs.at[p.other_r], rcs, p.half)
    rv[p.gy] = sv[p.gy]
    attn_g = [
        Reduce(p, a_all, a1, a2, a3, ag_ss.at[i], ag_rs.at[i], parts[i]) for i in range(2)
    ]

    def attn_grads(group):
        main = tn(flat(normed[...]), flat(act_s[group])[:, :512])
        outer = tn(flat(rows_all[...]), mix[group])
        both = jnp.concatenate(
            [main[:, :384], main[:, 384:] + outer[:, :128], outer[:, 128:]], axis=1
        )
        a_all[group] = both.astype(BF).reshape(4, feat, 640)

    attn_grads(p.other_r)
    for item in attn_g:
        item.begin(0)
    for item in scatter_n:
        item.relay()
    attn_grads(p.r)
    for item in attn_g:
        item.begin(1)
    for item in attn_g:
        item.second(0)
    for item in attn_g:
        item.second(1)
    slices.arrived(*range(8))
    total = rv[0]
    for g in range(1, 8):
        total = total + rv[g]
    mine = rt.at[p.gx]
    mine[0:8] = jnp.concatenate(
        [total, jnp.zeros((8, rt.shape[2] - total.shape[1]), F32)], axis=1
    )
    mine[8:16] = cs[p.r] + rcs[...]
    totals = Sends(t_ss, t_rs)
    for d in range(1, 4):
        totals.start(d - 1, mine, mine, (lax.rem(p.gx + d, 4), p.gy))
    copies = []
    for i in range(2):
        copies += feed_g[i].pieces(o_gf, l_sem.at[pl.ds(4 + 3 * i, 3)])
    for item in attn_g:
        item.third()
    scatter_m.sends.arrived(2, 3, 4, 5)
    moves = [
        pltpu.make_async_copy(m_land.at[i], c_all.at[i], l_sem.at[16 + i]) for i in range(2)
    ]
    for move in moves:
        move.start()
    for half, item in zip(halves, scatter_n):
        grad = item.total()
        hat, inverse = center_rows(x[half].astype(F32))
        o_gx[half] = (d_res[half] + norm_back(grad, vec[2:3], hat, inverse)).astype(BF)
    totals.arrived(0, 1, 2)
    o_small[...] = rt[0] + rt[1] + rt[2] + rt[3]
    for move in moves:
        move.wait()
    addend = part_m[p.t].astype(F32) + c_all[0].astype(F32) + c_all[1].astype(F32)
    o_out[...] = (res[...] + addend + vec[7:8]).astype(BF)
    for i in range(2):
        copies += attn_g[i].pieces(o_ga, l_sem.at[pl.ds(10 + 3 * i, 3)])
    for copy in copies:
        copy.wait()
    for item in (smalls, slices, totals):
        item.left()
    for item in (*gather_e, *feed_g, *attn_g, *scatter_n, scatter_m):
        item.end()


VM = pl.BlockSpec(memory_space=pltpu.VMEM)
ANY = pl.BlockSpec(memory_space=pl.ANY)


def dma(shape):
    return pltpu.SemaphoreType.DMA(shape)


def finish_kernel(
    out, gx, ga, gf, small,
    o_out, o_gx, o_g1, o_b1, o_q, o_qb, o_k, o_v, o_vb, o_o, o_ob, o_g2, o_b2, o_u, o_ub, o_d, o_db,
):
    per, hid = o_g1.shape[0], o_ub.shape[0]
    hidp = gf.shape[2] // 2
    o_out[...] = out[...]
    o_gx[...] = gx[...]
    stack = (ga[0].astype(F32) + ga[1].astype(F32) + ga[2].astype(F32)).T
    for index, item in enumerate((o_q, o_k, o_v, o_o)):
        item[...] = stack[per * index : per * (index + 1)]
    grads = gf[0].astype(F32) + gf[1].astype(F32) + gf[2].astype(F32)
    o_u[...] = grads[:, :hid]
    o_d[...] = grads[:, hidp : hidp + hid]
    for index, item in enumerate((o_g1, o_b1, o_ob, o_g2, o_b2, o_db)):
        item[...] = small[index : index + 1, :per].reshape(per)
    o_qb[...] = small[8:9, :per].reshape(per)
    o_vb[...] = pltpu.roll(small[8:9], small.shape[1] - 2 * per, 1)[:, :per].reshape(per)
    o_ub[...] = small[9:10, :hid].reshape(hid)


def fast_shards(
    layer_input, norm_one_gain, norm_one_bias, query_weight, query_bias, key_weight, value_weight,
    value_bias, output_weight, output_bias, norm_two_gain, norm_two_bias, up_weight, up_bias,
    down_weight, down_bias, cotangent,
):
    rows, width = layer_input.shape
    per, hid = query_weight.shape[1], up_weight.shape[1]
    feat = query_weight.shape[0]
    hidp = -(-hid // LANE) * LANE
    aw = 640
    shape, bf, f32 = jax.ShapeDtypeStruct, BF, F32
    params = lambda number: pltpu.CompilerParams(
        collective_id=number, has_side_effects=True, vmem_limit_bytes=VMEM_LIMIT
    )
    full = (rows, width)
    block4 = pltpu.VMEM((4, rows, width), bf)

    wide = -(-per // LANE) * LANE
    block = pltpu.VMEM(full, bf)
    hidden = pltpu.VMEM((2, 4, rows, hidp), bf)
    heads = pltpu.VMEM((4, 4 * rows, LANE), f32)
    six, seven, sixes, sevens = dma((6,)), dma((7,)), dma((2, 6)), dma((2, 7))
    (out, grad_input, smalls, ga, gfo, _) = pl.pallas_call(
        layer_kernel,
        name="layer",
        out_shape=[
            shape(full, bf), shape(full, bf), shape((16, aw), f32), shape((3, feat, aw), bf),
            shape((3, feat, 2 * hidp), bf), shape((2, rows, width), bf),
        ],
        in_specs=[VM] * 17,
        out_specs=[VM] * 3 + [ANY] * 3,
        scratch_shapes=[
            pltpu.VMEM((feat, aw), bf), pltpu.VMEM((feat, 2 * hidp), bf), pltpu.VMEM((8, aw), f32),
            pltpu.VMEM((8, 8, aw), f32), pltpu.VMEM((2, 4, feat, aw), bf),
            pltpu.VMEM((2, 4, feat, 2 * hidp), bf), block4, block4, block4,
            pltpu.VMEM((3, 4, 4 * rows, LANE), bf), pltpu.VMEM((4, LANE, 4 * rows), bf),
            pltpu.VMEM((2, 4 * rows, 256), bf), pltpu.VMEM((4, 4, 8, rows), f32),
            pltpu.VMEM((4, rows, LANE), f32), block4, block4, block, block,
            pltpu.VMEM((rows - 2 * HALF_CUT, width), bf), pltpu.VMEM((2 * HALF_CUT, width), bf),
            pltpu.VMEM((rows - CUT, width), bf), pltpu.VMEM((CUT, width), bf),
            hidden, hidden, pltpu.VMEM(full, f32), pltpu.VMEM(full, f32),
            pltpu.VMEM((4, rows, LANE), bf), heads, heads,
            pltpu.VMEM((2, 2, feat, 2 * hidp), bf), pltpu.VMEM((2, feat, 2 * hidp), bf),
            pltpu.VMEM((feat, 2 * hidp), bf), pltpu.VMEM((2, 2, feat, aw), bf),
            pltpu.VMEM((2, feat, aw), bf), pltpu.VMEM((feat, aw), bf),
            pltpu.VMEM((8, width), f32), pltpu.VMEM((8, 8, wide), f32),
            pltpu.VMEM((8, 8, wide), f32), pltpu.VMEM((8, hidp), f32), pltpu.VMEM((2, 8, aw), f32),
            pltpu.VMEM((8, aw), f32), pltpu.VMEM((4, 16, aw), f32),
            six, six, seven, seven, sevens, sevens, sevens, sevens, six, six,
            sixes, sixes, sixes, sixes, sixes, sixes, sixes, sixes, sixes, sixes, six, six,
            sevens, sevens, sevens, sevens,
            dma((8,)), dma((8,)), dma((3,)), dma((3,)), dma((18,)), pltpu.SemaphoreType.REGULAR,
        ],
        compiler_params=params(0),
    )(
        layer_input, cotangent, query_weight.T, key_weight.T, value_weight.T, output_weight,
        up_weight, down_weight.T, query_bias, value_bias, up_bias, norm_one_gain, norm_one_bias,
        output_bias, norm_two_gain, norm_two_bias, down_bias,
    )
    line = shape((per,), f32)
    turned = shape((per, feat), f32)
    done = pl.pallas_call(
        finish_kernel,
        name="finish",
        out_shape=[
            shape(full, bf), shape(full, bf), line, line, turned, line, turned, turned, line,
            turned, line, line, line, shape((feat, hid), f32), shape((hid,), f32),
            shape((feat, hid), f32), line,
        ],
        in_specs=[VM] * 5,
        out_specs=[VM] * 17,
        compiler_params=pltpu.CompilerParams(vmem_limit_bytes=VMEM_LIMIT),
    )(out, grad_input, ga, gfo, smalls)
    done = list(done)
    for index in (4, 6, 7, 15):
        done[index] = done[index].T
    return tuple(done)


def dot_plain(left, right):
    return jnp.dot(left, right, preferred_element_type=jnp.float32)


def dot_right_t(left, right):
    return lax.dot_general(
        left, right, (((1,), (1,)), ((), ())), preferred_element_type=jnp.float32
    )


def dot_left_t(left, right):
    return lax.dot_general(
        left, right, (((0,), (0,)), ((), ())), preferred_element_type=jnp.float32
    )


def normalize(rows):
    center = rows - jnp.mean(rows, axis=-1, keepdims=True)
    inverse = lax.rsqrt(jnp.mean(center * center, axis=-1, keepdims=True) + 1e-06)
    return (center * inverse, inverse)


def gelu_tanh(value):
    return jax.nn.gelu(value, approximate=True)


def image_shape(array):
    heads = array.shape[1] // HD
    return (array.shape[0] // LENGTH, LENGTH, heads, HD)


def attend(query, key, value):
    shape = image_shape(query)
    scale = HD ** (-0.5)

    def one_image(carry, pieces):
        q_img, k_img, v_img = pieces
        scores = (
            jnp.einsum("qhd,khd->hqk", q_img, k_img, preferred_element_type=jnp.float32) * scale
        )
        top = jnp.max(scores, axis=-1, keepdims=True)
        expo = jnp.exp(scores - top)
        total = jnp.sum(expo, axis=-1, keepdims=True)
        probs = (expo / total).astype(jnp.bfloat16)
        mixed = jnp.einsum("hqk,khd->qhd", probs, v_img, preferred_element_type=jnp.float32).astype(
            jnp.bfloat16
        )
        return (carry, (mixed, (top + jnp.log(total))[..., 0]))

    _, (mixed, lse) = lax.scan(
        one_image, 0, (query.reshape(shape), key.reshape(shape), value.reshape(shape))
    )
    return (mixed.reshape(query.shape), lse)


def attend_back(query, key, value, lse, d_mixed):
    shape = image_shape(query)
    scale = HD ** (-0.5)

    def one_image(carry, pieces):
        q_img, k_img, v_img, lse_img, dm_img = pieces
        scores = (
            jnp.einsum("qhd,khd->hqk", q_img, k_img, preferred_element_type=jnp.float32) * scale
        )
        probs = jnp.exp(scores - lse_img[..., None])
        d_probs = jnp.einsum("qhd,khd->hqk", dm_img, v_img, preferred_element_type=jnp.float32)
        d_scores = (probs * (d_probs - jnp.sum(d_probs * probs, axis=-1, keepdims=True))).astype(
            jnp.bfloat16
        )
        d_value = jnp.einsum(
            "hqk,qhd->khd", probs.astype(jnp.bfloat16), dm_img, preferred_element_type=jnp.float32
        ).astype(jnp.bfloat16)
        d_query = (
            jnp.einsum("hqk,khd->qhd", d_scores, k_img, preferred_element_type=jnp.float32) * scale
        ).astype(jnp.bfloat16)
        d_key = (
            jnp.einsum("hqk,qhd->khd", d_scores, q_img, preferred_element_type=jnp.float32) * scale
        ).astype(jnp.bfloat16)
        return (carry, (d_query, d_key, d_value))

    _, (d_query, d_key, d_value) = lax.scan(
        one_image,
        0,
        (
            query.reshape(shape),
            key.reshape(shape),
            value.reshape(shape),
            lse,
            d_mixed.reshape(shape),
        ),
    )
    return (d_query.reshape(query.shape), d_key.reshape(query.shape), d_value.reshape(query.shape))


def forward_pass(
    layer_input,
    norm_one_gain,
    norm_one_bias,
    query_weight,
    query_bias,
    key_weight,
    value_weight,
    value_bias,
    output_weight,
    output_bias,
    norm_two_gain,
    norm_two_bias,
    up_weight,
    up_bias,
    down_weight,
    down_bias,
):
    w_query, w_key, w_value, w_output, w_up, w_down = (
        lax.all_gather(query_weight, "gx", axis=0, tiled=True),
        lax.all_gather(key_weight, "gx", axis=0, tiled=True),
        lax.all_gather(value_weight, "gx", axis=0, tiled=True),
        lax.all_gather(output_weight, "gx", axis=1, tiled=True),
        lax.all_gather(up_weight, "gx", axis=0, tiled=True),
        lax.all_gather(down_weight, "gx", axis=1, tiled=True),
    )
    rows_one, gain_one, shift_one, out_shift, down_shift = (
        lax.all_gather(layer_input, "gy", axis=0, tiled=True),
        lax.all_gather(norm_one_gain, "gy", axis=0, tiled=True),
        lax.all_gather(norm_one_bias, "gy", axis=0, tiled=True),
        lax.all_gather(output_bias, "gy", axis=0, tiled=True),
        lax.all_gather(down_bias, "gy", axis=0, tiled=True),
    )
    hat_one, inv_one = normalize(rows_one.astype(jnp.float32))
    normed = (hat_one * gain_one.astype(jnp.float32) + shift_one.astype(jnp.float32)).astype(
        jnp.bfloat16
    )
    query = (dot_plain(normed, w_query) + query_bias.astype(jnp.float32)).astype(jnp.bfloat16)
    key = dot_plain(normed, w_key).astype(jnp.bfloat16)
    value = (dot_plain(normed, w_value) + value_bias.astype(jnp.float32)).astype(jnp.bfloat16)
    mixed, lse = attend(query, key, value)
    attn_part = lax.psum_scatter(
        dot_plain(mixed, w_output).astype(jnp.bfloat16), "gy", scatter_dimension=0, tiled=True
    ).astype(jnp.float32)
    residual = layer_input.astype(jnp.float32) + attn_part + out_shift.astype(jnp.float32)
    rows_two, gain_two, shift_two = (
        lax.all_gather(residual.astype(jnp.bfloat16), "gy", axis=0, tiled=True),
        lax.all_gather(norm_two_gain, "gy", axis=0, tiled=True),
        lax.all_gather(norm_two_bias, "gy", axis=0, tiled=True),
    )
    hat_two, inv_two = normalize(rows_two.astype(jnp.float32))
    normed_two = (hat_two * gain_two.astype(jnp.float32) + shift_two.astype(jnp.float32)).astype(
        jnp.bfloat16
    )
    upper = dot_plain(normed_two, w_up) + up_bias.astype(jnp.float32)
    active = gelu_tanh(upper).astype(jnp.bfloat16)
    mlp_part = lax.psum_scatter(
        dot_plain(active, w_down).astype(jnp.bfloat16), "gy", scatter_dimension=0, tiled=True
    ).astype(jnp.float32)
    result = (residual + mlp_part + down_shift.astype(jnp.float32)).astype(jnp.bfloat16)
    saved = (
        w_query,
        w_key,
        w_value,
        w_output,
        w_up,
        w_down,
        hat_one,
        inv_one,
        normed,
        query,
        key,
        value,
        mixed,
        lse,
        hat_two,
        inv_two,
        normed_two,
        upper,
        active,
        gain_one,
        gain_two,
    )
    return saved, result


def shards(
    layer_input,
    norm_one_gain,
    norm_one_bias,
    query_weight,
    query_bias,
    key_weight,
    value_weight,
    value_bias,
    output_weight,
    output_bias,
    norm_two_gain,
    norm_two_bias,
    up_weight,
    up_bias,
    down_weight,
    down_bias,
    cotangent,
):
    inputs = (
        layer_input,
        norm_one_gain,
        norm_one_bias,
        query_weight,
        query_bias,
        key_weight,
        value_weight,
        value_bias,
        output_weight,
        output_bias,
        norm_two_gain,
        norm_two_bias,
        up_weight,
        up_bias,
        down_weight,
        down_bias,
    )
    saved, layer_output = forward_pass(*inputs)
    (
        w_query,
        w_key,
        w_value,
        w_output,
        w_up,
        w_down,
        hat_one,
        inv_one,
        normed,
        query,
        key,
        value,
        mixed,
        lse,
        hat_two,
        inv_two,
        normed_two,
        upper,
        active,
        gain_one,
        gain_two,
    ) = saved
    local = layer_input.shape[0]
    start = lax.axis_index("gy") * local
    grad_rows = lax.all_gather(cotangent, "gy", axis=0, tiled=True)
    d_active = dot_right_t(grad_rows, w_down)
    _, gelu_pull = jax.vjp(gelu_tanh, upper)
    d_upper = gelu_pull(d_active)[0].astype(jnp.bfloat16)
    grad_up_weight, grad_down_weight = (
        lax.psum_scatter(
            dot_left_t(normed_two, d_upper).astype(jnp.bfloat16),
            "gx",
            scatter_dimension=0,
            tiled=True,
        ).astype(jnp.float32),
        lax.psum_scatter(
            dot_left_t(active, grad_rows).astype(jnp.bfloat16),
            "gx",
            scatter_dimension=1,
            tiled=True,
        ).astype(jnp.float32),
    )
    d_normed_two = lax.psum_scatter(
        dot_right_t(d_upper, w_up).astype(jnp.bfloat16), "gy", scatter_dimension=0, tiled=True
    ).astype(jnp.float32)
    hat_two_local = lax.dynamic_slice_in_dim(hat_two, start, local, 0)
    inv_two_local = lax.dynamic_slice_in_dim(inv_two, start, local, 0)
    scaled_two = d_normed_two * gain_two.astype(jnp.float32)
    mean_two = jnp.mean(scaled_two, axis=-1, keepdims=True)
    proj_two = jnp.mean(scaled_two * hat_two_local, axis=-1, keepdims=True)
    cot_float = cotangent.astype(jnp.float32)
    d_residual = cot_float + inv_two_local * (scaled_two - mean_two - hat_two_local * proj_two)
    part_two_gain = jnp.sum(d_normed_two * hat_two_local, axis=0)
    part_two_bias = jnp.sum(d_normed_two, axis=0)
    part_up_bias = jnp.sum(d_upper.astype(jnp.float32), axis=0)
    part_down_bias = jnp.sum(cot_float, axis=0)
    grad_attn = lax.all_gather(d_residual.astype(jnp.bfloat16), "gy", axis=0, tiled=True)
    part_output_bias = jnp.sum(d_residual, axis=0)
    d_mixed = dot_right_t(grad_attn, w_output).astype(jnp.bfloat16)
    d_query, d_key, d_value = attend_back(query, key, value, lse, d_mixed)
    grad_query_weight, grad_key_weight, grad_value_weight, grad_output_weight = (
        lax.psum_scatter(
            dot_left_t(normed, d_query).astype(jnp.bfloat16), "gx", scatter_dimension=0, tiled=True
        ).astype(jnp.float32),
        lax.psum_scatter(
            dot_left_t(normed, d_key).astype(jnp.bfloat16), "gx", scatter_dimension=0, tiled=True
        ).astype(jnp.float32),
        lax.psum_scatter(
            dot_left_t(normed, d_value).astype(jnp.bfloat16), "gx", scatter_dimension=0, tiled=True
        ).astype(jnp.float32),
        lax.psum_scatter(
            dot_left_t(mixed, grad_attn).astype(jnp.bfloat16), "gx", scatter_dimension=1, tiled=True
        ).astype(jnp.float32),
    )
    d_normed = lax.psum_scatter(
        (
            dot_right_t(d_query, w_query)
            + dot_right_t(d_key, w_key)
            + dot_right_t(d_value, w_value)
        ).astype(jnp.bfloat16),
        "gy",
        scatter_dimension=0,
        tiled=True,
    ).astype(jnp.float32)
    hat_one_local = lax.dynamic_slice_in_dim(hat_one, start, local, 0)
    inv_one_local = lax.dynamic_slice_in_dim(inv_one, start, local, 0)
    scaled_one = d_normed * gain_one.astype(jnp.float32)
    mean_one = jnp.mean(scaled_one, axis=-1, keepdims=True)
    proj_one = jnp.mean(scaled_one * hat_one_local, axis=-1, keepdims=True)
    grad_input = (
        d_residual + inv_one_local * (scaled_one - mean_one - hat_one_local * proj_one)
    ).astype(jnp.bfloat16)
    part_one_gain = jnp.sum(d_normed * hat_one_local, axis=0)
    part_one_bias = jnp.sum(d_normed, axis=0)
    part_query_bias = jnp.sum(d_query.astype(jnp.float32), axis=0)
    part_value_bias = jnp.sum(d_value.astype(jnp.float32), axis=0)
    feat_one_gain, feat_one_bias, feat_output_bias, feat_two_gain, feat_two_bias, feat_down_bias = (
        lax.psum_scatter(part_one_gain, "gy", scatter_dimension=0, tiled=True),
        lax.psum_scatter(part_one_bias, "gy", scatter_dimension=0, tiled=True),
        lax.psum_scatter(part_output_bias, "gy", scatter_dimension=0, tiled=True),
        lax.psum_scatter(part_two_gain, "gy", scatter_dimension=0, tiled=True),
        lax.psum_scatter(part_two_bias, "gy", scatter_dimension=0, tiled=True),
        lax.psum_scatter(part_down_bias, "gy", scatter_dimension=0, tiled=True),
    )
    (
        grad_one_gain,
        grad_one_bias,
        grad_query_bias,
        grad_value_bias,
        grad_output_bias,
        grad_two_gain,
        grad_two_bias,
        grad_up_bias,
        grad_down_bias,
    ) = lax.psum(
        (
            feat_one_gain,
            feat_one_bias,
            part_query_bias,
            part_value_bias,
            feat_output_bias,
            feat_two_gain,
            feat_two_bias,
            part_up_bias,
            feat_down_bias,
        ),
        "gx",
    )
    return (
        layer_output,
        grad_input,
        grad_one_gain,
        grad_one_bias,
        grad_query_weight,
        grad_query_bias,
        grad_key_weight,
        grad_value_weight,
        grad_value_bias,
        grad_output_weight,
        grad_output_bias,
        grad_two_gain,
        grad_two_bias,
        grad_up_weight,
        grad_up_bias,
        grad_down_weight,
        grad_down_bias,
    )


def solution(mesh):
    fits = mesh.shape["gx"] == 4 and mesh.shape["gy"] == 8
    return jax.shard_map(
        fast_shards if fits else shards,
        mesh=mesh,
        in_specs=(
            P(("gx", "gy"), None),
            P("gy"),
            P("gy"),
            P("gx", "gy"),
            P("gy"),
            P("gx", "gy"),
            P("gx", "gy"),
            P("gy"),
            P("gy", "gx"),
            P("gy"),
            P("gy"),
            P("gy"),
            P("gx", "gy"),
            P("gy"),
            P("gy", "gx"),
            P("gy"),
            P(("gx", "gy"), None),
        ),
        out_specs=(
            P(("gx", "gy"), None),
            P(("gx", "gy"), None),
            P("gy"),
            P("gy"),
            P("gx", "gy"),
            P("gy"),
            P("gx", "gy"),
            P("gx", "gy"),
            P("gy"),
            P("gy", "gx"),
            P("gy"),
            P("gy"),
            P("gy"),
            P("gx", "gy"),
            P("gy"),
            P("gy", "gx"),
            P("gy"),
        ),
        check_vma=False,
    )
```

```python
import functools
import math

import jax
import jax.numpy as jnp
from jax import lax
from jax.experimental import pallas as pl
from jax.experimental.pallas import tpu as pltpu
from jax.sharding import PartitionSpec as P

HD = 72
LENGTH = 1024
LANE = 128
BF = jnp.bfloat16
F32 = jnp.float32
MESH = pl.DeviceIdType.MESH
TP = 4
VMEM_LIMIT = 63 << 20
SCALE = HD ** (-0.5)
CUT = 80
HALF_CUT = 48
LOG2E = 1.4426950408889634
ROOT = math.sqrt(2.0 / math.pi)


def nn(left, right):
    return jnp.dot(left, right, preferred_element_type=F32)


def nt(left, right):
    return lax.dot_general(left, right, (((1,), (1,)), ((), ())), preferred_element_type=F32)


def tn(left, right):
    return lax.dot_general(left, right, (((0,), (0,)), ((), ())), preferred_element_type=F32)


def center_rows(rows):
    center = rows - jnp.mean(rows, axis=-1, keepdims=True)
    inverse = lax.rsqrt(jnp.mean(center * center, axis=-1, keepdims=True) + 1e-06)
    return center * inverse, inverse


def norm_back(grad, gain, hat, inverse):
    scaled = grad * gain
    mean = jnp.mean(scaled, axis=-1, keepdims=True)
    proj = jnp.mean(scaled * hat, axis=-1, keepdims=True)
    return inverse * (scaled - mean - hat * proj)


def lanes(value, start, width, keep):
    full = value.shape[1]
    moved = value if start == 0 else pltpu.roll(value, full - start, 1)
    part = moved[:, :width]
    return jnp.where(lax.broadcasted_iota(jnp.int32, part.shape, 1) < keep, part, 0.0)


def spread(value, start, full):
    wide = jnp.concatenate([value, jnp.zeros((value.shape[0], full - value.shape[1]), F32)], axis=1)
    return wide if start == 0 else pltpu.roll(wide, start, 1)


class Place:
    def __init__(self):
        gx, gy = lax.axis_index("gx"), lax.axis_index("gy")
        self.gx, self.gy = gx, gy
        self.t, self.r = lax.rem(gy, 4), lax.div(gy, 4)
        y, z = lax.rem(gy, 2), lax.rem(lax.div(gy, 2), 2)
        self.ty = self.t + 1 - 2 * y
        self.tz = self.t + 2 - 4 * z
        self.td = 3 - self.t
        base = 4 * self.r
        self.near_y = (gx, base + self.ty)
        self.near_z = (gx, base + self.tz)
        self.other_r = 1 - self.r
        self.half = (gx, lax.rem(gy + 4, 8))
        self.core_bit, self.x_bit = lax.rem(gx, 2), lax.div(gx, 2)
        self.gx_core = gx + 1 - 2 * self.core_bit
        self.gx_x = lax.rem(gx + 2, 4)
        self.core = (self.gx_core, gy)
        self.chip_x = (self.gx_x, gy)


def greet(peers, meanwhile):
    barrier = pltpu.get_barrier_semaphore()
    for peer in peers:
        pl.semaphore_signal(barrier, inc=1, device_id=peer, device_id_type=MESH)
    meanwhile()
    pl.semaphore_wait(barrier, len(peers))


class Sends:
    def __init__(self, send_sem, recv_sem):
        self.send_sem, self.recv_sem, self.copies = send_sem, recv_sem, {}

    def start(self, index, source, target, peer):
        copy = pltpu.make_async_remote_copy(
            src_ref=source,
            dst_ref=target,
            send_sem=self.send_sem.at[index],
            recv_sem=self.recv_sem.at[index],
            device_id=peer,
            device_id_type=MESH,
        )
        copy.start()
        self.copies[index] = copy

    def arrived(self, *indices):
        for index in indices:
            self.copies[index].wait_recv()

    def left(self):
        for copy in self.copies.values():
            copy.wait_send()


class Gather:
    def __init__(self, place, source, target, send_sem, recv_sem, cut):
        self.p, self.dst = place, target
        self.sends = Sends(send_sem, recv_sem)
        self.lo, self.hi = pl.ds(0, cut), pl.ds(cut, source.shape[0] - cut)
        self.src = source

    def begin(self):
        p, own = self.p, self.dst.at[self.p.t]
        for index, part, peer in (
            (0, self.lo, p.near_y),
            (2, self.hi, p.near_z),
            (1, self.hi, p.near_y),
            (3, self.lo, p.near_z),
        ):
            self.sends.start(index, self.src.at[part], own.at[part], peer)

    def forward(self):
        p = self.p
        self.sends.arrived(0)
        block = self.dst.at[p.ty].at[self.lo]
        self.sends.start(4, block, block, p.near_z)
        self.sends.arrived(2)
        block = self.dst.at[p.tz].at[self.hi]
        self.sends.start(5, block, block, p.near_y)

    def near(self):
        self.sends.arrived(1, 3)

    def far(self):
        self.sends.arrived(4, 5)

    def end(self):
        self.sends.left()


class Scatter:
    def __init__(self, place, part, from_y, from_z, relay_y, relay_z, send_sem, recv_sem):
        self.p, self.part = place, part
        self.from_y, self.from_z, self.relay_y, self.relay_z = from_y, from_z, relay_y, relay_z
        self.sends = Sends(send_sem, recv_sem)
        cut = relay_y.shape[0]
        self.cut = cut
        self.lo, self.hi = pl.ds(0, cut), pl.ds(cut, relay_z.shape[0])

    def far(self):
        p, block = self.p, self.part.at[self.p.td]
        self.sends.start(0, block.at[self.lo], self.relay_y, p.near_y)
        self.sends.start(1, block.at[self.hi], self.relay_z, p.near_z)

    def near_y(self):
        p = self.p
        self.sends.start(2, self.part.at[p.ty].at[self.lo], self.from_y.at[self.lo], p.near_y)

    def near_z(self):
        p = self.p
        self.sends.start(3, self.part.at[p.tz].at[self.hi], self.from_z.at[self.hi], p.near_z)

    def relay(self):
        p, cut = self.p, self.cut
        self.sends.arrived(0)
        block = self.part.at[p.tz]
        block[:cut] = (block[:cut].astype(F32) + self.relay_y[...].astype(F32)).astype(BF)
        self.sends.start(4, block.at[self.lo], self.from_z.at[self.lo], p.near_z)
        self.sends.arrived(1)
        block = self.part.at[p.ty]
        block[cut:] = (block[cut:].astype(F32) + self.relay_z[...].astype(F32)).astype(BF)
        self.sends.start(5, block.at[self.hi], self.from_y.at[self.hi], p.near_y)

    def total(self):
        self.sends.arrived(2, 3, 4, 5)
        own = self.part[self.p.t].astype(F32)
        return own + self.from_y[...].astype(F32) + self.from_z[...].astype(F32)

    def end(self):
        self.sends.left()


class Spread:
    def __init__(self, place, source, target, send_sem, recv_sem, local_sem, part):
        self.p, self.part = place, part
        self.src, self.dst = source.at[part], target
        self.sends = Sends(send_sem, recv_sem)
        self.local = pltpu.make_async_copy(
            self.src, target.at[place.r, place.gx].at[part], local_sem
        )

    def slot(self, group, column):
        return self.dst.at[group, column].at[self.part]

    def begin(self):
        p = self.p
        slot = self.slot(p.r, p.gx)
        self.sends.start(0, self.src, slot, p.half)
        self.sends.start(1, self.src, slot, p.chip_x)
        self.sends.start(2, self.src, slot, p.core)
        self.local.start()

    def second(self):
        p = self.p
        self.sends.arrived(0)
        slot = self.slot(p.other_r, p.gx)
        self.sends.start(3, slot, slot, p.chip_x)
        self.sends.start(4, slot, slot, p.core)

    def third(self):
        p = self.p
        self.sends.arrived(1)
        slot = self.slot(p.r, p.gx_x)
        self.sends.start(5, slot, slot, p.core)
        self.sends.arrived(3)
        slot = self.slot(p.other_r, p.gx_x)
        self.sends.start(6, slot, slot, p.core)

    def done(self):
        self.sends.arrived(2, 4, 5, 6)
        self.local.wait()

    def end(self):
        self.sends.left()


class Reduce:
    def __init__(self, place, source, first, second, third, send_sem, recv_sem, part):
        self.p, self.part = place, part
        self.src, self.b1, self.b2, self.b3 = source, first, second, third.at[part]
        self.sends = Sends(send_sem, recv_sem)

    def begin(self, late):
        p = self.p
        group = p.r if late else p.other_r
        for index, side in ((2 * late, 1 - p.x_bit), (2 * late + 1, p.x_bit)):
            block = self.src.at[group, 2 * side + 1 - p.core_bit].at[self.part]
            self.sends.start(index, block, self.b1.at[group, side].at[self.part], p.core)

    def add(self, index, group, side):
        self.sends.arrived(index)
        block = self.b1.at[group, side].at[self.part]
        mine = self.src.at[group, 2 * side + self.p.core_bit].at[self.part]
        block[...] = (block[...].astype(F32) + mine[...].astype(F32)).astype(BF)
        return block

    def second(self, late):
        p = self.p
        group = p.r if late else p.other_r
        block = self.add(2 * late, group, 1 - p.x_bit)
        self.sends.start(4 + late, block, self.b2.at[group].at[self.part], p.chip_x)
        self.add(2 * late + 1, group, p.x_bit)

    def third(self):
        p = self.p
        self.sends.arrived(4)
        block = self.b2.at[p.other_r].at[self.part]
        mine = self.b1.at[p.other_r, p.x_bit].at[self.part]
        block[...] = (block[...].astype(F32) + mine[...].astype(F32)).astype(BF)
        self.sends.start(6, block, self.b3, p.half)

    def pieces(self, target, sems):
        p = self.p
        self.sends.arrived(5, 6)
        copies = []
        for index, block in enumerate(
            (self.b2.at[p.r].at[self.part], self.b1.at[p.r, p.x_bit].at[self.part], self.b3)
        ):
            copies.append(
                pltpu.make_async_copy(block, target.at[index].at[self.part], sems.at[index])
            )
            copies[-1].start()
        return copies

    def end(self):
        self.sends.left()


def flat(block):
    return block.reshape(block.shape[0] * block.shape[1], block.shape[2])


def layer_kernel(
    x, cot, q_w, k_w, v_w, o_w, u_w, d_w, q_b, v_b, u_b, g1, b1, ob, g2, b2, db,
    o_out, o_gx, o_small, o_ga, o_gf, m_land,
    a_own, f_own, small, small_all, a_all, f_all, rows_all, c_all, normed, qkv, turned, mix, lse,
    out_s, part, part_m, from_y, from_z, relay_y, relay_z, m_relay_y, m_relay_z, act_s, dup_s, res, d_res,
    dm_s, dk_s, dv_s, f1, f2, f3, a1, a2, a3, sums, sv, rv, cols, cs, rcs, rt,
    x_ss, x_rs, s_ss, s_rs, a_ss, a_rs, f_ss, f_rs, c_ss, c_rs, p_ss, p_rs,
    n_ss, n_rs, d_ss, d_rs, e_ss, e_rs, r_ss, r_rs, m_ss, m_rs, fg_ss, fg_rs, ag_ss, ag_rs,
    v_ss, v_rs, t_ss, t_rs, l_sem, free_sem,
):
    p = Place()
    rows, width = x.shape
    feat = a_own.shape[0]
    per, hid = q_b.shape[0], u_b.shape[0]
    main = f_own.shape[1] // 2 - LANE // 2
    tail, hidp = hid - main, main + LANE

    def pack():
        stack = jnp.concatenate([w[...].astype(F32) for w in (q_w, k_w, v_w, o_w)], axis=0).T
        a_own[...] = jnp.concatenate(
            [stack, jnp.zeros((feat, a_own.shape[1] - stack.shape[1]), F32)], axis=1
        ).astype(BF)
        small[...] = jnp.zeros_like(small)
        small[0:1, :per] = q_b[...].astype(F32).reshape(1, per)
        value_row = jnp.concatenate(
            [v_b[...].astype(F32).reshape(1, per), jnp.zeros((1, small.shape[1] - per), F32)], axis=1
        )
        small[0:1] += pltpu.roll(value_row, 2 * per, 1)
        small[1:2, :hid] = u_b[...].astype(F32).reshape(1, hid)
        for index, item in enumerate((g1, b1, ob, g2, b2, db)):
            small[2 + index : 3 + index, :per] = item[...].astype(F32).reshape(1, per)

    greet(
        [(p.gx, lax.rem(p.gy + d, 8)) for d in range(1, 8)]
        + [(lax.rem(p.gx + d, 4), p.gy) for d in range(1, 4)],
        pack,
    )
    gather = Gather(p, x, rows_all, x_ss, x_rs, CUT)
    gather.begin()
    parts = (pl.ds(0, feat // 2), pl.ds(feat // 2, feat // 2))
    mid = rows // 2
    halves = (pl.ds(0, mid), pl.ds(mid, mid))

    def gathers(send_sem, recv_sem):
        return [
            Gather(
                p, rows_all.at[p.t].at[half], rows_all.at[:, half], send_sem.at[i], recv_sem.at[i],
                HALF_CUT,
            )
            for i, half in enumerate(halves)
        ]

    def scatters(send_sem, recv_sem):
        long, short = mid - HALF_CUT, HALF_CUT
        return [
            Scatter(
                p, part.at[:, half], from_y.at[half], from_z.at[half],
                relay_y.at[pl.ds(long * i, long)], relay_z.at[pl.ds(short * i, short)],
                send_sem.at[i], recv_sem.at[i],
            )
            for i, half in enumerate(halves)
        ]

    attn_w = [
        Spread(p, a_own, a_all, a_ss.at[i], a_rs.at[i], l_sem.at[i], parts[i]) for i in range(2)
    ]
    for item in attn_w:
        item.begin()
    small_all[p.gy] = small[...]
    smalls = Sends(s_ss, s_rs)
    for d in range(1, 8):
        smalls.start(d - 1, small, small_all.at[p.gy], (p.gx, lax.rem(p.gy + d, 8)))
    f_own[:, :main] = u_w[:, :main]
    f_own[:, hidp:] = d_w[:, :main]
    ends = jnp.concatenate(
        [u_w[:, main:].astype(F32), jnp.zeros((feat, LANE - tail), F32)], axis=1
    )
    more = jnp.concatenate(
        [d_w[:, main:].astype(F32), jnp.zeros((feat, LANE - tail), F32)], axis=1
    )
    f_own[:, main:hidp] = (ends + pltpu.roll(more, LANE // 2, 1)).astype(BF)
    feed_w = [
        Spread(p, f_own, f_all, f_ss.at[i], f_rs.at[i], l_sem.at[2 + i], parts[i])
        for i in range(2)
    ]
    cots = Gather(p, cot, c_all, c_ss, c_rs, CUT)
    c_all[p.t] = cot[...]
    smalls.arrived(*range(7))
    vec = jnp.zeros((8, width), F32)
    wide_per = -(-per // LANE) * LANE
    for g in range(8):
        vec = vec + spread(small_all[g][:, :wide_per], per * g, width)

    def norm(index, block):
        hat, _ = center_rows(block.astype(F32))
        normed[index] = (hat * vec[2:3] + vec[3:4]).astype(BF)

    norm(p.t, x[...])
    gather.forward()
    attn_w[0].second()
    attn_w[1].second()
    for item in feed_w:
        item.begin()
    gather.near()
    norm(p.ty, rows_all[p.ty])
    norm(p.tz, rows_all[p.tz])
    cots.begin()
    gather.far()
    norm(p.td, rows_all[p.td])
    for item in attn_w:
        item.third()
    for item in attn_w:
        item.done()

    def project(index, carry):
        block = normed[index]
        for group in range(2):
            bias = small_all[p.t + 4 * group, 0:1, :512]
            packed = nn(block, flat(a_all[group])[:, :512]) + bias
            for piece in range(6):
                qkv[piece // 2, 2 * group + piece % 2, pl.ds(index * rows, rows)] = lanes(
                    packed, HD * piece, LANE, HD
                ).astype(BF)
        return carry

    lax.fori_loop(0, 4, project, 0)
    for head in range(4):
        turned[head] = qkv[2, head].astype(F32).T.astype(BF)
    scatter = scatters(p_ss, p_rs)

    def attend(index):
        def one(head, carry):
            start = pl.multiple_of(index * rows, rows)
            scores = nt(qkv[1, head], qkv[0, head, pl.ds(start, rows)])
            top = jnp.max(scores, axis=0, keepdims=True)
            expo = jnp.exp2((scores - top) * (SCALE * LOG2E))
            total = jnp.sum(expo, axis=0, keepdims=True)
            mixed = nn(turned[head], expo.astype(BF)) / total
            out_s[head] = mixed.T
            lse[head, index] = jnp.broadcast_to(
                top * (SCALE * LOG2E) + jnp.log2(total), lse.shape[2:]
            )
            return carry

        lax.fori_loop(0, 4, one, 0)
        total = jnp.zeros((rows, width), F32)
        for group in range(2):
            both = (
                spread(out_s[2 * group], 48, 256) + spread(out_s[2 * group + 1], 48 + HD, 256)
            ).astype(BF)
            mix[group, pl.ds(pl.multiple_of(index * rows, rows), rows)] = both
            total = total + nt(both, flat(a_all[group])[:, 384:640])
        part[index] = total.astype(BF)

    gather.end()
    attend(p.td)
    for item in scatter:
        item.far()
    attend(p.ty)
    for item in scatter:
        item.near_y()
    attend(p.tz)
    for item in scatter:
        item.near_z()
    for item in scatter:
        item.relay()
    feed_w[0].second()
    cots.forward()
    attend(p.t)
    gather_n = gathers(n_ss, n_rs)
    for half, item, out in zip(halves, scatter, gather_n):
        residual = x[half].astype(F32) + item.total() + vec[4:5]
        res[half] = residual
        hat, _ = center_rows(residual.astype(BF).astype(F32))
        rows_all[p.t, half] = (hat * vec[5:6] + vec[6:7]).astype(BF)
        out.begin()
    for item in (*scatter, *attn_w):
        item.end()
    feed_w[1].second()
    for item in feed_w:
        item.third()
    for item in feed_w:
        item.done()
    scatter_d = scatters(d_ss, d_rs)
    cols[...] = jnp.zeros_like(cols)

    def feed(index):
        rows_two, rows_c = rows_all[index], c_all[index]
        out_m = jnp.zeros((rows, width), F32)
        out_d = jnp.zeros((rows, width), F32)
        live = lax.broadcasted_iota(jnp.int32, (rows, hidp), 1) < hid
        for group in range(2):
            upper = nn(rows_two, flat(f_all[group])[:, :hidp])
            upper = jnp.where(live, upper + small_all[p.t + 4 * group, 1:2, :hidp], 0.0)
            square = upper * upper
            tanh = jnp.tanh(ROOT * upper * (1.0 + 0.044715 * square))
            active = 0.5 * upper * (1.0 + tanh)
            slope = 0.5 * (1.0 + tanh) + 0.5 * upper * (1.0 - tanh * tanh) * (
                ROOT * (1.0 + 3.0 * 0.044715 * square)
            )
            act = jnp.concatenate(
                [pltpu.roll(active[:, main:], LANE // 2, 1), active[:, :main]], axis=1
            ).astype(BF)
            act_s[group, index] = act
            wide = nn(rows_c, flat(f_all[group])[:, main:])
            d_act = jnp.concatenate(
                [wide[:, LANE:], pltpu.roll(wide[:, :LANE], LANE // 2, 1)], axis=1
            )
            dup = jnp.where(live, d_act * slope, 0.0).astype(BF)
            dup_s[group, index] = dup
            cols[group : group + 1] += jnp.sum(dup.astype(F32), axis=0, keepdims=True)
            out_m = out_m + nt(act, flat(f_all[group])[:, main:])
            out_d = out_d + nt(dup, flat(f_all[group])[:, :hidp])
        part_m[index] = out_m.astype(BF)
        part[index] = out_d.astype(BF)

    gather_n[0].forward()
    feed(p.t)
    gather_n[1].forward()
    for item in gather_n:
        item.near()
    cots.near()
    feed(p.ty)
    for item in scatter_d:
        item.near_y()
    feed(p.tz)
    for item in scatter_d:
        item.near_z()
    for item in gather_n:
        item.far()
    cots.far()
    feed(p.td)
    for item in scatter_d:
        item.far()
    for item in feed_w:
        item.end()
    feed_g = [
        Reduce(p, f_all, f1, f2, f3, fg_ss.at[i], fg_rs.at[i], parts[i]) for i in range(2)
    ]

    def feed_grads(group):
        up = tn(flat(rows_all[...]), flat(dup_s[group]))
        f_all[group, :, :, :main] = up[:, :main].astype(BF).reshape(4, feat, main)
        down = tn(flat(c_all[...]), flat(act_s[group]))
        f_all[group, :, :, hidp:] = down[:, LANE:].astype(BF).reshape(4, feat, main)
        both = (up[:, main:] + down[:, :LANE]).astype(BF)
        f_all[group, :, :, main:hidp] = both.reshape(4, feat, LANE)

    feed_grads(p.other_r)
    for item in feed_g:
        item.begin(0)
    for item in scatter_d:
        item.relay()
    scatter_m = Scatter(
        p, part_m, m_land.at[0], m_land.at[1], m_relay_y, m_relay_z, m_ss, m_rs
    )
    feed_grads(p.r)
    for item in feed_g:
        item.begin(1)
    for item in gather_n:
        item.end()
    cots.end()
    for peer in (p.near_y, p.near_z):
        pl.semaphore_signal(free_sem, inc=1, device_id=peer, device_id_type=MESH)
    for item in feed_g:
        item.second(0)
    sums[...] = jnp.zeros_like(sums)
    gather_e = gathers(e_ss, e_rs)
    for half, item, out in zip(halves, scatter_d, gather_e):
        grad = item.total()
        hat, inverse = center_rows(res[half].astype(BF).astype(F32))
        cot_f = cot[half].astype(F32)
        d_residual = cot_f + norm_back(grad, vec[5:6], hat, inverse)
        d_res[half] = d_residual
        rows_all[p.t, half] = d_residual.astype(BF)
        if out is gather_e[0]:
            pl.semaphore_wait(free_sem, 2)
        out.begin()
        sums[2:3] += jnp.sum(d_residual, axis=0, keepdims=True)
        sums[3:4] += jnp.sum(grad * hat, axis=0, keepdims=True)
        sums[4:5] += jnp.sum(grad, axis=0, keepdims=True)
        sums[5:6] += jnp.sum(cot_f, axis=0, keepdims=True)
    for item in feed_g:
        item.second(1)
    for item in scatter_d:
        item.end()
    for head in range(4):
        turned[head] = qkv[1, head].astype(F32).T.astype(BF)
    dk_s[...] = jnp.zeros_like(dk_s)
    dv_s[...] = jnp.zeros_like(dv_s)

    def attend_back(index):
        block = rows_all[index]
        for group in range(2):
            mixed = nn(block, flat(a_all[group])[:, 384:640])
            dm_s[2 * group] = lanes(mixed, 48, LANE, HD).astype(BF)
            dm_s[2 * group + 1] = lanes(mixed, 48 + HD, LANE, HD).astype(BF)

        def one(head, carry):
            start = pl.multiple_of(index * rows, rows)
            q_rows, d_mix = qkv[0, head, pl.ds(start, rows)], dm_s[head]
            scores = nt(qkv[1, head], q_rows)
            probs = jnp.exp2(scores * (SCALE * LOG2E) - lse[head, index, 0:1])
            d_probs = nt(qkv[2, head], d_mix)
            delta = jnp.sum(d_probs * probs, axis=0, keepdims=True)
            d_scores = (probs * (d_probs - delta)).astype(BF)
            dv_s[head] += nn(probs.astype(BF), d_mix)
            dk_s[head] += nn(d_scores, q_rows)
            out_s[head] = nn(turned[head], d_scores).T * SCALE
            return carry

        lax.fori_loop(0, 4, one, 0)
        for head in range(4):
            place = LANE * (head % 2)
            dup_s[head // 2, index, :, place : place + LANE] = out_s[head].astype(BF)

    gather_e[0].forward()
    attend_back(p.t)
    gather_e[1].forward()
    for item in feed_g:
        item.third()
    for item in gather_e:
        item.near()
    attend_back(p.ty)
    scatter_m.far()
    scatter_m.near_y()
    scatter_m.near_z()
    attend_back(p.tz)
    for item in gather_e:
        item.far()
    attend_back(p.td)
    scatter_n = scatters(r_ss, r_rs)
    cs[...] = jnp.zeros_like(cs)

    def give(index):
        here = pl.ds(pl.multiple_of(index * rows, rows), rows)
        total = jnp.zeros((rows, width), F32)
        for group in range(2):
            packed = jnp.zeros((rows, 512), F32)
            for piece in range(6):
                head = 2 * group + piece % 2
                if piece < 2:
                    value = dup_s[group, index, :, LANE * piece : LANE * (piece + 1)].astype(F32)
                elif piece < 4:
                    value = dk_s[head, here] * SCALE
                else:
                    value = dv_s[head, here]
                packed = packed + spread(value, HD * piece, 512)
            packed = packed.astype(BF)
            act_s[group, index, :, :512] = packed
            cs[group, 0:1, :512] += jnp.sum(packed.astype(F32), axis=0, keepdims=True)
            total = total + nt(packed, flat(a_all[group])[:, :512])
        part[index] = total.astype(BF)
        sums[0:1] += jnp.sum(total * normed[index].astype(F32), axis=0, keepdims=True)
        sums[1:2] += jnp.sum(total, axis=0, keepdims=True)

    give(p.td)
    for item in scatter_n:
        item.far()
    give(p.ty)
    for item in scatter_n:
        item.near_y()
    give(p.tz)
    for item in scatter_n:
        item.near_z()
    give(p.t)
    scatter_m.relay()
    sums[0:1] = (sums[0:1] - vec[3:4] * sums[1:2]) / vec[2:3]
    all_sums = sums[...]
    for g in range(8):
        sv[g] = lanes(all_sums, per * g, sv.shape[2], per)
    for group in range(2):
        cs[group, 1:2] = cols[group : group + 1]
    slices = Sends(v_ss, v_rs)
    for d in range(1, 8):
        other = lax.rem(p.gy + d, 8)
        slices.start(d - 1, sv.at[other], rv.at[p.gy], (p.gx, other))
    slices.start(7, cs.at[p.other_r], rcs, p.half)
    rv[p.gy] = sv[p.gy]
    attn_g = [
        Reduce(p, a_all, a1, a2, a3, ag_ss.at[i], ag_rs.at[i], parts[i]) for i in range(2)
    ]

    def attn_grads(group):
        main = tn(flat(normed[...]), flat(act_s[group])[:, :512])
        outer = tn(flat(rows_all[...]), mix[group])
        both = jnp.concatenate(
            [main[:, :384], main[:, 384:] + outer[:, :128], outer[:, 128:]], axis=1
        )
        a_all[group] = both.astype(BF).reshape(4, feat, 640)

    attn_grads(p.other_r)
    for item in attn_g:
        item.begin(0)
    for item in scatter_n:
        item.relay()
    for item in attn_g:
        item.second(0)
    attn_grads(p.r)
    for item in attn_g:
        item.begin(1)
    for item in attn_g:
        item.third()
    for item in attn_g:
        item.second(1)
    slices.arrived(*range(8))
    total = rv[0]
    for g in range(1, 8):
        total = total + rv[g]
    mine = rt.at[p.gx]
    mine[0:8] = jnp.concatenate(
        [total, jnp.zeros((8, rt.shape[2] - total.shape[1]), F32)], axis=1
    )
    mine[8:16] = cs[p.r] + rcs[...]
    totals = Sends(t_ss, t_rs)
    for d in range(1, 4):
        totals.start(d - 1, mine, mine, (lax.rem(p.gx + d, 4), p.gy))
    copies = []
    for i in range(2):
        copies += feed_g[i].pieces(o_gf, l_sem.at[pl.ds(4 + 3 * i, 3)])
    scatter_m.sends.arrived(2, 3, 4, 5)
    moves = [
        pltpu.make_async_copy(m_land.at[i], c_all.at[i], l_sem.at[16 + i]) for i in range(2)
    ]
    for move in moves:
        move.start()
    for half, item in zip(halves, scatter_n):
        grad = item.total()
        hat, inverse = center_rows(x[half].astype(F32))
        o_gx[half] = (d_res[half] + norm_back(grad, vec[2:3], hat, inverse)).astype(BF)
    totals.arrived(0, 1, 2)
    o_small[...] = rt[0] + rt[1] + rt[2] + rt[3]
    for move in moves:
        move.wait()
    addend = part_m[p.t].astype(F32) + c_all[0].astype(F32) + c_all[1].astype(F32)
    o_out[...] = (res[...] + addend + vec[7:8]).astype(BF)
    for i in range(2):
        copies += attn_g[i].pieces(o_ga, l_sem.at[pl.ds(10 + 3 * i, 3)])
    for copy in copies:
        copy.wait()
    for item in (smalls, slices, totals):
        item.left()
    for item in (*gather_e, *feed_g, *attn_g, *scatter_n, scatter_m):
        item.end()


VM = pl.BlockSpec(memory_space=pltpu.VMEM)
ANY = pl.BlockSpec(memory_space=pl.ANY)


def dma(shape):
    return pltpu.SemaphoreType.DMA(shape)


def finish_kernel(
    out, gx, ga, gf, small,
    o_out, o_gx, o_g1, o_b1, o_q, o_qb, o_k, o_v, o_vb, o_o, o_ob, o_g2, o_b2, o_u, o_ub, o_d, o_db,
):
    per, hid = o_g1.shape[0], o_ub.shape[0]
    main = gf.shape[2] // 2 - LANE // 2
    tail = hid - main
    o_out[...] = out[...]
    o_gx[...] = gx[...]
    stack = (ga[0].astype(F32) + ga[1].astype(F32) + ga[2].astype(F32)).T
    for index, item in enumerate((o_q, o_k, o_v, o_o)):
        item[...] = stack[per * index : per * (index + 1)]
    grads = gf[0].astype(F32) + gf[1].astype(F32) + gf[2].astype(F32)
    ends = grads[:, main : main + LANE]
    o_u[:, :main] = grads[:, :main]
    o_u[:, main:] = ends[:, :tail]
    o_d[:, :main] = grads[:, main + LANE :]
    o_d[:, main:] = pltpu.roll(ends, LANE // 2, 1)[:, :tail]
    for index, item in enumerate((o_g1, o_b1, o_ob, o_g2, o_b2, o_db)):
        item[...] = small[index : index + 1, :per].reshape(per)
    o_qb[...] = small[8:9, :per].reshape(per)
    o_vb[...] = pltpu.roll(small[8:9], small.shape[1] - 2 * per, 1)[:, :per].reshape(per)
    o_ub[...] = small[9:10, :hid].reshape(hid)


def fast_shards(
    layer_input, norm_one_gain, norm_one_bias, query_weight, query_bias, key_weight, value_weight,
    value_bias, output_weight, output_bias, norm_two_gain, norm_two_bias, up_weight, up_bias,
    down_weight, down_bias, cotangent,
):
    rows, width = layer_input.shape
    per, hid = query_weight.shape[1], up_weight.shape[1]
    feat = query_weight.shape[0]
    hidp = -(-hid // LANE) * LANE
    fw = 2 * hidp - LANE
    aw = 640
    shape, bf, f32 = jax.ShapeDtypeStruct, BF, F32
    params = lambda number: pltpu.CompilerParams(
        collective_id=number, has_side_effects=True, vmem_limit_bytes=VMEM_LIMIT
    )
    full = (rows, width)
    block4 = pltpu.VMEM((4, rows, width), bf)

    wide = -(-per // LANE) * LANE
    block = pltpu.VMEM(full, bf)
    hidden = pltpu.VMEM((2, 4, rows, hidp), bf)
    heads = pltpu.VMEM((4, 4 * rows, LANE), f32)
    six, seven, sixes, sevens = dma((6,)), dma((7,)), dma((2, 6)), dma((2, 7))
    (out, grad_input, smalls, ga, gfo, _) = pl.pallas_call(
        layer_kernel,
        name="layer",
        out_shape=[
            shape(full, bf), shape(full, bf), shape((16, aw), f32), shape((3, feat, aw), bf),
            shape((3, feat, fw), bf), shape((2, rows, width), bf),
        ],
        in_specs=[VM] * 17,
        out_specs=[VM] * 3 + [ANY] * 3,
        scratch_shapes=[
            pltpu.VMEM((feat, aw), bf), pltpu.VMEM((feat, fw), bf), pltpu.VMEM((8, aw), f32),
            pltpu.VMEM((8, 8, aw), f32), pltpu.VMEM((2, 4, feat, aw), bf),
            pltpu.VMEM((2, 4, feat, fw), bf), block4, block4, block4,
            pltpu.VMEM((3, 4, 4 * rows, LANE), bf), pltpu.VMEM((4, LANE, 4 * rows), bf),
            pltpu.VMEM((2, 4 * rows, 256), bf), pltpu.VMEM((4, 4, 8, rows), f32),
            pltpu.VMEM((4, rows, LANE), f32), block4, block4, block, block,
            pltpu.VMEM((rows - 2 * HALF_CUT, width), bf), pltpu.VMEM((2 * HALF_CUT, width), bf),
            pltpu.VMEM((rows - CUT, width), bf), pltpu.VMEM((CUT, width), bf),
            hidden, hidden, pltpu.VMEM(full, f32), pltpu.VMEM(full, f32),
            pltpu.VMEM((4, rows, LANE), bf), heads, heads,
            pltpu.VMEM((2, 2, feat, fw), bf), pltpu.VMEM((2, feat, fw), bf),
            pltpu.VMEM((feat, fw), bf), pltpu.VMEM((2, 2, feat, aw), bf),
            pltpu.VMEM((2, feat, aw), bf), pltpu.VMEM((feat, aw), bf),
            pltpu.VMEM((8, width), f32), pltpu.VMEM((8, 8, wide), f32),
            pltpu.VMEM((8, 8, wide), f32), pltpu.VMEM((8, hidp), f32), pltpu.VMEM((2, 8, aw), f32),
            pltpu.VMEM((8, aw), f32), pltpu.VMEM((4, 16, aw), f32),
            six, six, seven, seven, sevens, sevens, sevens, sevens, six, six,
            sixes, sixes, sixes, sixes, sixes, sixes, sixes, sixes, sixes, sixes, six, six,
            sevens, sevens, sevens, sevens,
            dma((8,)), dma((8,)), dma((3,)), dma((3,)), dma((18,)), pltpu.SemaphoreType.REGULAR,
        ],
        compiler_params=params(0),
    )(
        layer_input, cotangent, query_weight.T, key_weight.T, value_weight.T, output_weight,
        up_weight, down_weight.T, query_bias, value_bias, up_bias, norm_one_gain, norm_one_bias,
        output_bias, norm_two_gain, norm_two_bias, down_bias,
    )
    line = shape((per,), f32)
    turned = shape((per, feat), f32)
    done = pl.pallas_call(
        finish_kernel,
        name="finish",
        out_shape=[
            shape(full, bf), shape(full, bf), line, line, turned, line, turned, turned, line,
            turned, line, line, line, shape((feat, hid), f32), shape((hid,), f32),
            shape((feat, hid), f32), line,
        ],
        in_specs=[VM] * 5,
        out_specs=[VM] * 17,
        compiler_params=pltpu.CompilerParams(vmem_limit_bytes=VMEM_LIMIT),
    )(out, grad_input, ga, gfo, smalls)
    done = list(done)
    for index in (4, 6, 7, 15):
        done[index] = done[index].T
    return tuple(done)


def dot_plain(left, right):
    return jnp.dot(left, right, preferred_element_type=jnp.float32)


def dot_right_t(left, right):
    return lax.dot_general(
        left, right, (((1,), (1,)), ((), ())), preferred_element_type=jnp.float32
    )


def dot_left_t(left, right):
    return lax.dot_general(
        left, right, (((0,), (0,)), ((), ())), preferred_element_type=jnp.float32
    )


def normalize(rows):
    center = rows - jnp.mean(rows, axis=-1, keepdims=True)
    inverse = lax.rsqrt(jnp.mean(center * center, axis=-1, keepdims=True) + 1e-06)
    return (center * inverse, inverse)


def gelu_tanh(value):
    return jax.nn.gelu(value, approximate=True)


def image_shape(array):
    heads = array.shape[1] // HD
    return (array.shape[0] // LENGTH, LENGTH, heads, HD)


def attend(query, key, value):
    shape = image_shape(query)
    scale = HD ** (-0.5)

    def one_image(carry, pieces):
        q_img, k_img, v_img = pieces
        scores = (
            jnp.einsum("qhd,khd->hqk", q_img, k_img, preferred_element_type=jnp.float32) * scale
        )
        top = jnp.max(scores, axis=-1, keepdims=True)
        expo = jnp.exp(scores - top)
        total = jnp.sum(expo, axis=-1, keepdims=True)
        probs = (expo / total).astype(jnp.bfloat16)
        mixed = jnp.einsum("hqk,khd->qhd", probs, v_img, preferred_element_type=jnp.float32).astype(
            jnp.bfloat16
        )
        return (carry, (mixed, (top + jnp.log(total))[..., 0]))

    _, (mixed, lse) = lax.scan(
        one_image, 0, (query.reshape(shape), key.reshape(shape), value.reshape(shape))
    )
    return (mixed.reshape(query.shape), lse)


def attend_back(query, key, value, lse, d_mixed):
    shape = image_shape(query)
    scale = HD ** (-0.5)

    def one_image(carry, pieces):
        q_img, k_img, v_img, lse_img, dm_img = pieces
        scores = (
            jnp.einsum("qhd,khd->hqk", q_img, k_img, preferred_element_type=jnp.float32) * scale
        )
        probs = jnp.exp(scores - lse_img[..., None])
        d_probs = jnp.einsum("qhd,khd->hqk", dm_img, v_img, preferred_element_type=jnp.float32)
        d_scores = (probs * (d_probs - jnp.sum(d_probs * probs, axis=-1, keepdims=True))).astype(
            jnp.bfloat16
        )
        d_value = jnp.einsum(
            "hqk,qhd->khd", probs.astype(jnp.bfloat16), dm_img, preferred_element_type=jnp.float32
        ).astype(jnp.bfloat16)
        d_query = (
            jnp.einsum("hqk,khd->qhd", d_scores, k_img, preferred_element_type=jnp.float32) * scale
        ).astype(jnp.bfloat16)
        d_key = (
            jnp.einsum("hqk,qhd->khd", d_scores, q_img, preferred_element_type=jnp.float32) * scale
        ).astype(jnp.bfloat16)
        return (carry, (d_query, d_key, d_value))

    _, (d_query, d_key, d_value) = lax.scan(
        one_image,
        0,
        (
            query.reshape(shape),
            key.reshape(shape),
            value.reshape(shape),
            lse,
            d_mixed.reshape(shape),
        ),
    )
    return (d_query.reshape(query.shape), d_key.reshape(query.shape), d_value.reshape(query.shape))


def forward_pass(
    layer_input,
    norm_one_gain,
    norm_one_bias,
    query_weight,
    query_bias,
    key_weight,
    value_weight,
    value_bias,
    output_weight,
    output_bias,
    norm_two_gain,
    norm_two_bias,
    up_weight,
    up_bias,
    down_weight,
    down_bias,
):
    w_query, w_key, w_value, w_output, w_up, w_down = (
        lax.all_gather(query_weight, "gx", axis=0, tiled=True),
        lax.all_gather(key_weight, "gx", axis=0, tiled=True),
        lax.all_gather(value_weight, "gx", axis=0, tiled=True),
        lax.all_gather(output_weight, "gx", axis=1, tiled=True),
        lax.all_gather(up_weight, "gx", axis=0, tiled=True),
        lax.all_gather(down_weight, "gx", axis=1, tiled=True),
    )
    rows_one, gain_one, shift_one, out_shift, down_shift = (
        lax.all_gather(layer_input, "gy", axis=0, tiled=True),
        lax.all_gather(norm_one_gain, "gy", axis=0, tiled=True),
        lax.all_gather(norm_one_bias, "gy", axis=0, tiled=True),
        lax.all_gather(output_bias, "gy", axis=0, tiled=True),
        lax.all_gather(down_bias, "gy", axis=0, tiled=True),
    )
    hat_one, inv_one = normalize(rows_one.astype(jnp.float32))
    normed = (hat_one * gain_one.astype(jnp.float32) + shift_one.astype(jnp.float32)).astype(
        jnp.bfloat16
    )
    query = (dot_plain(normed, w_query) + query_bias.astype(jnp.float32)).astype(jnp.bfloat16)
    key = dot_plain(normed, w_key).astype(jnp.bfloat16)
    value = (dot_plain(normed, w_value) + value_bias.astype(jnp.float32)).astype(jnp.bfloat16)
    mixed, lse = attend(query, key, value)
    attn_part = lax.psum_scatter(
        dot_plain(mixed, w_output).astype(jnp.bfloat16), "gy", scatter_dimension=0, tiled=True
    ).astype(jnp.float32)
    residual = layer_input.astype(jnp.float32) + attn_part + out_shift.astype(jnp.float32)
    rows_two, gain_two, shift_two = (
        lax.all_gather(residual.astype(jnp.bfloat16), "gy", axis=0, tiled=True),
        lax.all_gather(norm_two_gain, "gy", axis=0, tiled=True),
        lax.all_gather(norm_two_bias, "gy", axis=0, tiled=True),
    )
    hat_two, inv_two = normalize(rows_two.astype(jnp.float32))
    normed_two = (hat_two * gain_two.astype(jnp.float32) + shift_two.astype(jnp.float32)).astype(
        jnp.bfloat16
    )
    upper = dot_plain(normed_two, w_up) + up_bias.astype(jnp.float32)
    active = gelu_tanh(upper).astype(jnp.bfloat16)
    mlp_part = lax.psum_scatter(
        dot_plain(active, w_down).astype(jnp.bfloat16), "gy", scatter_dimension=0, tiled=True
    ).astype(jnp.float32)
    result = (residual + mlp_part + down_shift.astype(jnp.float32)).astype(jnp.bfloat16)
    saved = (
        w_query,
        w_key,
        w_value,
        w_output,
        w_up,
        w_down,
        hat_one,
        inv_one,
        normed,
        query,
        key,
        value,
        mixed,
        lse,
        hat_two,
        inv_two,
        normed_two,
        upper,
        active,
        gain_one,
        gain_two,
    )
    return saved, result


def shards(
    layer_input,
    norm_one_gain,
    norm_one_bias,
    query_weight,
    query_bias,
    key_weight,
    value_weight,
    value_bias,
    output_weight,
    output_bias,
    norm_two_gain,
    norm_two_bias,
    up_weight,
    up_bias,
    down_weight,
    down_bias,
    cotangent,
):
    inputs = (
        layer_input,
        norm_one_gain,
        norm_one_bias,
        query_weight,
        query_bias,
        key_weight,
        value_weight,
        value_bias,
        output_weight,
        output_bias,
        norm_two_gain,
        norm_two_bias,
        up_weight,
        up_bias,
        down_weight,
        down_bias,
    )
    saved, layer_output = forward_pass(*inputs)
    (
        w_query,
        w_key,
        w_value,
        w_output,
        w_up,
        w_down,
        hat_one,
        inv_one,
        normed,
        query,
        key,
        value,
        mixed,
        lse,
        hat_two,
        inv_two,
        normed_two,
        upper,
        active,
        gain_one,
        gain_two,
    ) = saved
    local = layer_input.shape[0]
    start = lax.axis_index("gy") * local
    grad_rows = lax.all_gather(cotangent, "gy", axis=0, tiled=True)
    d_active = dot_right_t(grad_rows, w_down)
    _, gelu_pull = jax.vjp(gelu_tanh, upper)
    d_upper = gelu_pull(d_active)[0].astype(jnp.bfloat16)
    grad_up_weight, grad_down_weight = (
        lax.psum_scatter(
            dot_left_t(normed_two, d_upper).astype(jnp.bfloat16),
            "gx",
            scatter_dimension=0,
            tiled=True,
        ).astype(jnp.float32),
        lax.psum_scatter(
            dot_left_t(active, grad_rows).astype(jnp.bfloat16),
            "gx",
            scatter_dimension=1,
            tiled=True,
        ).astype(jnp.float32),
    )
    d_normed_two = lax.psum_scatter(
        dot_right_t(d_upper, w_up).astype(jnp.bfloat16), "gy", scatter_dimension=0, tiled=True
    ).astype(jnp.float32)
    hat_two_local = lax.dynamic_slice_in_dim(hat_two, start, local, 0)
    inv_two_local = lax.dynamic_slice_in_dim(inv_two, start, local, 0)
    scaled_two = d_normed_two * gain_two.astype(jnp.float32)
    mean_two = jnp.mean(scaled_two, axis=-1, keepdims=True)
    proj_two = jnp.mean(scaled_two * hat_two_local, axis=-1, keepdims=True)
    cot_float = cotangent.astype(jnp.float32)
    d_residual = cot_float + inv_two_local * (scaled_two - mean_two - hat_two_local * proj_two)
    part_two_gain = jnp.sum(d_normed_two * hat_two_local, axis=0)
    part_two_bias = jnp.sum(d_normed_two, axis=0)
    part_up_bias = jnp.sum(d_upper.astype(jnp.float32), axis=0)
    part_down_bias = jnp.sum(cot_float, axis=0)
    grad_attn = lax.all_gather(d_residual.astype(jnp.bfloat16), "gy", axis=0, tiled=True)
    part_output_bias = jnp.sum(d_residual, axis=0)
    d_mixed = dot_right_t(grad_attn, w_output).astype(jnp.bfloat16)
    d_query, d_key, d_value = attend_back(query, key, value, lse, d_mixed)
    grad_query_weight, grad_key_weight, grad_value_weight, grad_output_weight = (
        lax.psum_scatter(
            dot_left_t(normed, d_query).astype(jnp.bfloat16), "gx", scatter_dimension=0, tiled=True
        ).astype(jnp.float32),
        lax.psum_scatter(
            dot_left_t(normed, d_key).astype(jnp.bfloat16), "gx", scatter_dimension=0, tiled=True
        ).astype(jnp.float32),
        lax.psum_scatter(
            dot_left_t(normed, d_value).astype(jnp.bfloat16), "gx", scatter_dimension=0, tiled=True
        ).astype(jnp.float32),
        lax.psum_scatter(
            dot_left_t(mixed, grad_attn).astype(jnp.bfloat16), "gx", scatter_dimension=1, tiled=True
        ).astype(jnp.float32),
    )
    d_normed = lax.psum_scatter(
        (
            dot_right_t(d_query, w_query)
            + dot_right_t(d_key, w_key)
            + dot_right_t(d_value, w_value)
        ).astype(jnp.bfloat16),
        "gy",
        scatter_dimension=0,
        tiled=True,
    ).astype(jnp.float32)
    hat_one_local = lax.dynamic_slice_in_dim(hat_one, start, local, 0)
    inv_one_local = lax.dynamic_slice_in_dim(inv_one, start, local, 0)
    scaled_one = d_normed * gain_one.astype(jnp.float32)
    mean_one = jnp.mean(scaled_one, axis=-1, keepdims=True)
    proj_one = jnp.mean(scaled_one * hat_one_local, axis=-1, keepdims=True)
    grad_input = (
        d_residual + inv_one_local * (scaled_one - mean_one - hat_one_local * proj_one)
    ).astype(jnp.bfloat16)
    part_one_gain = jnp.sum(d_normed * hat_one_local, axis=0)
    part_one_bias = jnp.sum(d_normed, axis=0)
    part_query_bias = jnp.sum(d_query.astype(jnp.float32), axis=0)
    part_value_bias = jnp.sum(d_value.astype(jnp.float32), axis=0)
    feat_one_gain, feat_one_bias, feat_output_bias, feat_two_gain, feat_two_bias, feat_down_bias = (
        lax.psum_scatter(part_one_gain, "gy", scatter_dimension=0, tiled=True),
        lax.psum_scatter(part_one_bias, "gy", scatter_dimension=0, tiled=True),
        lax.psum_scatter(part_output_bias, "gy", scatter_dimension=0, tiled=True),
        lax.psum_scatter(part_two_gain, "gy", scatter_dimension=0, tiled=True),
        lax.psum_scatter(part_two_bias, "gy", scatter_dimension=0, tiled=True),
        lax.psum_scatter(part_down_bias, "gy", scatter_dimension=0, tiled=True),
    )
    (
        grad_one_gain,
        grad_one_bias,
        grad_query_bias,
        grad_value_bias,
        grad_output_bias,
        grad_two_gain,
        grad_two_bias,
        grad_up_bias,
        grad_down_bias,
    ) = lax.psum(
        (
            feat_one_gain,
            feat_one_bias,
            part_query_bias,
            part_value_bias,
            feat_output_bias,
            feat_two_gain,
            feat_two_bias,
            part_up_bias,
            feat_down_bias,
        ),
        "gx",
    )
    return (
        layer_output,
        grad_input,
        grad_one_gain,
        grad_one_bias,
        grad_query_weight,
        grad_query_bias,
        grad_key_weight,
        grad_value_weight,
        grad_value_bias,
        grad_output_weight,
        grad_output_bias,
        grad_two_gain,
        grad_two_bias,
        grad_up_weight,
        grad_up_bias,
        grad_down_weight,
        grad_down_bias,
    )


def solution(mesh):
    fits = mesh.shape["gx"] == 4 and mesh.shape["gy"] == 8
    return jax.shard_map(
        fast_shards if fits else shards,
        mesh=mesh,
        in_specs=(
            P(("gx", "gy"), None),
            P("gy"),
            P("gy"),
            P("gx", "gy"),
            P("gy"),
            P("gx", "gy"),
            P("gx", "gy"),
            P("gy"),
            P("gy", "gx"),
            P("gy"),
            P("gy"),
            P("gy"),
            P("gx", "gy"),
            P("gy"),
            P("gy", "gx"),
            P("gy"),
            P(("gx", "gy"), None),
        ),
        out_specs=(
            P(("gx", "gy"), None),
            P(("gx", "gy"), None),
            P("gy"),
            P("gy"),
            P("gx", "gy"),
            P("gy"),
            P("gx", "gy"),
            P("gx", "gy"),
            P("gy"),
            P("gy", "gx"),
            P("gy"),
            P("gy"),
            P("gy"),
            P("gx", "gy"),
            P("gy"),
            P("gy", "gx"),
            P("gy"),
        ),
        check_vma=False,
    )
```

```python
import functools
import math

import jax
import jax.numpy as jnp
from jax import lax
from jax.experimental import pallas as pl
from jax.experimental.pallas import tpu as pltpu
from jax.sharding import PartitionSpec as P

HD = 72
LENGTH = 1024
LANE = 128
BF = jnp.bfloat16
F32 = jnp.float32
MESH = pl.DeviceIdType.MESH
TP = 4
VMEM_LIMIT = 63 << 20
SCALE = HD ** (-0.5)
CUT = 80
LAST_CUT = 32
MLP_CUT = 32
HALF_CUT = 48
LOG2E = 1.4426950408889634
ROOT = math.sqrt(2.0 / math.pi)


def nn(left, right):
    return jnp.dot(left, right, preferred_element_type=F32)


def nt(left, right):
    return lax.dot_general(left, right, (((1,), (1,)), ((), ())), preferred_element_type=F32)


def tn(left, right):
    return lax.dot_general(left, right, (((0,), (0,)), ((), ())), preferred_element_type=F32)


def center_rows(rows):
    center = rows - jnp.mean(rows, axis=-1, keepdims=True)
    inverse = lax.rsqrt(jnp.mean(center * center, axis=-1, keepdims=True) + 1e-06)
    return center * inverse, inverse


def norm_back(grad, gain, hat, inverse):
    scaled = grad * gain
    mean = jnp.mean(scaled, axis=-1, keepdims=True)
    proj = jnp.mean(scaled * hat, axis=-1, keepdims=True)
    return inverse * (scaled - mean - hat * proj)


def lanes(value, start, width, keep):
    full = value.shape[1]
    moved = value if start == 0 else pltpu.roll(value, full - start, 1)
    part = moved[:, :width]
    return jnp.where(lax.broadcasted_iota(jnp.int32, part.shape, 1) < keep, part, 0.0)


def spread(value, start, full):
    wide = jnp.concatenate([value, jnp.zeros((value.shape[0], full - value.shape[1]), F32)], axis=1)
    return wide if start == 0 else pltpu.roll(wide, start, 1)


class Place:
    def __init__(self):
        gx, gy = lax.axis_index("gx"), lax.axis_index("gy")
        self.gx, self.gy = gx, gy
        self.t, self.r = lax.rem(gy, 4), lax.div(gy, 4)
        y, z = lax.rem(gy, 2), lax.rem(lax.div(gy, 2), 2)
        self.ty = self.t + 1 - 2 * y
        self.tz = self.t + 2 - 4 * z
        self.td = 3 - self.t
        base = 4 * self.r
        self.near_y = (gx, base + self.ty)
        self.near_z = (gx, base + self.tz)
        self.other_r = 1 - self.r
        self.half = (gx, lax.rem(gy + 4, 8))
        self.core_bit, self.x_bit = lax.rem(gx, 2), lax.div(gx, 2)
        self.gx_core = gx + 1 - 2 * self.core_bit
        self.gx_x = lax.rem(gx + 2, 4)
        self.core = (self.gx_core, gy)
        self.chip_x = (self.gx_x, gy)


def greet(peers, meanwhile):
    barrier = pltpu.get_barrier_semaphore()
    for peer in peers:
        pl.semaphore_signal(barrier, inc=1, device_id=peer, device_id_type=MESH)
    meanwhile()
    pl.semaphore_wait(barrier, len(peers))


class Sends:
    def __init__(self, send_sem, recv_sem):
        self.send_sem, self.recv_sem, self.copies = send_sem, recv_sem, {}

    def start(self, index, source, target, peer):
        copy = pltpu.make_async_remote_copy(
            src_ref=source,
            dst_ref=target,
            send_sem=self.send_sem.at[index],
            recv_sem=self.recv_sem.at[index],
            device_id=peer,
            device_id_type=MESH,
        )
        copy.start()
        self.copies[index] = copy

    def arrived(self, *indices):
        for index in indices:
            self.copies[index].wait_recv()

    def left(self):
        for copy in self.copies.values():
            copy.wait_send()


class Gather:
    def __init__(self, place, source, target, send_sem, recv_sem, cut):
        self.p, self.dst = place, target
        self.sends = Sends(send_sem, recv_sem)
        self.lo, self.hi = pl.ds(0, cut), pl.ds(cut, source.shape[0] - cut)
        self.src = source

    def begin(self):
        p, own = self.p, self.dst.at[self.p.t]
        for index, part, peer in (
            (0, self.lo, p.near_y),
            (2, self.hi, p.near_z),
            (1, self.hi, p.near_y),
            (3, self.lo, p.near_z),
        ):
            self.sends.start(index, self.src.at[part], own.at[part], peer)

    def forward(self):
        p = self.p
        self.sends.arrived(0)
        block = self.dst.at[p.ty].at[self.lo]
        self.sends.start(4, block, block, p.near_z)
        self.sends.arrived(2)
        block = self.dst.at[p.tz].at[self.hi]
        self.sends.start(5, block, block, p.near_y)

    def near(self):
        self.sends.arrived(1, 3)

    def far(self):
        self.sends.arrived(4, 5)

    def end(self):
        self.sends.left()


class Scatter:
    def __init__(self, place, part, from_y, from_z, relay_y, relay_z, send_sem, recv_sem):
        self.p, self.part = place, part
        self.from_y, self.from_z, self.relay_y, self.relay_z = from_y, from_z, relay_y, relay_z
        self.sends = Sends(send_sem, recv_sem)
        cut = relay_y.shape[0]
        self.cut = cut
        self.lo, self.hi = pl.ds(0, cut), pl.ds(cut, relay_z.shape[0])

    def far(self):
        p, block = self.p, self.part.at[self.p.td]
        self.sends.start(0, block.at[self.lo], self.relay_y, p.near_y)
        self.sends.start(1, block.at[self.hi], self.relay_z, p.near_z)

    def near_y(self):
        p = self.p
        self.sends.start(2, self.part.at[p.ty].at[self.lo], self.from_y.at[self.lo], p.near_y)

    def near_z(self):
        p = self.p
        self.sends.start(3, self.part.at[p.tz].at[self.hi], self.from_z.at[self.hi], p.near_z)

    def relay(self):
        p, cut = self.p, self.cut
        self.sends.arrived(0)
        block = self.part.at[p.tz]
        block[:cut] = (block[:cut].astype(F32) + self.relay_y[...].astype(F32)).astype(BF)
        self.sends.start(4, block.at[self.lo], self.from_z.at[self.lo], p.near_z)
        self.sends.arrived(1)
        block = self.part.at[p.ty]
        block[cut:] = (block[cut:].astype(F32) + self.relay_z[...].astype(F32)).astype(BF)
        self.sends.start(5, block.at[self.hi], self.from_y.at[self.hi], p.near_y)

    def total(self):
        self.sends.arrived(2, 3, 4, 5)
        own = self.part[self.p.t].astype(F32)
        return own + self.from_y[...].astype(F32) + self.from_z[...].astype(F32)

    def end(self):
        self.sends.left()


class Spread:
    def __init__(self, place, source, target, send_sem, recv_sem, local_sem, part):
        self.p, self.part = place, part
        self.src, self.dst = source.at[part], target
        self.sends = Sends(send_sem, recv_sem)
        self.local = pltpu.make_async_copy(
            self.src, target.at[place.r, place.gx].at[part], local_sem
        )

    def slot(self, group, column):
        return self.dst.at[group, column].at[self.part]

    def begin(self):
        p = self.p
        slot = self.slot(p.r, p.gx)
        self.sends.start(0, self.src, slot, p.half)
        self.sends.start(1, self.src, slot, p.chip_x)
        self.sends.start(2, self.src, slot, p.core)
        self.local.start()

    def second(self):
        p = self.p
        self.sends.arrived(0)
        slot = self.slot(p.other_r, p.gx)
        self.sends.start(3, slot, slot, p.chip_x)
        self.sends.start(4, slot, slot, p.core)

    def third(self):
        p = self.p
        self.sends.arrived(1)
        slot = self.slot(p.r, p.gx_x)
        self.sends.start(5, slot, slot, p.core)
        self.sends.arrived(3)
        slot = self.slot(p.other_r, p.gx_x)
        self.sends.start(6, slot, slot, p.core)

    def done(self):
        self.sends.arrived(2, 4, 5, 6)
        self.local.wait()

    def end(self):
        self.sends.left()


class Reduce:
    def __init__(self, place, source, first, second, third, send_sem, recv_sem, part):
        self.p, self.part = place, part
        self.src, self.b1, self.b2, self.b3 = source, first, second, third.at[part]
        self.sends = Sends(send_sem, recv_sem)

    def begin(self, late):
        p = self.p
        group = p.r if late else p.other_r
        for index, side in ((2 * late, 1 - p.x_bit), (2 * late + 1, p.x_bit)):
            block = self.src.at[group, 2 * side + 1 - p.core_bit].at[self.part]
            self.sends.start(index, block, self.b1.at[group, side].at[self.part], p.core)

    def add(self, index, group, side):
        self.sends.arrived(index)
        block = self.b1.at[group, side].at[self.part]
        mine = self.src.at[group, 2 * side + self.p.core_bit].at[self.part]
        block[...] = (block[...].astype(F32) + mine[...].astype(F32)).astype(BF)
        return block

    def second(self, late):
        p = self.p
        group = p.r if late else p.other_r
        block = self.add(2 * late, group, 1 - p.x_bit)
        self.sends.start(4 + late, block, self.b2.at[group].at[self.part], p.chip_x)
        self.add(2 * late + 1, group, p.x_bit)

    def third(self):
        p = self.p
        self.sends.arrived(4)
        block = self.b2.at[p.other_r].at[self.part]
        mine = self.b1.at[p.other_r, p.x_bit].at[self.part]
        block[...] = (block[...].astype(F32) + mine[...].astype(F32)).astype(BF)
        self.sends.start(6, block, self.b3, p.half)

    def pieces(self, target, sems):
        p = self.p
        self.sends.arrived(5, 6)
        copies = []
        for index, block in enumerate(
            (self.b2.at[p.r].at[self.part], self.b1.at[p.r, p.x_bit].at[self.part], self.b3)
        ):
            copies.append(
                pltpu.make_async_copy(block, target.at[index].at[self.part], sems.at[index])
            )
            copies[-1].start()
        return copies

    def end(self):
        self.sends.left()


def flat(block):
    return block.reshape(block.shape[0] * block.shape[1], block.shape[2])


def layer_kernel(
    x, cot, q_w, k_w, v_w, o_w, u_w, d_w, q_b, v_b, u_b, g1, b1, ob, g2, b2, db,
    o_out, o_gx, o_small, o_ga, o_gf, m_land,
    a_own, f_own, small, small_all, a_all, f_all, rows_all, c_all, normed, qkv, turned, mix, lse,
    out_s, part, part_m, from_y, from_z, relay_y, relay_z, m_relay_y, m_relay_z, act_s, dup_s, res, d_res,
    dm_s, dk_s, dv_s, f1, f2, f3, a1, a2, a3, sums, sv, rv, cols, cs, rcs, rt,
    x_ss, x_rs, s_ss, s_rs, a_ss, a_rs, f_ss, f_rs, c_ss, c_rs, p_ss, p_rs,
    n_ss, n_rs, d_ss, d_rs, e_ss, e_rs, r_ss, r_rs, m_ss, m_rs, fg_ss, fg_rs, ag_ss, ag_rs,
    v_ss, v_rs, t_ss, t_rs, l_sem, free_sem,
):
    p = Place()
    rows, width = x.shape
    feat = a_own.shape[0]
    per, hid = q_b.shape[0], u_b.shape[0]
    main = f_own.shape[1] // 2 - LANE // 2
    tail, hidp = hid - main, main + LANE

    def pack():
        stack = jnp.concatenate([w[...].astype(F32) for w in (q_w, k_w, v_w, o_w)], axis=0).T
        a_own[...] = jnp.concatenate(
            [stack, jnp.zeros((feat, a_own.shape[1] - stack.shape[1]), F32)], axis=1
        ).astype(BF)
        small[...] = jnp.zeros_like(small)
        small[0:1, :per] = q_b[...].astype(F32).reshape(1, per)
        value_row = jnp.concatenate(
            [v_b[...].astype(F32).reshape(1, per), jnp.zeros((1, small.shape[1] - per), F32)], axis=1
        )
        small[0:1] += pltpu.roll(value_row, 2 * per, 1)
        small[1:2, :hid] = u_b[...].astype(F32).reshape(1, hid)
        for index, item in enumerate((g1, b1, ob, g2, b2, db)):
            small[2 + index : 3 + index, :per] = item[...].astype(F32).reshape(1, per)

    greet(
        [(p.gx, lax.rem(p.gy + d, 8)) for d in range(1, 8)]
        + [(lax.rem(p.gx + d, 4), p.gy) for d in range(1, 4)],
        pack,
    )
    gather = Gather(p, x, rows_all, x_ss, x_rs, CUT)
    gather.begin()
    parts = (pl.ds(0, feat // 2), pl.ds(feat // 2, feat // 2))
    mid = rows // 2
    halves = (pl.ds(0, mid), pl.ds(mid, mid))

    def gathers(send_sem, recv_sem):
        return [
            Gather(
                p, rows_all.at[p.t].at[half], rows_all.at[:, half], send_sem.at[i], recv_sem.at[i],
                HALF_CUT,
            )
            for i, half in enumerate(halves)
        ]

    def scatters(send_sem, recv_sem, short=HALF_CUT):
        long = mid - short
        return [
            Scatter(
                p, part.at[:, half], from_y.at[half], from_z.at[half],
                relay_y.at[pl.ds(long * i, long)], relay_z.at[pl.ds(short * i, short)],
                send_sem.at[i], recv_sem.at[i],
            )
            for i, half in enumerate(halves)
        ]

    attn_w = [
        Spread(p, a_own, a_all, a_ss.at[i], a_rs.at[i], l_sem.at[i], parts[i]) for i in range(2)
    ]
    for item in attn_w:
        item.begin()
    small_all[p.gy] = small[...]
    smalls = Sends(s_ss, s_rs)
    for d in range(1, 8):
        smalls.start(d - 1, small, small_all.at[p.gy], (p.gx, lax.rem(p.gy + d, 8)))
    f_own[:, :main] = u_w[:, :main]
    f_own[:, hidp:] = d_w[:, :main]
    ends = jnp.concatenate(
        [u_w[:, main:].astype(F32), jnp.zeros((feat, LANE - tail), F32)], axis=1
    )
    more = jnp.concatenate(
        [d_w[:, main:].astype(F32), jnp.zeros((feat, LANE - tail), F32)], axis=1
    )
    f_own[:, main:hidp] = (ends + pltpu.roll(more, LANE // 2, 1)).astype(BF)
    feed_w = [
        Spread(p, f_own, f_all, f_ss.at[i], f_rs.at[i], l_sem.at[2 + i], parts[i])
        for i in range(2)
    ]
    cots = Gather(p, cot, c_all, c_ss, c_rs, CUT)
    c_all[p.t] = cot[...]
    smalls.arrived(*range(7))
    vec = jnp.zeros((8, width), F32)
    wide_per = -(-per // LANE) * LANE
    for g in range(8):
        vec = vec + spread(small_all[g][:, :wide_per], per * g, width)

    def norm(index, block):
        hat, _ = center_rows(block.astype(F32))
        normed[index] = (hat * vec[2:3] + vec[3:4]).astype(BF)

    norm(p.t, x[...])
    gather.forward()
    attn_w[0].second()
    attn_w[1].second()
    for item in feed_w:
        item.begin()
    gather.near()
    norm(p.ty, rows_all[p.ty])
    norm(p.tz, rows_all[p.tz])
    cots.begin()
    gather.far()
    norm(p.td, rows_all[p.td])
    for item in attn_w:
        item.third()
    for item in attn_w:
        item.done()

    def project(index, carry):
        block = normed[index]
        for group in range(2):
            bias = small_all[p.t + 4 * group, 0:1, :512]
            packed = nn(block, flat(a_all[group])[:, :512]) + bias
            for piece in range(6):
                qkv[piece // 2, 2 * group + piece % 2, pl.ds(index * rows, rows)] = lanes(
                    packed, HD * piece, LANE, HD
                ).astype(BF)
        return carry

    lax.fori_loop(0, 4, project, 0)
    for head in range(4):
        turned[head] = qkv[2, head].astype(F32).T.astype(BF)
    scatter = scatters(p_ss, p_rs)

    def attend(index):
        def one(head, carry):
            start = pl.multiple_of(index * rows, rows)
            scores = nt(qkv[1, head], qkv[0, head, pl.ds(start, rows)])
            top = jnp.max(scores, axis=0, keepdims=True)
            expo = jnp.exp2((scores - top) * (SCALE * LOG2E))
            total = jnp.sum(expo, axis=0, keepdims=True)
            mixed = nn(turned[head], expo.astype(BF)) / total
            out_s[head] = mixed.T
            lse[head, index] = jnp.broadcast_to(
                top * (SCALE * LOG2E) + jnp.log2(total), lse.shape[2:]
            )
            return carry

        lax.fori_loop(0, 4, one, 0)
        total = jnp.zeros((rows, width), F32)
        for group in range(2):
            both = (
                spread(out_s[2 * group], 48, 256) + spread(out_s[2 * group + 1], 48 + HD, 256)
            ).astype(BF)
            mix[group, pl.ds(pl.multiple_of(index * rows, rows), rows)] = both
            total = total + nt(both, flat(a_all[group])[:, 384:640])
        part[index] = total.astype(BF)

    gather.end()
    attend(p.td)
    for item in scatter:
        item.far()
    attend(p.ty)
    for item in scatter:
        item.near_y()
    attend(p.tz)
    for item in scatter:
        item.near_z()
    for item in scatter:
        item.relay()
    feed_w[0].second()
    cots.forward()
    attend(p.t)
    gather_n = gathers(n_ss, n_rs)
    for half, item, out in zip(halves, scatter, gather_n):
        residual = x[half].astype(F32) + item.total() + vec[4:5]
        res[half] = residual
        hat, _ = center_rows(residual.astype(BF).astype(F32))
        rows_all[p.t, half] = (hat * vec[5:6] + vec[6:7]).astype(BF)
        out.begin()
    for item in (*scatter, *attn_w):
        item.end()
    feed_w[1].second()
    for item in feed_w:
        item.third()
    for item in feed_w:
        item.done()
    scatter_d = scatters(d_ss, d_rs)
    cols[...] = jnp.zeros_like(cols)

    def feed(index):
        rows_two, rows_c = rows_all[index], c_all[index]
        out_m = jnp.zeros((rows, width), F32)
        out_d = jnp.zeros((rows, width), F32)
        live = lax.broadcasted_iota(jnp.int32, (rows, hidp), 1) < hid
        for group in range(2):
            upper = nn(rows_two, flat(f_all[group])[:, :hidp])
            upper = jnp.where(live, upper + small_all[p.t + 4 * group, 1:2, :hidp], 0.0)
            square = upper * upper
            tanh = jnp.tanh(ROOT * upper * (1.0 + 0.044715 * square))
            active = 0.5 * upper * (1.0 + tanh)
            slope = 0.5 * (1.0 + tanh) + 0.5 * upper * (1.0 - tanh * tanh) * (
                ROOT * (1.0 + 3.0 * 0.044715 * square)
            )
            act = jnp.concatenate(
                [pltpu.roll(active[:, main:], LANE // 2, 1), active[:, :main]], axis=1
            ).astype(BF)
            act_s[group, index] = act
            wide = nn(rows_c, flat(f_all[group])[:, main:])
            d_act = jnp.concatenate(
                [wide[:, LANE:], pltpu.roll(wide[:, :LANE], LANE // 2, 1)], axis=1
            )
            dup = jnp.where(live, d_act * slope, 0.0).astype(BF)
            dup_s[group, index] = dup
            cols[group : group + 1] += jnp.sum(dup.astype(F32), axis=0, keepdims=True)
            out_m = out_m + nt(act, flat(f_all[group])[:, main:])
            out_d = out_d + nt(dup, flat(f_all[group])[:, :hidp])
        part_m[index] = out_m.astype(BF)
        part[index] = out_d.astype(BF)

    gather_n[0].forward()
    feed(p.t)
    gather_n[1].forward()
    for item in gather_n:
        item.near()
    cots.near()
    feed(p.ty)
    for item in scatter_d:
        item.near_y()
    feed(p.tz)
    for item in scatter_d:
        item.near_z()
    for item in gather_n:
        item.far()
    cots.far()
    feed(p.td)
    for item in scatter_d:
        item.far()
    for item in feed_w:
        item.end()
    feed_g = [
        Reduce(p, f_all, f1, f2, f3, fg_ss.at[i], fg_rs.at[i], parts[i]) for i in range(2)
    ]

    def feed_grads(group):
        up = tn(flat(rows_all[...]), flat(dup_s[group]))
        f_all[group, :, :, :main] = up[:, :main].astype(BF).reshape(4, feat, main)
        down = tn(flat(c_all[...]), flat(act_s[group]))
        f_all[group, :, :, hidp:] = down[:, LANE:].astype(BF).reshape(4, feat, main)
        both = (up[:, main:] + down[:, :LANE]).astype(BF)
        f_all[group, :, :, main:hidp] = both.reshape(4, feat, LANE)

    feed_grads(p.other_r)
    for item in feed_g:
        item.begin(0)
    for item in scatter_d:
        item.relay()
    scatter_m = Scatter(
        p, part_m, m_land.at[0], m_land.at[1], m_relay_y, m_relay_z, m_ss, m_rs
    )
    feed_grads(p.r)
    for item in feed_g:
        item.begin(1)
    for item in gather_n:
        item.end()
    cots.end()
    for peer in (p.near_y, p.near_z):
        pl.semaphore_signal(free_sem, inc=1, device_id=peer, device_id_type=MESH)
    for item in feed_g:
        item.second(0)
    sums[...] = jnp.zeros_like(sums)
    gather_e = gathers(e_ss, e_rs)
    for half, item, out in zip(halves, scatter_d, gather_e):
        grad = item.total()
        hat, inverse = center_rows(res[half].astype(BF).astype(F32))
        cot_f = cot[half].astype(F32)
        d_residual = cot_f + norm_back(grad, vec[5:6], hat, inverse)
        d_res[half] = d_residual
        rows_all[p.t, half] = d_residual.astype(BF)
        if out is gather_e[0]:
            pl.semaphore_wait(free_sem, 2)
        out.begin()
        sums[2:3] += jnp.sum(d_residual, axis=0, keepdims=True)
        sums[3:4] += jnp.sum(grad * hat, axis=0, keepdims=True)
        sums[4:5] += jnp.sum(grad, axis=0, keepdims=True)
        sums[5:6] += jnp.sum(cot_f, axis=0, keepdims=True)
    for item in feed_g:
        item.second(1)
    for item in scatter_d:
        item.end()
    for head in range(4):
        turned[head] = qkv[1, head].astype(F32).T.astype(BF)
    dk_s[...] = jnp.zeros_like(dk_s)
    dv_s[...] = jnp.zeros_like(dv_s)

    def attend_back(index):
        block = rows_all[index]
        for group in range(2):
            mixed = nn(block, flat(a_all[group])[:, 384:640])
            dm_s[2 * group] = lanes(mixed, 48, LANE, HD).astype(BF)
            dm_s[2 * group + 1] = lanes(mixed, 48 + HD, LANE, HD).astype(BF)

        def one(head, carry):
            start = pl.multiple_of(index * rows, rows)
            q_rows, d_mix = qkv[0, head, pl.ds(start, rows)], dm_s[head]
            scores = nt(qkv[1, head], q_rows)
            probs = jnp.exp2(scores * (SCALE * LOG2E) - lse[head, index, 0:1])
            d_probs = nt(qkv[2, head], d_mix)
            delta = jnp.sum(d_probs * probs, axis=0, keepdims=True)
            d_scores = (probs * (d_probs - delta)).astype(BF)
            dv_s[head] += nn(probs.astype(BF), d_mix)
            dk_s[head] += nn(d_scores, q_rows)
            out_s[head] = nn(turned[head], d_scores).T * SCALE
            return carry

        lax.fori_loop(0, 4, one, 0)
        for head in range(4):
            place = LANE * (head % 2)
            dup_s[head // 2, index, :, place : place + LANE] = out_s[head].astype(BF)

    gather_e[0].forward()
    attend_back(p.t)
    gather_e[1].forward()
    for item in feed_g:
        item.third()
    for item in gather_e:
        item.near()
    scatter_m.far()
    scatter_m.near_y()
    scatter_m.near_z()
    attend_back(p.ty)
    attend_back(p.tz)
    for item in gather_e:
        item.far()
    attend_back(p.td)
    scatter_n = scatters(r_ss, r_rs, LAST_CUT)
    cs[...] = jnp.zeros_like(cs)

    def give(index):
        here = pl.ds(pl.multiple_of(index * rows, rows), rows)
        total = jnp.zeros((rows, width), F32)
        for group in range(2):
            packed = jnp.zeros((rows, 512), F32)
            for piece in range(6):
                head = 2 * group + piece % 2
                if piece < 2:
                    value = dup_s[group, index, :, LANE * piece : LANE * (piece + 1)].astype(F32)
                elif piece < 4:
                    value = dk_s[head, here] * SCALE
                else:
                    value = dv_s[head, here]
                packed = packed + spread(value, HD * piece, 512)
            packed = packed.astype(BF)
            act_s[group, index, :, :512] = packed
            cs[group, 0:1, :512] += jnp.sum(packed.astype(F32), axis=0, keepdims=True)
            total = total + nt(packed, flat(a_all[group])[:, :512])
        part[index] = total.astype(BF)
        sums[0:1] += jnp.sum(total * normed[index].astype(F32), axis=0, keepdims=True)
        sums[1:2] += jnp.sum(total, axis=0, keepdims=True)

    give(p.td)
    for item in scatter_n:
        item.far()
    give(p.ty)
    for item in scatter_n:
        item.near_y()
    give(p.tz)
    for item in scatter_n:
        item.near_z()
    give(p.t)
    scatter_m.relay()
    sums[0:1] = (sums[0:1] - vec[3:4] * sums[1:2]) / vec[2:3]
    all_sums = sums[...]
    for g in range(8):
        sv[g] = lanes(all_sums, per * g, sv.shape[2], per)
    for group in range(2):
        cs[group, 1:2] = cols[group : group + 1]
    slices = Sends(v_ss, v_rs)
    for d in range(1, 8):
        other = lax.rem(p.gy + d, 8)
        slices.start(d - 1, sv.at[other], rv.at[p.gy], (p.gx, other))
    slices.start(7, cs.at[p.other_r], rcs, p.half)
    rv[p.gy] = sv[p.gy]
    attn_g = [
        Reduce(p, a_all, a1, a2, a3, ag_ss.at[i], ag_rs.at[i], parts[i]) for i in range(2)
    ]

    def attn_grads(group):
        main = tn(flat(normed[...]), flat(act_s[group])[:, :512])
        outer = tn(flat(rows_all[...]), mix[group])
        both = jnp.concatenate(
            [main[:, :384], main[:, 384:] + outer[:, :128], outer[:, 128:]], axis=1
        )
        a_all[group] = both.astype(BF).reshape(4, feat, 640)

    attn_grads(p.other_r)
    for item in attn_g:
        item.begin(0)
    for item in scatter_n:
        item.relay()
    for item in attn_g:
        item.second(0)
    attn_grads(p.r)
    for item in attn_g:
        item.begin(1)
    for item in attn_g:
        item.third()
    for item in attn_g:
        item.second(1)
    slices.arrived(*range(8))
    total = rv[0]
    for g in range(1, 8):
        total = total + rv[g]
    mine = rt.at[p.gx]
    mine[0:8] = jnp.concatenate(
        [total, jnp.zeros((8, rt.shape[2] - total.shape[1]), F32)], axis=1
    )
    mine[8:16] = cs[p.r] + rcs[...]
    totals = Sends(t_ss, t_rs)
    for d in range(1, 4):
        totals.start(d - 1, mine, mine, (lax.rem(p.gx + d, 4), p.gy))
    copies = []
    for i in range(2):
        copies += feed_g[i].pieces(o_gf, l_sem.at[pl.ds(4 + 3 * i, 3)])
    scatter_m.sends.arrived(2, 3, 4, 5)
    moves = [
        pltpu.make_async_copy(m_land.at[i], c_all.at[i], l_sem.at[16 + i]) for i in range(2)
    ]
    for move in moves:
        move.start()
    for half, item in zip(halves, scatter_n):
        grad = item.total()
        hat, inverse = center_rows(x[half].astype(F32))
        o_gx[half] = (d_res[half] + norm_back(grad, vec[2:3], hat, inverse)).astype(BF)
    totals.arrived(0, 1, 2)
    o_small[...] = rt[0] + rt[1] + rt[2] + rt[3]
    for move in moves:
        move.wait()
    addend = part_m[p.t].astype(F32) + c_all[0].astype(F32) + c_all[1].astype(F32)
    o_out[...] = (res[...] + addend + vec[7:8]).astype(BF)
    for i in range(2):
        copies += attn_g[i].pieces(o_ga, l_sem.at[pl.ds(10 + 3 * i, 3)])
    for copy in copies:
        copy.wait()
    for item in (smalls, slices, totals):
        item.left()
    for item in (*gather_e, *feed_g, *attn_g, *scatter_n, scatter_m):
        item.end()


VM = pl.BlockSpec(memory_space=pltpu.VMEM)
ANY = pl.BlockSpec(memory_space=pl.ANY)


def dma(shape):
    return pltpu.SemaphoreType.DMA(shape)


def finish_kernel(
    out, gx, ga, gf, small,
    o_out, o_gx, o_g1, o_b1, o_q, o_qb, o_k, o_v, o_vb, o_o, o_ob, o_g2, o_b2, o_u, o_ub, o_d, o_db,
):
    per, hid = o_g1.shape[0], o_ub.shape[0]
    main = gf.shape[2] // 2 - LANE // 2
    tail = hid - main
    o_out[...] = out[...]
    o_gx[...] = gx[...]
    stack = (ga[0].astype(F32) + ga[1].astype(F32) + ga[2].astype(F32)).T
    for index, item in enumerate((o_q, o_k, o_v, o_o)):
        item[...] = stack[per * index : per * (index + 1)]
    grads = gf[0].astype(F32) + gf[1].astype(F32) + gf[2].astype(F32)
    ends = grads[:, main : main + LANE]
    o_u[:, :main] = grads[:, :main]
    o_u[:, main:] = ends[:, :tail]
    o_d[:, :main] = grads[:, main + LANE :]
    o_d[:, main:] = pltpu.roll(ends, LANE // 2, 1)[:, :tail]
    for index, item in enumerate((o_g1, o_b1, o_ob, o_g2, o_b2, o_db)):
        item[...] = small[index : index + 1, :per].reshape(per)
    o_qb[...] = small[8:9, :per].reshape(per)
    o_vb[...] = pltpu.roll(small[8:9], small.shape[1] - 2 * per, 1)[:, :per].reshape(per)
    o_ub[...] = small[9:10, :hid].reshape(hid)


def fast_shards(
    layer_input, norm_one_gain, norm_one_bias, query_weight, query_bias, key_weight, value_weight,
    value_bias, output_weight, output_bias, norm_two_gain, norm_two_bias, up_weight, up_bias,
    down_weight, down_bias, cotangent,
):
    rows, width = layer_input.shape
    per, hid = query_weight.shape[1], up_weight.shape[1]
    feat = query_weight.shape[0]
    hidp = -(-hid // LANE) * LANE
    fw = 2 * hidp - LANE
    aw = 640
    shape, bf, f32 = jax.ShapeDtypeStruct, BF, F32
    params = lambda number: pltpu.CompilerParams(
        collective_id=number, has_side_effects=True, vmem_limit_bytes=VMEM_LIMIT
    )
    full = (rows, width)
    block4 = pltpu.VMEM((4, rows, width), bf)

    wide = -(-per // LANE) * LANE
    block = pltpu.VMEM(full, bf)
    hidden = pltpu.VMEM((2, 4, rows, hidp), bf)
    heads = pltpu.VMEM((4, 4 * rows, LANE), f32)
    six, seven, sixes, sevens = dma((6,)), dma((7,)), dma((2, 6)), dma((2, 7))
    (out, grad_input, smalls, ga, gfo, _) = pl.pallas_call(
        layer_kernel,
        name="layer",
        out_shape=[
            shape(full, bf), shape(full, bf), shape((16, aw), f32), shape((3, feat, aw), bf),
            shape((3, feat, fw), bf), shape((2, rows, width), bf),
        ],
        in_specs=[VM] * 17,
        out_specs=[VM] * 3 + [ANY] * 3,
        scratch_shapes=[
            pltpu.VMEM((feat, aw), bf), pltpu.VMEM((feat, fw), bf), pltpu.VMEM((8, aw), f32),
            pltpu.VMEM((8, 8, aw), f32), pltpu.VMEM((2, 4, feat, aw), bf),
            pltpu.VMEM((2, 4, feat, fw), bf), block4, block4, block4,
            pltpu.VMEM((3, 4, 4 * rows, LANE), bf), pltpu.VMEM((4, LANE, 4 * rows), bf),
            pltpu.VMEM((2, 4 * rows, 256), bf), pltpu.VMEM((4, 4, 8, rows), f32),
            pltpu.VMEM((4, rows, LANE), f32), block4, block4, block, block,
            pltpu.VMEM((rows - 2 * LAST_CUT, width), bf), pltpu.VMEM((2 * HALF_CUT, width), bf),
            pltpu.VMEM((rows - MLP_CUT, width), bf), pltpu.VMEM((MLP_CUT, width), bf),
            hidden, hidden, pltpu.VMEM(full, f32), pltpu.VMEM(full, f32),
            pltpu.VMEM((4, rows, LANE), bf), heads, heads,
            pltpu.VMEM((2, 2, feat, fw), bf), pltpu.VMEM((2, feat, fw), bf),
            pltpu.VMEM((feat, fw), bf), pltpu.VMEM((2, 2, feat, aw), bf),
            pltpu.VMEM((2, feat, aw), bf), pltpu.VMEM((feat, aw), bf),
            pltpu.VMEM((8, width), f32), pltpu.VMEM((8, 8, wide), f32),
            pltpu.VMEM((8, 8, wide), f32), pltpu.VMEM((8, hidp), f32), pltpu.VMEM((2, 8, aw), f32),
            pltpu.VMEM((8, aw), f32), pltpu.VMEM((4, 16, aw), f32),
            six, six, seven, seven, sevens, sevens, sevens, sevens, six, six,
            sixes, sixes, sixes, sixes, sixes, sixes, sixes, sixes, sixes, sixes, six, six,
            sevens, sevens, sevens, sevens,
            dma((8,)), dma((8,)), dma((3,)), dma((3,)), dma((18,)), pltpu.SemaphoreType.REGULAR,
        ],
        compiler_params=params(0),
    )(
        layer_input, cotangent, query_weight.T, key_weight.T, value_weight.T, output_weight,
        up_weight, down_weight.T, query_bias, value_bias, up_bias, norm_one_gain, norm_one_bias,
        output_bias, norm_two_gain, norm_two_bias, down_bias,
    )
    line = shape((per,), f32)
    turned = shape((per, feat), f32)
    done = pl.pallas_call(
        finish_kernel,
        name="finish",
        out_shape=[
            shape(full, bf), shape(full, bf), line, line, turned, line, turned, turned, line,
            turned, line, line, line, shape((feat, hid), f32), shape((hid,), f32),
            shape((feat, hid), f32), line,
        ],
        in_specs=[VM] * 5,
        out_specs=[VM] * 17,
        compiler_params=pltpu.CompilerParams(vmem_limit_bytes=VMEM_LIMIT),
    )(out, grad_input, ga, gfo, smalls)
    done = list(done)
    for index in (4, 6, 7, 15):
        done[index] = done[index].T
    return tuple(done)


def dot_plain(left, right):
    return jnp.dot(left, right, preferred_element_type=jnp.float32)


def dot_right_t(left, right):
    return lax.dot_general(
        left, right, (((1,), (1,)), ((), ())), preferred_element_type=jnp.float32
    )


def dot_left_t(left, right):
    return lax.dot_general(
        left, right, (((0,), (0,)), ((), ())), preferred_element_type=jnp.float32
    )


def normalize(rows):
    center = rows - jnp.mean(rows, axis=-1, keepdims=True)
    inverse = lax.rsqrt(jnp.mean(center * center, axis=-1, keepdims=True) + 1e-06)
    return (center * inverse, inverse)


def gelu_tanh(value):
    return jax.nn.gelu(value, approximate=True)


def image_shape(array):
    heads = array.shape[1] // HD
    return (array.shape[0] // LENGTH, LENGTH, heads, HD)


def attend(query, key, value):
    shape = image_shape(query)
    scale = HD ** (-0.5)

    def one_image(carry, pieces):
        q_img, k_img, v_img = pieces
        scores = (
            jnp.einsum("qhd,khd->hqk", q_img, k_img, preferred_element_type=jnp.float32) * scale
        )
        top = jnp.max(scores, axis=-1, keepdims=True)
        expo = jnp.exp(scores - top)
        total = jnp.sum(expo, axis=-1, keepdims=True)
        probs = (expo / total).astype(jnp.bfloat16)
        mixed = jnp.einsum("hqk,khd->qhd", probs, v_img, preferred_element_type=jnp.float32).astype(
            jnp.bfloat16
        )
        return (carry, (mixed, (top + jnp.log(total))[..., 0]))

    _, (mixed, lse) = lax.scan(
        one_image, 0, (query.reshape(shape), key.reshape(shape), value.reshape(shape))
    )
    return (mixed.reshape(query.shape), lse)


def attend_back(query, key, value, lse, d_mixed):
    shape = image_shape(query)
    scale = HD ** (-0.5)

    def one_image(carry, pieces):
        q_img, k_img, v_img, lse_img, dm_img = pieces
        scores = (
            jnp.einsum("qhd,khd->hqk", q_img, k_img, preferred_element_type=jnp.float32) * scale
        )
        probs = jnp.exp(scores - lse_img[..., None])
        d_probs = jnp.einsum("qhd,khd->hqk", dm_img, v_img, preferred_element_type=jnp.float32)
        d_scores = (probs * (d_probs - jnp.sum(d_probs * probs, axis=-1, keepdims=True))).astype(
            jnp.bfloat16
        )
        d_value = jnp.einsum(
            "hqk,qhd->khd", probs.astype(jnp.bfloat16), dm_img, preferred_element_type=jnp.float32
        ).astype(jnp.bfloat16)
        d_query = (
            jnp.einsum("hqk,khd->qhd", d_scores, k_img, preferred_element_type=jnp.float32) * scale
        ).astype(jnp.bfloat16)
        d_key = (
            jnp.einsum("hqk,qhd->khd", d_scores, q_img, preferred_element_type=jnp.float32) * scale
        ).astype(jnp.bfloat16)
        return (carry, (d_query, d_key, d_value))

    _, (d_query, d_key, d_value) = lax.scan(
        one_image,
        0,
        (
            query.reshape(shape),
            key.reshape(shape),
            value.reshape(shape),
            lse,
            d_mixed.reshape(shape),
        ),
    )
    return (d_query.reshape(query.shape), d_key.reshape(query.shape), d_value.reshape(query.shape))


def forward_pass(
    layer_input,
    norm_one_gain,
    norm_one_bias,
    query_weight,
    query_bias,
    key_weight,
    value_weight,
    value_bias,
    output_weight,
    output_bias,
    norm_two_gain,
    norm_two_bias,
    up_weight,
    up_bias,
    down_weight,
    down_bias,
):
    w_query, w_key, w_value, w_output, w_up, w_down = (
        lax.all_gather(query_weight, "gx", axis=0, tiled=True),
        lax.all_gather(key_weight, "gx", axis=0, tiled=True),
        lax.all_gather(value_weight, "gx", axis=0, tiled=True),
        lax.all_gather(output_weight, "gx", axis=1, tiled=True),
        lax.all_gather(up_weight, "gx", axis=0, tiled=True),
        lax.all_gather(down_weight, "gx", axis=1, tiled=True),
    )
    rows_one, gain_one, shift_one, out_shift, down_shift = (
        lax.all_gather(layer_input, "gy", axis=0, tiled=True),
        lax.all_gather(norm_one_gain, "gy", axis=0, tiled=True),
        lax.all_gather(norm_one_bias, "gy", axis=0, tiled=True),
        lax.all_gather(output_bias, "gy", axis=0, tiled=True),
        lax.all_gather(down_bias, "gy", axis=0, tiled=True),
    )
    hat_one, inv_one = normalize(rows_one.astype(jnp.float32))
    normed = (hat_one * gain_one.astype(jnp.float32) + shift_one.astype(jnp.float32)).astype(
        jnp.bfloat16
    )
    query = (dot_plain(normed, w_query) + query_bias.astype(jnp.float32)).astype(jnp.bfloat16)
    key = dot_plain(normed, w_key).astype(jnp.bfloat16)
    value = (dot_plain(normed, w_value) + value_bias.astype(jnp.float32)).astype(jnp.bfloat16)
    mixed, lse = attend(query, key, value)
    attn_part = lax.psum_scatter(
        dot_plain(mixed, w_output).astype(jnp.bfloat16), "gy", scatter_dimension=0, tiled=True
    ).astype(jnp.float32)
    residual = layer_input.astype(jnp.float32) + attn_part + out_shift.astype(jnp.float32)
    rows_two, gain_two, shift_two = (
        lax.all_gather(residual.astype(jnp.bfloat16), "gy", axis=0, tiled=True),
        lax.all_gather(norm_two_gain, "gy", axis=0, tiled=True),
        lax.all_gather(norm_two_bias, "gy", axis=0, tiled=True),
    )
    hat_two, inv_two = normalize(rows_two.astype(jnp.float32))
    normed_two = (hat_two * gain_two.astype(jnp.float32) + shift_two.astype(jnp.float32)).astype(
        jnp.bfloat16
    )
    upper = dot_plain(normed_two, w_up) + up_bias.astype(jnp.float32)
    active = gelu_tanh(upper).astype(jnp.bfloat16)
    mlp_part = lax.psum_scatter(
        dot_plain(active, w_down).astype(jnp.bfloat16), "gy", scatter_dimension=0, tiled=True
    ).astype(jnp.float32)
    result = (residual + mlp_part + down_shift.astype(jnp.float32)).astype(jnp.bfloat16)
    saved = (
        w_query,
        w_key,
        w_value,
        w_output,
        w_up,
        w_down,
        hat_one,
        inv_one,
        normed,
        query,
        key,
        value,
        mixed,
        lse,
        hat_two,
        inv_two,
        normed_two,
        upper,
        active,
        gain_one,
        gain_two,
    )
    return saved, result


def shards(
    layer_input,
    norm_one_gain,
    norm_one_bias,
    query_weight,
    query_bias,
    key_weight,
    value_weight,
    value_bias,
    output_weight,
    output_bias,
    norm_two_gain,
    norm_two_bias,
    up_weight,
    up_bias,
    down_weight,
    down_bias,
    cotangent,
):
    inputs = (
        layer_input,
        norm_one_gain,
        norm_one_bias,
        query_weight,
        query_bias,
        key_weight,
        value_weight,
        value_bias,
        output_weight,
        output_bias,
        norm_two_gain,
        norm_two_bias,
        up_weight,
        up_bias,
        down_weight,
        down_bias,
    )
    saved, layer_output = forward_pass(*inputs)
    (
        w_query,
        w_key,
        w_value,
        w_output,
        w_up,
        w_down,
        hat_one,
        inv_one,
        normed,
        query,
        key,
        value,
        mixed,
        lse,
        hat_two,
        inv_two,
        normed_two,
        upper,
        active,
        gain_one,
        gain_two,
    ) = saved
    local = layer_input.shape[0]
    start = lax.axis_index("gy") * local
    grad_rows = lax.all_gather(cotangent, "gy", axis=0, tiled=True)
    d_active = dot_right_t(grad_rows, w_down)
    _, gelu_pull = jax.vjp(gelu_tanh, upper)
    d_upper = gelu_pull(d_active)[0].astype(jnp.bfloat16)
    grad_up_weight, grad_down_weight = (
        lax.psum_scatter(
            dot_left_t(normed_two, d_upper).astype(jnp.bfloat16),
            "gx",
            scatter_dimension=0,
            tiled=True,
        ).astype(jnp.float32),
        lax.psum_scatter(
            dot_left_t(active, grad_rows).astype(jnp.bfloat16),
            "gx",
            scatter_dimension=1,
            tiled=True,
        ).astype(jnp.float32),
    )
    d_normed_two = lax.psum_scatter(
        dot_right_t(d_upper, w_up).astype(jnp.bfloat16), "gy", scatter_dimension=0, tiled=True
    ).astype(jnp.float32)
    hat_two_local = lax.dynamic_slice_in_dim(hat_two, start, local, 0)
    inv_two_local = lax.dynamic_slice_in_dim(inv_two, start, local, 0)
    scaled_two = d_normed_two * gain_two.astype(jnp.float32)
    mean_two = jnp.mean(scaled_two, axis=-1, keepdims=True)
    proj_two = jnp.mean(scaled_two * hat_two_local, axis=-1, keepdims=True)
    cot_float = cotangent.astype(jnp.float32)
    d_residual = cot_float + inv_two_local * (scaled_two - mean_two - hat_two_local * proj_two)
    part_two_gain = jnp.sum(d_normed_two * hat_two_local, axis=0)
    part_two_bias = jnp.sum(d_normed_two, axis=0)
    part_up_bias = jnp.sum(d_upper.astype(jnp.float32), axis=0)
    part_down_bias = jnp.sum(cot_float, axis=0)
    grad_attn = lax.all_gather(d_residual.astype(jnp.bfloat16), "gy", axis=0, tiled=True)
    part_output_bias = jnp.sum(d_residual, axis=0)
    d_mixed = dot_right_t(grad_attn, w_output).astype(jnp.bfloat16)
    d_query, d_key, d_value = attend_back(query, key, value, lse, d_mixed)
    grad_query_weight, grad_key_weight, grad_value_weight, grad_output_weight = (
        lax.psum_scatter(
            dot_left_t(normed, d_query).astype(jnp.bfloat16), "gx", scatter_dimension=0, tiled=True
        ).astype(jnp.float32),
        lax.psum_scatter(
            dot_left_t(normed, d_key).astype(jnp.bfloat16), "gx", scatter_dimension=0, tiled=True
        ).astype(jnp.float32),
        lax.psum_scatter(
            dot_left_t(normed, d_value).astype(jnp.bfloat16), "gx", scatter_dimension=0, tiled=True
        ).astype(jnp.float32),
        lax.psum_scatter(
            dot_left_t(mixed, grad_attn).astype(jnp.bfloat16), "gx", scatter_dimension=1, tiled=True
        ).astype(jnp.float32),
    )
    d_normed = lax.psum_scatter(
        (
            dot_right_t(d_query, w_query)
            + dot_right_t(d_key, w_key)
            + dot_right_t(d_value, w_value)
        ).astype(jnp.bfloat16),
        "gy",
        scatter_dimension=0,
        tiled=True,
    ).astype(jnp.float32)
    hat_one_local = lax.dynamic_slice_in_dim(hat_one, start, local, 0)
    inv_one_local = lax.dynamic_slice_in_dim(inv_one, start, local, 0)
    scaled_one = d_normed * gain_one.astype(jnp.float32)
    mean_one = jnp.mean(scaled_one, axis=-1, keepdims=True)
    proj_one = jnp.mean(scaled_one * hat_one_local, axis=-1, keepdims=True)
    grad_input = (
        d_residual + inv_one_local * (scaled_one - mean_one - hat_one_local * proj_one)
    ).astype(jnp.bfloat16)
    part_one_gain = jnp.sum(d_normed * hat_one_local, axis=0)
    part_one_bias = jnp.sum(d_normed, axis=0)
    part_query_bias = jnp.sum(d_query.astype(jnp.float32), axis=0)
    part_value_bias = jnp.sum(d_value.astype(jnp.float32), axis=0)
    feat_one_gain, feat_one_bias, feat_output_bias, feat_two_gain, feat_two_bias, feat_down_bias = (
        lax.psum_scatter(part_one_gain, "gy", scatter_dimension=0, tiled=True),
        lax.psum_scatter(part_one_bias, "gy", scatter_dimension=0, tiled=True),
        lax.psum_scatter(part_output_bias, "gy", scatter_dimension=0, tiled=True),
        lax.psum_scatter(part_two_gain, "gy", scatter_dimension=0, tiled=True),
        lax.psum_scatter(part_two_bias, "gy", scatter_dimension=0, tiled=True),
        lax.psum_scatter(part_down_bias, "gy", scatter_dimension=0, tiled=True),
    )
    (
        grad_one_gain,
        grad_one_bias,
        grad_query_bias,
        grad_value_bias,
        grad_output_bias,
        grad_two_gain,
        grad_two_bias,
        grad_up_bias,
        grad_down_bias,
    ) = lax.psum(
        (
            feat_one_gain,
            feat_one_bias,
            part_query_bias,
            part_value_bias,
            feat_output_bias,
            feat_two_gain,
            feat_two_bias,
            part_up_bias,
            feat_down_bias,
        ),
        "gx",
    )
    return (
        layer_output,
        grad_input,
        grad_one_gain,
        grad_one_bias,
        grad_query_weight,
        grad_query_bias,
        grad_key_weight,
        grad_value_weight,
        grad_value_bias,
        grad_output_weight,
        grad_output_bias,
        grad_two_gain,
        grad_two_bias,
        grad_up_weight,
        grad_up_bias,
        grad_down_weight,
        grad_down_bias,
    )


def solution(mesh):
    fits = mesh.shape["gx"] == 4 and mesh.shape["gy"] == 8
    return jax.shard_map(
        fast_shards if fits else shards,
        mesh=mesh,
        in_specs=(
            P(("gx", "gy"), None),
            P("gy"),
            P("gy"),
            P("gx", "gy"),
            P("gy"),
            P("gx", "gy"),
            P("gx", "gy"),
            P("gy"),
            P("gy", "gx"),
            P("gy"),
            P("gy"),
            P("gy"),
            P("gx", "gy"),
            P("gy"),
            P("gy", "gx"),
            P("gy"),
            P(("gx", "gy"), None),
        ),
        out_specs=(
            P(("gx", "gy"), None),
            P(("gx", "gy"), None),
            P("gy"),
            P("gy"),
            P("gx", "gy"),
            P("gy"),
            P("gx", "gy"),
            P("gx", "gy"),
            P("gy"),
            P("gy", "gx"),
            P("gy"),
            P("gy"),
            P("gy"),
            P("gx", "gy"),
            P("gy"),
            P("gy", "gx"),
            P("gy"),
        ),
        check_vma=False,
    )
```
